32 devices in a mesh: grp: 1, row: 8 (over z, y), col: 2 (over x), rep: 2 (over core).
Axes of the slice: x: 2, y: 2, z: 4, core: 2. Of those that a mesh axis runs over, the one named last changes fastest.
Arguments:
- seq_in: bfloat16 [512, 512], P(('grp', 'row')), may hold values from -6 to 6
- pair_in: bfloat16 [48, 512, 512], P(('grp', 'rep'), 'row', 'col'), may hold values from -6 to 6
- w_row: bfloat16 [512, 48], replicated, may hold values from -0.25 to 0.25
- w_col: bfloat16 [512, 48], replicated, may hold values from -0.25 to 0.25
- w_value: bfloat16 [512, 48], replicated, may hold values from -0.25 to 0.25
- conv_first: bfloat16 [9, 48, 48], replicated, may hold values from -0.3125 to 0.3125
- conv_second: bfloat16 [9, 48, 48], replicated, may hold values from -0.3125 to 0.3125
- w_out: bfloat16 [48, 512], replicated, may hold values from -0.875 to 0.875
Outputs:
- seq_out: bfloat16 [512, 512], P(('grp', 'row'))
- pair_out: bfloat16 [48, 512, 512], P(('grp', 'rep'), 'row', 'col')
The draws below stay inside these ranges and needn't reach their ends.
All inputs are finite; a program needn't handle non-finite values.
Results may differ from the reference program's by a relative error of at most 0.012.
Values may be sent and summed in bfloat16 or wider, within the bound.
No kernel may reach another device: no remote copies, remote signals or barrier semaphores. Data moves between devices by JAX's collectives and lax.ppermute only.
A program may use at most 64 MiB of HBM per device.

```python
import jax
import jax.numpy as jnp
from jax import lax

S = 512
C = 48
ROWS_DEV = 64
CYCLES = 2
L = 512


def shard_levels(own_key, shape, shards, least, largest):
    factor_of, own = 1.0, jax.random.fold_in(own_key, 6)
    for dim, parts in shards:
        draws = jnp.exp(jax.random.uniform(jax.random.fold_in(own, dim), (parts,), jnp.float32, least / len(shards), largest / len(shards)))
        factor_of = factor_of * jnp.repeat(draws, shape[dim] // parts).reshape([-1 if axis == dim else 1 for axis in range(len(shape))])
    return factor_of


def centred(stream_key, dims, scale, most, shards=(), kind=jnp.bfloat16):
    entries = jax.random.normal(stream_key, dims, jnp.float32) * scale
    if len(shards) > 0:
        entries = shard_levels(stream_key, dims, shards, -0.22, 0.18) * entries
    return jnp.clip(entries, min=-most, max=most).astype(kind)


def setup_inputs(seed: int = 0, part: int = 0) -> dict:
    key_list = jax.random.split(jax.random.key(seed), 9)
    own_keys = jax.random.split(jax.random.fold_in(key_list[8], part), 9)
    seq_in = centred(own_keys[0], (L, S), 1.0, 6.0, ((0, 8),))
    pair_in = centred(own_keys[1], (C, L, L), 1.0, 6.0, ((0, 2), (1, 8), (2, 2)))
    w_row = centred(key_list[2], (S, C), S ** -0.5, 0.25)
    w_col = centred(key_list[3], (S, C), S ** -0.5, 0.25)
    w_value = centred(key_list[4], (S, C), S ** -0.5, 0.25)
    conv_first = centred(key_list[5], (9, C, C), (9 * C) ** -0.5, 0.3125)
    conv_second = centred(key_list[6], (9, C, C), (9 * C) ** -0.5, 0.3125)
    w_out = centred(key_list[7], (C, S), C ** -0.5, 0.875)
    return {"seq_in": seq_in, "pair_in": pair_in, "w_row": w_row, "w_col": w_col, "w_value": w_value, "conv_first": conv_first, "conv_second": conv_second, "w_out": w_out}


def conv_full(field, kernel):
    padded = jnp.pad(field, ((0, 0), (2, 2), (2, 2)))
    kernel_f = kernel.astype(jnp.float32)

    def one_block(start_row):
        strip = lax.dynamic_slice_in_dim(padded, start_row, ROWS_DEV + 4, 1)
        total = jnp.zeros((C, ROWS_DEV, L), jnp.float32)
        for tap_index in range(9):
            row_off = tap_index // 3 * 2
            col_off = tap_index % 3 * 2
            window = strip[:, row_off:row_off + ROWS_DEV, col_off:col_off + L].astype(jnp.float32)
            total = total + jnp.einsum('oc,cij->oij', kernel_f[tap_index], window)
        return total
    starts = (jnp.arange(L // ROWS_DEV) * ROWS_DEV).astype(jnp.int32)
    blocks = lax.map(one_block, starts)
    return blocks.transpose(1, 0, 2, 3).reshape(C, L, L)

def reference(seq_in, pair_in, w_row, w_col, w_value, conv_first, conv_second, w_out):
    feats = seq_in
    pair = pair_in
    for cycle in range(CYCLES):
        rowproj = jnp.dot(feats, w_row, preferred_element_type=jnp.float32).astype(jnp.bfloat16)
        colproj = jnp.dot(feats, w_col, preferred_element_type=jnp.float32).astype(jnp.bfloat16)
        values = jnp.dot(feats, w_value, preferred_element_type=jnp.float32).astype(jnp.bfloat16)
        start = (pair.astype(jnp.float32) + rowproj.T.astype(jnp.float32)[:, :, None] + colproj.T.astype(jnp.float32)[:, None, :]).astype(jnp.bfloat16)
        hidden = jax.nn.relu(conv_full(start, conv_first)).astype(jnp.bfloat16)
        pair = (start.astype(jnp.float32) + jax.nn.relu(conv_full(hidden, conv_second))).astype(jnp.bfloat16)
        gate = jax.nn.sigmoid(pair.astype(jnp.float32)).astype(jnp.bfloat16)
        summed = jnp.einsum('cij,jc->ic', gate.astype(jnp.float32), values.astype(jnp.float32))
        gathered = summed / jnp.sqrt(jnp.float32(L))
        update = jnp.dot(gathered.astype(jnp.bfloat16), w_out, preferred_element_type=jnp.float32)
        feats = (feats.astype(jnp.float32) + update).astype(jnp.bfloat16)
    return (feats, pair)
```

```python
import functools

import jax
import jax.numpy as jnp
import numpy as np
from jax import lax
from jax.experimental import pallas as pl
from jax.experimental.pallas import tpu as pltpu
from jax.sharding import PartitionSpec as P

CYCLES = 2
HALO = 8
GROUP = 8


def shift_perms(size):
    up = [(i, (i + 1) % size) for i in range(size - 1)]
    return up, [(j, i) for i, j in up]


def sum_over(value, axis):
    size = lax.axis_size(axis)
    if size & (size - 1):
        return lax.psum(value, axis)
    bit = 1
    while bit < size:
        value = value + lax.ppermute(value, axis, [(i, i ^ bit) for i in range(size)])
        bit *= 2
    return value


def gather_over(value, axis):
    size = lax.axis_size(axis)
    if size & (size - 1):
        return lax.all_gather(value, axis, axis=1, tiled=True)
    index = lax.axis_index(axis)
    bit = 1
    while bit < size:
        other = lax.ppermute(value, axis, [(i, i ^ bit) for i in range(size)])
        high = (index & bit) > 0
        value = jnp.concatenate(
            [jnp.where(high, other, value), jnp.where(high, value, other)], axis=1
        )
        bit *= 2
    return value


def update_kernel(
    channels, rows, cols, last,
    pair_ref, row_ref, colval_ref, mask_ref, first_ref, second_ref, spread_row, spread_col, collect,
    pair_out, sums_out, start_buf, hidden_buf, taps,
):
    stride = cols + 2 * HALO
    total = (rows + 2 * HALO) * stride
    strip = GROUP * stride
    chunk = 1280
    guard = 128
    reach = 2 * stride
    far = -(-reach // 128) * 128
    f32, bf16 = jnp.float32, jnp.bfloat16

    for buf in (start_buf, hidden_buf):
        buf[:, 0:guard] = jnp.zeros((channels, guard), bf16)
        buf[:, guard + total : total + 2 * guard] = jnp.zeros((channels, guard), bf16)
    taps[:, 0:far] = jnp.zeros((3 * channels, far), f32)
    taps[:, far + total : total + 2 * far] = jnp.zeros((3 * channels, far), f32)

    colval = jnp.dot(colval_ref[...], spread_col[...], preferred_element_type=f32)
    col_flat, val_flat = colval[:channels], colval[channels:]
    for k in range((rows + 2 * HALO) // GROUP):
        lanes = slice(k * strip, (k + 1) * strip)
        row_flat = jnp.dot(
            row_ref[:, k * GROUP : (k + 1) * GROUP], spread_row[...], preferred_element_type=f32
        )
        start = pair_ref[:, lanes].astype(f32) + row_flat + col_flat
        start = jnp.where(mask_ref[:, lanes] > 0, start, 0.0)
        start_buf[:, guard + k * strip : guard + (k + 1) * strip] = start.astype(bf16)

    def conv(source, kernel_ref, finish):
        count = total // chunk

        def spread(k):
            window = source[:, k * chunk : (k + 1) * chunk + 2 * guard]
            stacked = jnp.concatenate(
                [window[:, guard + d : guard + d + chunk] for d in (-2, 0, 2)], axis=0
            )
            taps[:, far + k * chunk : far + (k + 1) * chunk] = jnp.dot(
                kernel_ref[...], stacked, preferred_element_type=f32
            )

        def gather(k):
            base = far + k * chunk
            total_of = taps[channels : 2 * channels, base : base + chunk]
            for part, lane in ((0, base - reach), (2, base + reach)):
                low = lane // 128 * 128
                high = -(-(lane + chunk) // 128) * 128
                window = taps[part * channels : (part + 1) * channels, low:high]
                total_of = total_of + window[:, lane - low : lane - low + chunk]
            finish(k, jnp.maximum(total_of, 0.0))

        for k in range(count + 1):
            if k < count:
                spread(k)
            if k > 0:
                gather(k - 1)

    def hidden_done(k, value):
        lanes = slice(k * chunk, (k + 1) * chunk)
        value = jnp.where(mask_ref[:, lanes] > 0, value, 0.0)
        hidden_buf[:, guard + k * chunk : guard + (k + 1) * chunk] = value.astype(bf16)

    def pair_done(k, value):
        lanes = slice(guard + k * chunk, guard + (k + 1) * chunk)
        pair = start_buf[:, lanes].astype(f32) + value
        start_buf[:, lanes] = pair.astype(bf16)

    conv(start_buf, first_ref, hidden_done)
    conv(hidden_buf, second_ref, pair_done)

    for k in range((rows + 2 * HALO) // GROUP):
        pair = start_buf[:, guard + k * strip : guard + (k + 1) * strip]
        gate = jax.nn.sigmoid(pair.astype(f32)).astype(bf16)
        product = (gate.astype(f32) * val_flat).astype(bf16)
        sums_out[:, k * GROUP : (k + 1) * GROUP] = jnp.dot(
            product, collect[...], preferred_element_type=f32
        )
        if not last:
            pair_out[:, k * strip : (k + 1) * strip] = pair
        elif HALO <= k * GROUP < HALO + rows:
            for i in range(GROUP):
                pair_out[k * GROUP - HALO + i] = pair[:, i * stride + HALO : i * stride + HALO + cols]


def update(pair, row_proj, colval, mask, first, second, rows, cols, last):
    channels = pair.shape[0]
    stride = cols + 2 * HALO
    total = (rows + 2 * HALO) * stride
    strip = GROUP * stride
    lane = np.arange(strip)
    spread_row = (lane[None, :] // stride == np.arange(GROUP)[:, None]).astype(jnp.bfloat16)
    spread_col = (lane[None, :] % stride == np.arange(stride)[:, None]).astype(jnp.bfloat16)
    inner = (lane % stride >= HALO) & (lane % stride < HALO + cols)
    collect = (spread_row.T.astype(np.float32) * inner[:, None]).astype(jnp.bfloat16)
    far = -(-2 * stride // 128) * 128
    shape = (rows, channels, cols) if last else (channels, total)
    whole = pl.BlockSpec(memory_space=pltpu.VMEM)
    return pl.pallas_call(
        functools.partial(update_kernel, channels, rows, cols, last),
        out_shape=(
            jax.ShapeDtypeStruct(shape, jnp.bfloat16),
            jax.ShapeDtypeStruct((channels, rows + 2 * HALO), jnp.float32),
        ),
        in_specs=[whole] * 9,
        out_specs=(whole, whole),
        scratch_shapes=[
            pltpu.VMEM((channels, total + 256), jnp.bfloat16),
            pltpu.VMEM((channels, total + 256), jnp.bfloat16),
            pltpu.VMEM((3 * channels, total + 2 * far), jnp.float32),
        ],
        compiler_params=pltpu.CompilerParams(vmem_limit_bytes=58 << 20),
    )(pair, row_proj, colval, mask, first, second, spread_row, spread_col, collect)


def on_device(seq_in, pair_in, w_row, w_col, w_value, conv_first, conv_second, w_out):
    rows = seq_in.shape[0]
    channels = w_row.shape[1]
    cols = pair_in.shape[2] // 2
    stride = cols + 2 * HALO
    row_index = lax.axis_index("row")
    col_index = lax.axis_index("col") * 2 + lax.axis_index("rep")
    length = rows * lax.axis_size("row")
    root_length = jnp.sqrt(jnp.float32(length))
    f32, bf16 = jnp.float32, jnp.bfloat16

    def stacked(kernel):
        taps = kernel.reshape(3, 3, channels, channels).transpose(0, 2, 1, 3)
        return taps.reshape(3 * channels, 3 * channels)

    first, second = stacked(conv_first), stacked(conv_second)
    weights = jnp.concatenate([w_row, w_col, w_value], axis=1)

    row_at = row_index * rows - HALO + jnp.arange(rows + 2 * HALO)
    col_at = col_index * cols - HALO + jnp.arange(stride)
    row_in = (row_at >= 0) & (row_at < length)
    col_in = (col_at >= 0) & (col_at < length)
    mask = (row_in[:, None] & col_in[None, :]).astype(f32).reshape(1, -1)

    def projections(feats):
        mine = lax.dot_general(weights, feats, (((0,), (1,)), ((), ())), preferred_element_type=f32)
        every = gather_over(mine.astype(bf16), "row")
        every = jnp.pad(every, ((0, 0), (HALO, HALO)))
        row_proj = lax.dynamic_slice_in_dim(every[:channels], row_index * rows, rows + 2 * HALO, 1)
        colval = lax.dynamic_slice_in_dim(every[channels:], col_index * cols, stride, 1)
        return row_proj, colval

    pair = lax.all_to_all(pair_in, "rep", split_axis=2, concat_axis=0, tiled=True)
    up, down = shift_perms(lax.axis_size("row"))
    above = lax.ppermute(pair[:, rows - HALO :], "row", up)
    below = lax.ppermute(pair[:, :HALO], "row", down)
    pair = jnp.concatenate([above, pair, below], axis=1)
    tall = rows + 2 * HALO
    up, down = shift_perms(lax.axis_size("col") * 2)
    left = lax.ppermute(pair[:, :, cols - HALO :].reshape(channels, -1), ("col", "rep"), up)
    right = lax.ppermute(pair[:, :, :HALO].reshape(channels, -1), ("col", "rep"), down)
    left, right = (edge.reshape(channels, tall, HALO) for edge in (left, right))
    pair = jnp.concatenate([left, pair, right], axis=2).reshape(channels, tall * stride)

    feats = seq_in
    for cycle in range(CYCLES):
        row_proj, colval = projections(feats)
        pair, sums = update(
            pair, row_proj, colval, mask, first, second, rows, cols, cycle == CYCLES - 1
        )
        full = sum_over(sum_over(sums[:, HALO : HALO + rows], "rep"), "col")
        gathered = (full / root_length).astype(bf16)
        change = lax.dot_general(gathered, w_out, (((0,), (0,)), ((), ())), preferred_element_type=f32)
        feats = (feats.astype(f32) + change).astype(bf16)
    pair = pair.transpose(1, 0, 2)
    pair = lax.all_to_all(pair, "rep", split_axis=0, concat_axis=2, tiled=True)
    return (feats, pair)


def solution(mesh):
    in_specs = (
        P(("grp", "row"), None),
        P(("grp", "rep"), "row", "col"),
        P(),
        P(),
        P(),
        P(),
        P(),
        P(),
    )
    out_specs = (P(("grp", "row"), None), P(("grp", "rep"), "row", "col"))
    return jax.shard_map(
        on_device, mesh=mesh, in_specs=in_specs, out_specs=out_specs, check_vma=False
    )
```

```python
import functools

import jax
import jax.numpy as jnp
import numpy as np
from jax import lax
from jax.experimental import pallas as pl
from jax.experimental.pallas import tpu as pltpu
from jax.sharding import PartitionSpec as P

CYCLES = 2
HALO = 8
GROUP = 8
LANES = 128
CHUNK = 1280
F32, BF16 = jnp.float32, jnp.bfloat16
WHOLE = pl.BlockSpec(memory_space=pltpu.VMEM)
PARAMS = pltpu.CompilerParams(vmem_limit_bytes=58 << 20)


def call(kernel, outs, scratch, *args, flops=1 << 20):
    moved = sum(int(np.prod(x.shape)) * x.dtype.itemsize for x in args)
    return pl.pallas_call(
        kernel,
        out_shape=tuple(jax.ShapeDtypeStruct(shape, dtype) for shape, dtype in outs),
        in_specs=[WHOLE] * len(args),
        out_specs=(WHOLE,) * len(outs),
        scratch_shapes=scratch,
        compiler_params=PARAMS,
        cost_estimate=pl.CostEstimate(flops=flops, bytes_accessed=moved, transcendentals=0),
    )(*args)


def lane_ids(shape):
    return lax.broadcasted_iota(jnp.int32, shape, len(shape) - 1)


def edges_kernel(tile_ref, out_ref):
    half, rows, width = tile_ref.shape
    groups = rows // GROUP
    packed = jnp.zeros((half, GROUP, LANES), F32)
    lane = lane_ids(packed.shape)
    first = tile_ref[:, :, 0:LANES].astype(F32)
    last = tile_ref[:, :, width - LANES : width].astype(F32)
    for m in range(groups):
        for value, at, source in ((first, 0, 0), (last, LANES // 2, LANES - HALO)):
            place = at + HALO * m
            moved = pltpu.roll(value[:, m * GROUP : (m + 1) * GROUP], (place - source) % LANES, 2)
            packed = jnp.where((lane >= place) & (lane < place + HALO), moved, packed)
    out_ref[...] = packed.reshape(half * GROUP, LANES).astype(BF16)


def unpack(tiles, edges, raw, groups_at, cols):
    rep = lax.axis_index("rep")
    tiles_across = cols // LANES
    for part in range(2):
        tile_ref, edge_ref = tiles[part], edges[part]
        half = tile_ref.shape[0]
        base = (rep if part == 0 else 1 - rep) * half
        owner = pl.ds(base, half)
        edge = pltpu.roll(edge_ref[...].astype(F32), jnp.where(rep == 0, LANES // 2, HALO), 1)
        edge = edge.reshape(half, GROUP, LANES)
        inner_at = pl.multiple_of(jnp.where(rep == 0, cols, cols - LANES), LANES)
        is_outer = (lane_ids((half, GROUP, LANES)) < HALO) == (rep == 0)
        for low, size, members in groups_at:
            for t in range(tiles_across):
                at = pl.multiple_of(rep * cols + t * LANES, LANES)
                value = tile_ref[:, low : low + size, pl.ds(at, LANES)].astype(F32)
                for m, place in members:
                    piece = value[:, m * GROUP - low : m * GROUP - low + GROUP]
                    raw[t, owner, place * GROUP : (place + 1) * GROUP, :] = piece
            inner = tile_ref[:, low : low + size, pl.ds(inner_at, LANES)].astype(F32)
            for m, place in members:
                outer = pltpu.roll(edge, (-HALO * m) % LANES, 2)
                near = pltpu.roll(inner[:, m * GROUP - low : m * GROUP - low + GROUP], HALO, 2)
                raw[tiles_across, owner, place * GROUP : (place + 1) * GROUP, :] = jnp.where(
                    is_outer, outer, near
                )


def raw_strip(raw, place):
    across, channels, rows, _ = raw.shape
    pieces = []
    for i in range(place * GROUP, (place + 1) * GROUP):
        tiles = [
            raw.at[t].reshape(channels * rows, LANES)[pl.ds(i, channels, stride=rows), :]
            for t in range(across)
        ]
        side = tiles.pop()
        pieces += [side[:, :HALO], *tiles, side[:, HALO : 2 * HALO]]
    return jnp.concatenate(pieces, axis=1)


def strips_kernel(cols, own_ref, far_ref, own_edge, far_edge, top_ref, bottom_ref, raw):
    rows = own_ref.shape[1]
    groups = rows // GROUP
    at = ((0, 2 * GROUP, ((0, 0),)), (rows - 2 * GROUP, 2 * GROUP, ((groups - 1, 1),)))
    unpack((own_ref, far_ref), (own_edge, far_edge), raw, at, cols)
    top_ref[...] = raw_strip(raw, 0).astype(BF16)
    bottom_ref[...] = raw_strip(raw, 1).astype(BF16)


def project(feats, weight_refs, row_ref, colval_ref):
    row, col, value = (
        jnp.dot(feats, ref[...], preferred_element_type=F32) for ref in weight_refs
    )
    channels = row.shape[1]
    row_ref[...] = row.T.astype(BF16)
    colval_ref[0:channels] = col.T.astype(BF16)
    colval_ref[channels:] = value.T.astype(BF16)


def project_kernel(seq_ref, above_ref, below_ref, *refs):
    weight_refs, (feats_ref, row_ref, colval_ref) = refs[:3], refs[3:]
    pieces = (above_ref, seq_ref, below_ref)
    feats = jnp.concatenate([ref[...].astype(F32) for ref in pieces], axis=0).astype(BF16)
    feats_ref[...] = feats
    project(feats, weight_refs, row_ref, colval_ref)


def advance(sum_refs, feats_ref, out_ref, root):
    total = sum_refs[0][...]
    for ref in sum_refs[1:]:
        total = total + ref[...]
    gathered = (total / root).T.astype(BF16)
    change = jnp.dot(gathered, out_ref[...], preferred_element_type=F32)
    return feats_ref[...].astype(F32) + change


def middle_kernel(root, parts, *refs):
    sum_refs, refs = refs[:parts], refs[parts:]
    feats_in, out_w, weight_refs, (feats_ref, row_ref, colval_ref) = (
        refs[0], refs[1], refs[2:5], refs[5:]
    )
    feats = advance(sum_refs, feats_in, out_w, root).astype(BF16)
    feats_ref[...] = feats
    project(feats, weight_refs, row_ref, colval_ref)


def finish_kernel(root, parts, *refs):
    sum_refs, refs = refs[:parts], refs[parts:]
    feats_in, out_w, own_ref, far_ref, seq_ref, pair_ref = refs
    rep = lax.axis_index("rep")
    rows, cols = seq_ref.shape[0], own_ref.shape[2]
    seq_ref[...] = advance(sum_refs, feats_in, out_w, root)[HALO : HALO + rows].astype(BF16)
    pair_ref[:, :, pl.ds(pl.multiple_of(rep * cols, LANES), cols)] = own_ref[...]
    pair_ref[:, :, pl.ds(pl.multiple_of((1 - rep) * cols, LANES), cols)] = far_ref[...]


def spans(low_row, high_row, stride, total):
    low = low_row * stride // LANES * LANES
    size = -(-(high_row * stride - low) // 256) * 256
    high = min(low + size, total)
    return [(at, min(at + CHUNK, high)) for at in range(low, high, CHUNK)]


def cycle_kernel(rows, cols, length, last, sources, windows, *refs):
    (start_buf, hidden_buf, taps, mask, raw), refs = refs[-5:], refs[:-5]
    pair_refs, refs = refs[:sources], refs[sources:]
    row_ref, window_refs, refs = refs[0], refs[1 : 1 + windows], refs[1 + windows :]
    first_ref, second_ref, spread_row, spread_col, collect, place_ref, *outs = refs
    channels = row_ref.shape[0]
    stride = cols + 2 * HALO
    total = (rows + 2 * HALO) * stride
    strip = GROUP * stride
    strips = (rows + 2 * HALO) // GROUP
    guard = LANES
    reach = 2 * stride
    far = -(-reach // LANES) * LANES
    rep = lax.axis_index("rep")
    row_index = lax.axis_index("row")
    chunk_index = lax.axis_index("col") * 2 + rep
    margin = 2 * CYCLES * 2 - (8 if not last else 4)
    spans_in = spans(margin, rows + 2 * HALO - margin, stride, total)
    spans_mid = spans(margin + 2, rows + 2 * HALO - margin - 2, stride, total)
    spans_out = spans(margin + 4, rows + 2 * HALO - margin - 4, stride, total)

    for k in range(strips):
        row_at = row_index * rows - HALO + k * GROUP + place_ref[0:1, :]
        col_at = chunk_index * cols - HALO + place_ref[1:2, :]
        inside = (row_at >= 0) & (row_at < length) & (col_at >= 0) & (col_at < length)
        mask[:, k * strip : (k + 1) * strip] = jnp.where(inside, 1.0, 0.0)

    turn = row_index // (length // cols)
    ordered = []
    for offset in range(windows):
        value = window_refs[0][...]
        for t in range(1, windows):
            value = jnp.where(lax.rem(t + turn, windows) == offset, window_refs[t][...], value)
        low = 0 if offset == 0 else HALO
        high = rows + (2 * HALO if offset == windows - 1 else HALO)
        ordered.append(value[:, low:high].astype(F32))
    colval = jnp.concatenate(ordered, axis=1).astype(BF16)
    colval = jnp.dot(colval, spread_col[...], preferred_element_type=F32)
    col_flat, val_flat = colval[:channels], colval[channels:]

    start_ends, hidden_ends, taps_ends = (
        (part[0][0], part[-1][1]) for part in (((0, total),), spans_mid, spans_in)
    )
    for buf, edge, (low, high) in (
        (start_buf, guard, start_ends), (hidden_buf, guard, hidden_ends), (taps, far, taps_ends)
    ):
        fill = jnp.zeros((buf.shape[0], edge), buf.dtype)
        buf[:, low : low + edge] = fill
        buf[:, high + edge : high + 2 * edge] = fill

    if sources == 6:
        own_ref, far_ref, own_edge, far_edge, above_ref, below_ref = pair_refs
        groups = rows // GROUP
        everything = ((0, rows, tuple((m, m) for m in range(groups))),)
        unpack((own_ref, far_ref), (own_edge, far_edge), raw, everything, cols)

        def pair_strip(k):
            if k == 0:
                return above_ref[...].astype(F32)
            if k == strips - 1:
                return below_ref[...].astype(F32)
            return raw_strip(raw, k - 1)
    else:

        def pair_strip(k):
            return pair_refs[0][:, k * strip : (k + 1) * strip].astype(F32)

    def start_strip(k):
        row_flat = jnp.dot(
            row_ref[:, k * GROUP : (k + 1) * GROUP], spread_row[...], preferred_element_type=F32
        )
        value = pair_strip(k) + row_flat + col_flat
        value = jnp.where(mask[:, k * strip : (k + 1) * strip] > 0, value, 0.0)
        start_buf[:, guard + k * strip : guard + (k + 1) * strip] = value.astype(BF16)

    def spread(source, kernel_ref, low, high):
        window = source[:, low : high + 2 * guard]
        stacked = jnp.concatenate(
            [window[:, guard + d : guard + d + high - low] for d in (-2, 0, 2)], axis=0
        )
        taps[:, far + low : far + high] = jnp.dot(
            kernel_ref[...], stacked, preferred_element_type=F32
        )

    def gather(low, high):
        size = high - low
        value = taps[channels : 2 * channels, far + low : far + high]
        for part, lane in ((0, far + low - reach), (2, far + low + reach)):
            begin = lane // LANES * LANES
            end = -(-(lane + size) // LANES) * LANES
            window = taps[part * channels : (part + 1) * channels, begin:end]
            value = value + window[:, lane - begin : lane - begin + size]
        return jnp.maximum(value, 0.0)

    def hidden_span(low, high):
        value = jnp.where(mask[:, low:high] > 0, gather(low, high), 0.0)
        hidden_buf[:, guard + low : guard + high] = value.astype(BF16)

    def pair_span(low, high):
        pair = start_buf[:, guard + low : guard + high].astype(F32) + gather(low, high)
        start_buf[:, guard + low : guard + high] = pair.astype(BF16)

    def gate_strip(k):
        pair = start_buf[:, guard + k * strip : guard + (k + 1) * strip]
        wide = pair.astype(F32)
        gate = jax.nn.sigmoid(wide).astype(BF16)
        product = (gate.astype(F32) * val_flat).astype(BF16)
        outs[0][:, k * GROUP : (k + 1) * GROUP] = jnp.dot(
            product, collect[...], preferred_element_type=F32
        )
        if not last:
            outs[1][:, k * strip : (k + 1) * strip] = pair
        elif 0 < k < strips - 1:
            for i in range(GROUP):
                for t in range(cols // LANES):
                    at = i * stride + HALO + t * LANES
                    flat = raw.at[t].reshape(channels * rows, LANES)
                    flat[pl.ds((k - 1) * GROUP + i, channels, stride=rows), :] = wide[:, at : at + LANES]

    for k in range(strips):
        start_strip(k)
    for low, high in spans_in:
        spread(start_buf, first_ref, low, high)
    for low, high in spans_mid:
        hidden_span(low, high)
    for low, high in spans_mid:
        spread(hidden_buf, second_ref, low, high)
    for low, high in spans_out:
        pair_span(low, high)
    for k in range(strips):
        gate_strip(k)
    if last:
        half = channels // 2
        for t in range(cols // LANES):
            lanes = slice(t * LANES, (t + 1) * LANES)
            outs[1][:, :, lanes] = raw[t, pl.ds(rep * half, half)].astype(BF16)
            outs[2][:, :, lanes] = raw[t, pl.ds((1 - rep) * half, half)].astype(BF16)


def run_cycle(pieces, row_proj, windows, first, second, rows, cols, length, last):
    channels = row_proj.shape[0]
    stride = cols + 2 * HALO
    total = (rows + 2 * HALO) * stride
    strip = GROUP * stride
    lane = np.arange(strip)
    place = np.stack([lane // stride, lane % stride] + [0 * lane] * 6).astype(np.int32)
    spread_row = (place[0] == np.arange(GROUP)[:, None]).astype(BF16)
    spread_col = (place[1] == np.arange(stride)[:, None]).astype(BF16)
    inner = (place[1] >= HALO) & (place[1] < HALO + cols)
    collect = (spread_row.T.astype(np.float32) * inner[:, None]).astype(BF16)
    far = -(-2 * stride // LANES) * LANES
    sums = ((channels, rows + 2 * HALO), F32)
    half = ((channels // 2, rows, cols), BF16)
    outs = (sums, half, half) if last else (sums, ((channels, total), BF16))
    scratch = [
        pltpu.VMEM((channels, total + 2 * LANES), BF16),
        pltpu.VMEM((channels, total + 2 * LANES), BF16),
        pltpu.VMEM((3 * channels, total + 2 * far), F32),
        pltpu.VMEM((1, total), F32),
        pltpu.VMEM((cols // LANES + 1, channels, rows, LANES), F32),
    ]
    kernel = functools.partial(cycle_kernel, rows, cols, length, last, len(pieces), len(windows))
    return call(
        kernel, outs, scratch, *pieces, row_proj, *windows, first, second,
        spread_row, spread_col, collect, place, flops=40 * channels * channels * total,
    )


def on_device(seq_in, pair_in, w_row, w_col, w_value, conv_first, conv_second, w_out):
    rows, features = seq_in.shape
    channels = w_row.shape[1]
    half = channels // 2
    cols = pair_in.shape[2] // 2
    stride = cols + 2 * HALO
    tall = rows + 2 * HALO
    row_size, col_size = lax.axis_size("row"), lax.axis_size("col")
    chunks = 2 * col_size
    length = rows * row_size
    windows = cols // rows
    root = np.float32(np.sqrt(np.float32(length)))
    every = ("row", "col", "rep")
    weights = (w_row, w_col, w_value)

    def stacked(kernel):
        taps = kernel.reshape(3, 3, channels, channels).transpose(0, 2, 1, 3)
        return taps.reshape(3 * channels, 3 * channels)

    first, second = stacked(conv_first), stacked(conv_second)
    up = [(i, i + 1) for i in range(row_size - 1)]
    down = [(j, i) for i, j in up]
    swap = [(0, 1), (1, 0)]

    def edge_perm(cross):
        moves = []
        for c in range(col_size):
            if c > 0:
                moves.append(((c - 1) * 2 + cross, c * 2))
            if c < col_size - 1:
                moves.append(((c + 1) * 2 + 1 - cross, c * 2 + 1))
        return moves

    def to_columns(value):
        received = []
        for t in range(windows):
            moves = []
            for r in range(row_size):
                for q in range(chunks):
                    source = windows * q + (t + r // chunks) % windows
                    moves.append((source * chunks + r % chunks, r * chunks + q))
            received.append(lax.ppermute(value, every, moves))
        return received

    def all_parts(value):
        return [value] + [
            lax.ppermute(value, ("col", "rep"), [(i, (i + b) % chunks) for i in range(chunks)])
            for b in range(1, chunks)
        ]

    far_pair = lax.ppermute(pair_in, "rep", swap)
    above_seq = lax.ppermute(seq_in[rows - HALO :], "row", up)
    below_seq = lax.ppermute(seq_in[:HALO], "row", down)
    (edge,) = call(edges_kernel, [((half * GROUP, LANES), BF16)], [], pair_in)
    own_edge = lax.ppermute(edge, ("col", "rep"), edge_perm(0))
    far_edge = lax.ppermute(edge, ("col", "rep"), edge_perm(1))
    wide = [((tall, features), BF16), ((channels, tall), BF16), ((2 * channels, tall), BF16)]
    feats, row_proj, colval = call(project_kernel, wide, [], seq_in, above_seq, below_seq, *weights)
    col_windows = to_columns(colval)
    flat = (channels, GROUP * stride)
    top, bottom = call(
        functools.partial(strips_kernel, cols), [(flat, BF16), (flat, BF16)],
        [pltpu.VMEM((cols // LANES + 1, channels, 2 * GROUP, LANES), F32)],
        pair_in, far_pair, own_edge, far_edge,
    )
    above = lax.ppermute(bottom, "row", up)
    below = lax.ppermute(top, "row", down)

    pieces = (pair_in, far_pair, own_edge, far_edge, above, below)
    sums, pair = run_cycle(
        pieces, row_proj, col_windows, first, second, rows, cols, length, False
    )
    parts = all_parts(sums)
    feats, row_proj, colval = call(
        functools.partial(middle_kernel, root, chunks), wide, [], *parts, feats, w_out, *weights
    )
    col_windows = to_columns(colval)
    sums, own, send = run_cycle(
        (pair,), row_proj, col_windows, first, second, rows, cols, length, True
    )
    parts = all_parts(sums)
    far_half = lax.ppermute(send, "rep", swap)
    return call(
        functools.partial(finish_kernel, root, chunks),
        [(seq_in.shape, BF16), (pair_in.shape, BF16)], [],
        *parts, feats, w_out, own, far_half,
    )


def solution(mesh):
    in_specs = (
        P(("grp", "row"), None),
        P(("grp", "rep"), "row", "col"),
        P(),
        P(),
        P(),
        P(),
        P(),
        P(),
    )
    out_specs = (P(("grp", "row"), None), P(("grp", "rep"), "row", "col"))
    return jax.shard_map(
        on_device, mesh=mesh, in_specs=in_specs, out_specs=out_specs, check_vma=False
    )
```

```python
import functools

import jax
import jax.numpy as jnp
import numpy as np
from jax import lax
from jax.experimental import pallas as pl
from jax.experimental.pallas import tpu as pltpu
from jax.sharding import PartitionSpec as P

CYCLES = 2
HALO = 8
GROUP = 8
LANES = 128
CHUNK = 1280
F32, BF16 = jnp.float32, jnp.bfloat16
def call(kernel, outs, scratch, *args, near=(), limit=16, flops=1 << 20):
    moved = sum(int(np.prod(x.shape)) * x.dtype.itemsize for x in args)
    count = len(args)
    whole = pl.BlockSpec(memory_space=pltpu.VMEM)
    anywhere = pl.BlockSpec(memory_space=pl.ANY)

    def body(*refs):
        refs, copies, sems = refs[: -len(near) - 1], refs[-len(near) - 1 : -1], refs[-1]
        moves = [
            pltpu.make_async_copy(refs[i], copies[n], sems.at[n]) for n, i in enumerate(near)
        ]
        for move in moves:
            move.start()
        for move in moves:
            move.wait()
        refs = list(refs)
        for n, i in enumerate(near):
            refs[i] = copies[n]
        kernel(*refs)

    copies = [pltpu.VMEM(args[i].shape, args[i].dtype) for i in near]
    sems = [pltpu.SemaphoreType.DMA((len(near),))] if near else []
    return pl.pallas_call(
        body if near else kernel,
        out_shape=tuple(jax.ShapeDtypeStruct(shape, dtype) for shape, dtype in outs),
        in_specs=[anywhere if i in near else whole for i in range(count)],
        out_specs=(whole,) * len(outs),
        scratch_shapes=[*scratch, *copies, *sems],
        compiler_params=pltpu.CompilerParams(vmem_limit_bytes=limit << 20),
        cost_estimate=pl.CostEstimate(flops=flops, bytes_accessed=moved, transcendentals=0),
    )(*args)


def lane_ids(shape):
    return lax.broadcasted_iota(jnp.int32, shape, len(shape) - 1)


def is_even():
    return lax.rem(lax.axis_index("row"), 2) == 0


def strips_kernel(tile_ref, seq_ref, first_ref, second_ref):
    half, rows, width = tile_ref.shape
    even = is_even()

    def message(pair, seq):
        pieces = [pair.reshape(half * GROUP, width)]
        pieces += [seq[:, at : at + width] for at in range(0, seq.shape[1], width)]
        rest = first_ref.shape[0] - GROUP * (half + len(pieces) - 1)
        if rest:
            pieces.append(jnp.zeros((rest, width), F32))
        return jnp.concatenate(pieces, axis=0)

    top = message(
        tile_ref[:, 0 : 2 * GROUP, :].astype(F32)[:, :GROUP],
        seq_ref[0 : 2 * GROUP, :].astype(F32)[:GROUP],
    )
    bottom = message(
        tile_ref[:, rows - 2 * GROUP : rows, :].astype(F32)[:, GROUP:],
        seq_ref[rows - 2 * GROUP : rows, :].astype(F32)[GROUP:],
    )
    first_ref[...] = jnp.where(even, bottom, top).astype(BF16)
    second_ref[...] = jnp.where(even, top, bottom).astype(BF16)


def received(first, second):
    even = is_even()
    return jnp.where(even, second, first), jnp.where(even, first, second)


def tile_pieces(tile_ref, first_ref, second_ref, at):
    half, rows, _ = tile_ref.shape
    middle = tile_ref[:, :, pl.ds(at, LANES)].astype(F32)
    above, below = received(
        *(
            ref[0 : half * GROUP, pl.ds(at, LANES)].astype(F32).reshape(half, GROUP, LANES)
            for ref in (first_ref, second_ref)
        )
    )
    middle = [middle[:, m * GROUP : (m + 1) * GROUP] for m in range(rows // GROUP)]
    return [above, *middle, below]


def edges_kernel(*refs):
    parts, out_ref = (refs[0:3], refs[3:6]), refs[6]
    rep = lax.axis_index("rep")
    half, _, width = refs[0].shape
    lane = lane_ids((half, GROUP, LANES))
    at = pl.multiple_of(jnp.where(rep == 0, 0, width - LANES), LANES)
    for part in range(2):
        packed = jnp.zeros((half, GROUP, LANES), F32)
        turn = jnp.where(rep == 0, 0, HALO)
        for g, piece in enumerate(tile_pieces(*parts[part], at)):
            moved = pltpu.roll(piece, turn + HALO * g, 2)
            packed = jnp.where((lane >= HALO * g) & (lane < HALO * (g + 1)), moved, packed)
        base = (rep if part == 0 else 1 - rep) * half * GROUP
        out_ref[pl.ds(pl.multiple_of(base, 2 * GROUP), half * GROUP), :] = packed.reshape(
            half * GROUP, LANES
        ).astype(BF16)


def unpack(parts, edge_ref, raw, cols):
    rep = lax.axis_index("rep")
    across = cols // LANES
    half = parts[0][0].shape[0]
    inner_at = pl.multiple_of(jnp.where(rep == 0, cols, cols - LANES), LANES)
    is_outer = (lane_ids((half, GROUP, LANES)) < HALO) == (rep == 0)
    for part in range(2):
        owner = pl.ds((rep if part == 0 else 1 - rep) * half, half)
        for t in range(across):
            at = pl.multiple_of(rep * cols + t * LANES, LANES)
            for g, piece in enumerate(tile_pieces(*parts[part], at)):
                raw[t, owner, g * GROUP : (g + 1) * GROUP, :] = piece
        base = (rep if part == 0 else 1 - rep) * half * GROUP
        edge = edge_ref[pl.ds(pl.multiple_of(base, 2 * GROUP), half * GROUP), :].astype(F32)
        edge = edge.reshape(half, GROUP, LANES)
        outer = pltpu.roll(edge, jnp.where(rep == 0, 0, HALO), 2)
        for g, piece in enumerate(tile_pieces(*parts[part], inner_at)):
            raw[across, owner, g * GROUP : (g + 1) * GROUP, :] = jnp.where(
                is_outer,
                pltpu.roll(outer, (-HALO * g) % LANES, 2),
                pltpu.roll(piece, HALO, 2),
            )


def raw_strip(raw, place):
    across, channels, rows, _ = raw.shape
    pieces = []
    for i in range(place * GROUP, (place + 1) * GROUP):
        tiles = [
            raw.at[t].reshape(channels * rows, LANES)[pl.ds(i, channels, stride=rows), :]
            for t in range(across)
        ]
        side = tiles.pop()
        pieces += [side[:, :HALO], *tiles, side[:, HALO : 2 * HALO]]
    return jnp.concatenate(pieces, axis=1)


def project(feats, weight_refs, row_ref, colval_ref):
    row, col, value = (
        lax.dot_general(ref[...], feats, (((1,), (1,)), ((), ())), preferred_element_type=F32)
        for ref in weight_refs
    )
    channels = row.shape[0]
    row_ref[...] = row.astype(BF16)
    colval_ref[0:channels] = col.astype(BF16)
    colval_ref[channels:] = value.astype(BF16)


def project_kernel(half, seq_ref, first_ref, second_ref, *refs):
    weight_refs, (feats_ref, row_ref, colval_ref) = refs[:3], refs[3:]
    width = first_ref.shape[1]
    split = seq_ref.shape[1] // width
    halos = []
    for ref in (first_ref, second_ref):
        tail = ref[half * GROUP :, :].astype(F32)
        pieces = [tail[j * GROUP : (j + 1) * GROUP] for j in range(split)]
        halos.append(jnp.concatenate(pieces, axis=1))
    above, below = received(*halos)
    feats = jnp.concatenate([above, seq_ref[...].astype(F32), below], axis=0).astype(BF16)
    feats_ref[...] = feats
    project(feats, weight_refs, row_ref, colval_ref)


def advance(sum_refs, feats_ref, out_ref, root):
    total = sum_refs[0][...]
    for ref in sum_refs[1:]:
        total = total + ref[...]
    gathered = (total / root).T.astype(BF16)
    change = jnp.dot(gathered, out_ref[...], preferred_element_type=F32)
    return feats_ref[...].astype(F32) + change


def middle_kernel(root, parts, *refs):
    sum_refs, refs = refs[:parts], refs[parts:]
    feats_in, out_w, weight_refs, (feats_ref, row_ref, colval_ref) = (
        refs[0], refs[1], refs[2:5], refs[5:]
    )
    feats = advance(sum_refs, feats_in, out_w, root).astype(BF16)
    feats_ref[...] = feats
    project(feats, weight_refs, row_ref, colval_ref)


def finish_kernel(root, parts, *refs):
    sum_refs, refs = refs[:parts], refs[parts:]
    feats_in, out_w, own_ref, far_ref, seq_ref, pair_ref = refs
    rep = lax.axis_index("rep")
    rows, cols = seq_ref.shape[0], own_ref.shape[2]
    seq_ref[...] = advance(sum_refs, feats_in, out_w, root)[HALO : HALO + rows].astype(BF16)
    pair_ref[:, :, pl.ds(pl.multiple_of(rep * cols, LANES), cols)] = own_ref[...]
    pair_ref[:, :, pl.ds(pl.multiple_of((1 - rep) * cols, LANES), cols)] = far_ref[...]


def spans(low_row, high_row, stride, total):
    low = low_row * stride // LANES * LANES
    size = -(-(high_row * stride - low) // 256) * 256
    high = min(low + size, total)
    return [(at, min(at + CHUNK, high)) for at in range(low, high, CHUNK)]


def cycle_kernel(rows, cols, length, last, sources, windows, *refs):
    (start_buf, hidden_buf, taps_first, taps_second, stack, mask, raw), refs = refs[-7:], refs[:-7]
    pair_refs, refs = refs[:sources], refs[sources:]
    row_ref, window_refs, refs = refs[0], refs[1 : 1 + windows], refs[1 + windows :]
    first_ref, second_ref, spread_row, spread_col, collect, place_ref, *outs = refs
    channels = row_ref.shape[0]
    stride = cols + 2 * HALO
    tall = rows + 2 * HALO
    total = tall * stride
    strip = GROUP * stride
    strips = tall // GROUP
    guard = LANES
    reach = 2 * stride
    far = -(-reach // LANES) * LANES
    rep = lax.axis_index("rep")
    row_index = lax.axis_index("row")
    chunk_index = lax.axis_index("col") * 2 + rep
    margin = 2 * CYCLES * 2 - (8 if not last else 4)
    spans_in = spans(margin, rows + 2 * HALO - margin, stride, total)
    spans_mid = spans(margin + 2, rows + 2 * HALO - margin - 2, stride, total)
    spans_out = spans(margin + 4, rows + 2 * HALO - margin - 4, stride, total)

    for k in range(strips):
        row_at = row_index * rows - HALO + k * GROUP + place_ref[0:1, :]
        col_at = chunk_index * cols - HALO + place_ref[1:2, :]
        inside = (row_at >= 0) & (row_at < length) & (col_at >= 0) & (col_at < length)
        mask[:, k * strip : (k + 1) * strip] = jnp.where(inside, 1.0, 0.0)

    turn = lax.rem(row_index, windows)
    for n, ref in enumerate((first_ref, second_ref)):
        lines = []
        for ti in range(3):
            blocks = [ref[3 * ti + tj].astype(F32) for tj in range(3)]
            lines.append(jnp.concatenate(blocks, axis=1))
        stack[n] = jnp.concatenate(lines, axis=0).astype(BF16)

    ordered = []
    for offset in range(windows):
        value = window_refs[0][...]
        for t in range(1, windows):
            piece = lax.rem(t - turn + windows, windows)
            value = jnp.where(piece == offset, window_refs[t][...], value)
        low = 0 if offset == 0 else HALO
        high = rows + (2 * HALO if offset == windows - 1 else HALO)
        ordered.append(value[:, low:high].astype(F32))
    colval = jnp.concatenate(ordered, axis=1).astype(BF16)
    colval = jnp.dot(colval, spread_col[...], preferred_element_type=F32)
    col_flat, val_flat = colval[:channels], colval[channels:]

    for buf, edge, part in (
        (start_buf, guard, ((0, total),)), (hidden_buf, guard, spans_mid),
        (taps_first, far, spans_in), (taps_second, far, spans_mid),
    ):
        low, high = part[0][0], part[-1][1]
        fill = jnp.zeros((buf.shape[0], edge), buf.dtype)
        buf[:, low : low + edge] = fill
        buf[:, high + edge : high + 2 * edge] = fill

    if sources > 1:
        unpack((pair_refs[0:3], pair_refs[3:6]), pair_refs[6], raw, cols)

    def pair_strip(k):
        if sources > 1:
            return raw_strip(raw, k)
        return pair_refs[0][:, k * strip : (k + 1) * strip].astype(F32)

    def start_strip(k):
        row_flat = jnp.dot(
            row_ref[:, k * GROUP : (k + 1) * GROUP], spread_row[...], preferred_element_type=F32
        )
        value = pair_strip(k) + row_flat + col_flat
        value = jnp.where(mask[:, k * strip : (k + 1) * strip] > 0, value, 0.0)
        start_buf[:, guard + k * strip : guard + (k + 1) * strip] = value.astype(BF16)

    def spread(source, taps, n, low, high):
        window = source[:, low : high + 2 * guard]
        stacked = jnp.concatenate(
            [window[:, guard + d : guard + d + high - low] for d in (-2, 0, 2)], axis=0
        )
        taps[:, far + low : far + high] = jnp.dot(
            stack[n], stacked, preferred_element_type=F32
        )

    def gather(taps, low, high):
        size = high - low
        value = taps[channels : 2 * channels, far + low : far + high]
        for part, lane in ((0, far + low - reach), (2, far + low + reach)):
            begin = lane // LANES * LANES
            end = -(-(lane + size) // LANES) * LANES
            window = taps[part * channels : (part + 1) * channels, begin:end]
            value = value + window[:, lane - begin : lane - begin + size]
        return jnp.maximum(value, 0.0)

    def first_span(low, high):
        spread(start_buf, taps_first, 0, low, high)

    def hidden_span(low, high):
        value = jnp.where(mask[:, low:high] > 0, gather(taps_first, low, high), 0.0)
        hidden_buf[:, guard + low : guard + high] = value.astype(BF16)

    def second_span(low, high):
        spread(hidden_buf, taps_second, 1, low, high)

    def pair_span(low, high):
        value = gather(taps_second, low, high)
        pair = start_buf[:, guard + low : guard + high].astype(F32) + value
        start_buf[:, guard + low : guard + high] = pair.astype(BF16)

    def gate_strip(k):
        pair = start_buf[:, guard + k * strip : guard + (k + 1) * strip]
        wide = pair.astype(F32)
        gate = jax.nn.sigmoid(wide).astype(BF16)
        product = (gate.astype(F32) * val_flat).astype(BF16)
        outs[0][:, k * GROUP : (k + 1) * GROUP] = jnp.dot(
            product, collect[...], preferred_element_type=F32
        )
        if not last:
            outs[1][:, k * strip : (k + 1) * strip] = pair
        else:
            for i in range(GROUP):
                for t in range(cols // LANES):
                    at = i * stride + HALO + t * LANES
                    flat = raw.at[t].reshape(channels * tall, LANES)
                    flat[pl.ds(k * GROUP + i, channels, stride=tall), :] = wide[:, at : at + LANES]

    strip_spans = [(k * strip, (k + 1) * strip) for k in range(strips)]
    stages = [
        (strip_spans, lambda low, high: start_strip(low // strip), 0),
        (spans_in, first_span, guard),
        (spans_mid, hidden_span, reach),
        (spans_mid, second_span, guard),
        (spans_out, pair_span, reach),
        (strip_spans, lambda low, high: gate_strip(low // strip), 0),
    ]
    done, made = [0] * len(stages), [0] * len(stages)

    def ready(n):
        parts, _, ahead = stages[n]
        if done[n] == len(parts):
            return False
        if n == 0 or done[n - 1] == len(stages[n - 1][0]):
            return True
        return parts[done[n]][1] + ahead <= made[n - 1]

    while any(done[n] < len(stages[n][0]) for n in range(len(stages))):
        for n in reversed(range(len(stages))):
            if ready(n):
                low, high = stages[n][0][done[n]]
                stages[n][1](low, high)
                done[n], made[n] = done[n] + 1, high

    if last:
        half = channels // 2
        for t in range(cols // LANES):
            lanes = slice(t * LANES, (t + 1) * LANES)
            for out, owner in ((outs[1], rep), (outs[2], 1 - rep)):
                value = raw[t, pl.ds(owner * half, half), HALO : HALO + rows, :]
                out[:, :, lanes] = value.astype(BF16)


def run_cycle(pieces, row_proj, windows, first, second, rows, cols, length, last):
    channels = row_proj.shape[0]
    stride = cols + 2 * HALO
    total = (rows + 2 * HALO) * stride
    strip = GROUP * stride
    lane = np.arange(strip)
    place = np.stack([lane // stride, lane % stride] + [0 * lane] * 6).astype(np.int32)
    spread_row = (place[0] == np.arange(GROUP)[:, None]).astype(BF16)
    spread_col = (place[1] == np.arange(stride)[:, None]).astype(BF16)
    inner = (place[1] >= HALO) & (place[1] < HALO + cols)
    collect = (spread_row.T.astype(np.float32) * inner[:, None]).astype(BF16)
    far = -(-2 * stride // LANES) * LANES
    sums = ((channels, rows + 2 * HALO), F32)
    half = ((channels // 2, rows, cols), BF16)
    outs = (sums, half, half) if last else (sums, ((channels, total), BF16))
    scratch = [
        pltpu.VMEM((channels, total + 2 * LANES), BF16),
        pltpu.VMEM((channels, total + 2 * LANES), BF16),
        pltpu.VMEM((3 * channels, total + 2 * far), F32),
        pltpu.VMEM((3 * channels, total + 2 * far), F32),
        pltpu.VMEM((2, 3 * channels, 3 * channels), BF16),
        pltpu.VMEM((1, total), F32),
        pltpu.VMEM((cols // LANES + 1, channels, rows + 2 * HALO, LANES), F32),
    ]
    kernel = functools.partial(cycle_kernel, rows, cols, length, last, len(pieces), len(windows))
    near = tuple(range(1, len(pieces))) + tuple(
        len(pieces) + 1 + t for t in range(len(windows))
    )
    return call(
        kernel, outs, scratch, *pieces, row_proj, *windows, first, second,
        spread_row, spread_col, collect, place,
        near=near, limit=57, flops=40 * channels * channels * total,
    )


def on_device(seq_in, pair_in, w_row, w_col, w_value, conv_first, conv_second, w_out):
    rows, features = seq_in.shape
    channels = w_row.shape[1]
    half = channels // 2
    cols = pair_in.shape[2] // 2
    stride = cols + 2 * HALO
    tall = rows + 2 * HALO
    row_size, col_size = lax.axis_size("row"), lax.axis_size("col")
    chunks = 2 * col_size
    length = rows * row_size
    windows = cols // rows
    root = np.float32(np.sqrt(np.float32(length)))
    every = ("row", "col", "rep")
    weights = (w_row.T, w_col.T, w_value.T)
    swap = [(0, 1), (1, 0)]

    def pairs(begin, size):
        moves = []
        for i in range(begin, size - 1, 2):
            moves += [(i, i + 1), (i + 1, i)]
        return moves

    across = pairs(1, chunks)
    if chunks == 4:
        across += [(0, 3), (3, 0)]

    def to_columns(value):
        results = []
        for t in range(windows):
            moves = []
            for r in range(row_size):
                for q in range(chunks):
                    source = windows * q + (t - r) % windows
                    moves.append((source * chunks + r // windows, r * chunks + q))
            results.append(lax.ppermute(value, every, moves))
        return results

    def all_parts(value):
        if chunks & (chunks - 1):
            partners = [[(i, (i + b) % chunks) for i in range(chunks)] for b in range(1, chunks)]
        else:
            partners = [[(i, i ^ b) for i in range(chunks)] for b in range(1, chunks)]
        return [value] + [lax.ppermute(value, ("col", "rep"), moves) for moves in partners]

    far_pair = lax.ppermute(pair_in, "rep", swap)
    width = pair_in.shape[2]
    message = ((-(-GROUP * (half + features // width) // 16) * 16, width), BF16)
    first_out, second_out = call(strips_kernel, [message, message], [], pair_in, seq_in)
    first = lax.ppermute(first_out, "row", pairs(0, row_size))
    second = lax.ppermute(second_out, "row", pairs(1, row_size))
    wide = [((tall, features), BF16), ((channels, tall), BF16), ((2 * channels, tall), BF16)]
    feats, row_proj, colval = call(
        functools.partial(project_kernel, half), wide, [],
        seq_in, first, second, *weights, near=(1, 2),
    )
    col_windows = to_columns(colval)
    first_far = lax.ppermute(first, "rep", swap)
    second_far = lax.ppermute(second, "rep", swap)
    pieces = (pair_in, first, second, far_pair, first_far, second_far)
    (edge,) = call(
        edges_kernel, [((channels * GROUP, LANES), BF16)], [], *pieces, near=(1, 2, 3, 4, 5)
    )
    pieces += (lax.ppermute(edge, ("col", "rep"), across),)

    sums, pair = run_cycle(
        pieces, row_proj, col_windows, conv_first, conv_second, rows, cols, length, False
    )
    parts = all_parts(sums)
    near = tuple(range(1, chunks))
    feats, row_proj, colval = call(
        functools.partial(middle_kernel, root, chunks), wide, [],
        *parts, feats, w_out, *weights, near=near,
    )
    col_windows = to_columns(colval)
    sums, own, send = run_cycle(
        (pair,), row_proj, col_windows, conv_first, conv_second, rows, cols, length, True
    )
    parts = all_parts(sums)
    far_half = lax.ppermute(send, "rep", swap)
    return call(
        functools.partial(finish_kernel, root, chunks),
        [(seq_in.shape, BF16), (pair_in.shape, BF16)], [],
        *parts, feats, w_out, own, far_half, near=near + (chunks + 3,),
    )


def solution(mesh):
    in_specs = (
        P(("grp", "row"), None),
        P(("grp", "rep"), "row", "col"),
        P(),
        P(),
        P(),
        P(),
        P(),
        P(),
    )
    out_specs = (P(("grp", "row"), None), P(("grp", "rep"), "row", "col"))
    return jax.shard_map(
        on_device, mesh=mesh, in_specs=in_specs, out_specs=out_specs, check_vma=False
    )
```

```python
import functools

import jax
import jax.numpy as jnp
import numpy as np
from jax import lax
from jax.experimental import pallas as pl
from jax.experimental.pallas import tpu as pltpu
from jax.sharding import PartitionSpec as P

CYCLES = 2
HALO = 8
GROUP = 8
LANES = 128
CHUNK = 3840
F32, BF16 = jnp.float32, jnp.bfloat16
def call(kernel, outs, scratch, *args, space=pltpu.VMEM, limit=16, flops=1 << 20):
    moved = sum(int(np.prod(x.shape)) * x.dtype.itemsize for x in args)
    return pl.pallas_call(
        kernel,
        out_shape=tuple(jax.ShapeDtypeStruct(shape, dtype) for shape, dtype in outs),
        in_specs=[pl.BlockSpec(memory_space=space)] * len(args),
        out_specs=(pl.BlockSpec(memory_space=pltpu.VMEM),) * len(outs),
        scratch_shapes=scratch,
        compiler_params=pltpu.CompilerParams(vmem_limit_bytes=limit << 20),
        cost_estimate=pl.CostEstimate(flops=flops, bytes_accessed=moved, transcendentals=0),
    )(*args)


def lane_ids(shape):
    return lax.broadcasted_iota(jnp.int32, shape, len(shape) - 1)


def is_even():
    return lax.rem(lax.axis_index("row"), 2) == 0


def strips_kernel(tile_ref, seq_ref, first_ref, second_ref, tile_ends, seq_ends, sems):
    half, rows, width = tile_ref.shape
    even = is_even()

    def message(pair, seq):
        pieces = [pair.reshape(half * GROUP, width)]
        pieces += [seq[:, at : at + width] for at in range(0, seq.shape[1], width)]
        rest = first_ref.shape[0] - GROUP * (half + len(pieces) - 1)
        if rest:
            pieces.append(jnp.zeros((rest, width), F32))
        return jnp.concatenate(pieces, axis=0)

    moves = []
    for n, at in enumerate((0, rows - 2 * GROUP)):
        lines = pl.ds(at, 2 * GROUP)
        moves += [
            pltpu.make_async_copy(tile_ref.at[:, lines, :], tile_ends.at[n], sems.at[2 * n]),
            pltpu.make_async_copy(seq_ref.at[lines, :], seq_ends.at[n], sems.at[2 * n + 1]),
        ]
    for move in moves:
        move.start()
    for move in moves:
        move.wait()
    top = message(
        tile_ends[0].astype(F32)[:, :GROUP], seq_ends[0].astype(F32)[:GROUP]
    )
    bottom = message(
        tile_ends[1].astype(F32)[:, GROUP:], seq_ends[1].astype(F32)[GROUP:]
    )
    first_ref[...] = jnp.where(even, bottom, top).astype(BF16)
    second_ref[...] = jnp.where(even, top, bottom).astype(BF16)


def received(first, second):
    even = is_even()
    return jnp.where(even, second, first), jnp.where(even, first, second)


def tile_pieces(tile_ref, first_ref, second_ref, at):
    half, rows, _ = tile_ref.shape
    middle = tile_ref[:, :, pl.ds(at, LANES)].astype(F32)
    above, below = received(
        *(
            ref[0 : half * GROUP, pl.ds(at, LANES)].astype(F32).reshape(half, GROUP, LANES)
            for ref in (first_ref, second_ref)
        )
    )
    middle = [middle[:, m * GROUP : (m + 1) * GROUP] for m in range(rows // GROUP)]
    return [above, *middle, below]


def edges_kernel(*refs):
    parts, out_ref = (refs[0:3], refs[3:6]), refs[6]
    rep = lax.axis_index("rep")
    half, _, width = refs[0].shape
    lane = lane_ids((half, GROUP, LANES))
    at = pl.multiple_of(jnp.where(rep == 0, 0, width - LANES), LANES)
    for part in range(2):
        packed = jnp.zeros((half, GROUP, LANES), F32)
        turn = jnp.where(rep == 0, 0, HALO)
        for g, piece in enumerate(tile_pieces(*parts[part], at)):
            moved = pltpu.roll(piece, turn + HALO * g, 2)
            packed = jnp.where((lane >= HALO * g) & (lane < HALO * (g + 1)), moved, packed)
        base = (rep if part == 0 else 1 - rep) * half * GROUP
        out_ref[pl.ds(pl.multiple_of(base, 2 * GROUP), half * GROUP), :] = packed.reshape(
            half * GROUP, LANES
        ).astype(BF16)


def unpack(parts, edge_ref, raw, cols):
    rep = lax.axis_index("rep")
    across = cols // LANES
    half = parts[0][0].shape[0]
    inner_at = pl.multiple_of(jnp.where(rep == 0, cols, cols - LANES), LANES)
    is_outer = (lane_ids((half, GROUP, LANES)) < HALO) == (rep == 0)
    for part in range(2):
        owner = pl.ds((rep if part == 0 else 1 - rep) * half, half)
        for t in range(across):
            at = pl.multiple_of(rep * cols + t * LANES, LANES)
            for g, piece in enumerate(tile_pieces(*parts[part], at)):
                raw[t, owner, g * GROUP : (g + 1) * GROUP, :] = piece
        base = (rep if part == 0 else 1 - rep) * half * GROUP
        edge = edge_ref[pl.ds(pl.multiple_of(base, 2 * GROUP), half * GROUP), :].astype(F32)
        edge = edge.reshape(half, GROUP, LANES)
        outer = pltpu.roll(edge, jnp.where(rep == 0, 0, HALO), 2)
        for g, piece in enumerate(tile_pieces(*parts[part], inner_at)):
            raw[across, owner, g * GROUP : (g + 1) * GROUP, :] = jnp.where(
                is_outer,
                pltpu.roll(outer, (-HALO * g) % LANES, 2),
                pltpu.roll(piece, HALO, 2),
            )


def raw_strip(raw, place):
    across, channels, rows, _ = raw.shape
    pieces = []
    for i in range(place * GROUP, (place + 1) * GROUP):
        tiles = [
            raw.at[t].reshape(channels * rows, LANES)[pl.ds(i, channels, stride=rows), :]
            for t in range(across)
        ]
        side = tiles.pop()
        pieces += [side[:, :HALO], *tiles, side[:, HALO : 2 * HALO]]
    return jnp.concatenate(pieces, axis=1)


def project(feats, weight_refs, row_ref, colval_ref):
    row, col, value = (
        lax.dot_general(ref[...], feats, (((1,), (1,)), ((), ())), preferred_element_type=F32)
        for ref in weight_refs
    )
    channels = row.shape[0]
    row_ref[...] = row.astype(BF16)
    colval_ref[0:channels] = col.astype(BF16)
    colval_ref[channels:] = value.astype(BF16)


def project_kernel(half, seq_ref, first_ref, second_ref, *refs):
    weight_refs, (feats_ref, row_ref, colval_ref) = refs[:3], refs[3:]
    width = first_ref.shape[1]
    split = seq_ref.shape[1] // width
    halos = []
    for ref in (first_ref, second_ref):
        tail = ref[half * GROUP :, :].astype(F32)
        pieces = [tail[j * GROUP : (j + 1) * GROUP] for j in range(split)]
        halos.append(jnp.concatenate(pieces, axis=1))
    above, below = received(*halos)
    feats = jnp.concatenate([above, seq_ref[...].astype(F32), below], axis=0).astype(BF16)
    feats_ref[...] = feats
    project(feats, weight_refs, row_ref, colval_ref)


def advance(sum_refs, feats_ref, out_ref, root):
    total = sum_refs[0][...]
    for ref in sum_refs[1:]:
        total = total + ref[...]
    gathered = (total / root).T.astype(BF16)
    change = jnp.dot(gathered, out_ref[...], preferred_element_type=F32)
    return feats_ref[...].astype(F32) + change


def middle_kernel(root, parts, *refs):
    sum_refs, refs = refs[:parts], refs[parts:]
    feats_in, out_w, weight_refs, (feats_ref, row_ref, colval_ref) = (
        refs[0], refs[1], refs[2:5], refs[5:]
    )
    feats = advance(sum_refs, feats_in, out_w, root).astype(BF16)
    feats_ref[...] = feats
    project(feats, weight_refs, row_ref, colval_ref)


def finish_kernel(root, parts, *refs):
    sum_refs, refs = refs[:parts], refs[parts:]
    feats_in, out_w, own_ref, far_ref, seq_ref, pair_ref = refs
    rep = lax.axis_index("rep")
    rows, cols = seq_ref.shape[0], own_ref.shape[2]
    seq_ref[...] = advance(sum_refs, feats_in, out_w, root)[HALO : HALO + rows].astype(BF16)
    pair_ref[:, :, pl.ds(pl.multiple_of(rep * cols, LANES), cols)] = own_ref[...]
    pair_ref[:, :, pl.ds(pl.multiple_of((1 - rep) * cols, LANES), cols)] = far_ref[...]


def spans(low_row, high_row, stride, total):
    low = low_row * stride // LANES * LANES
    size = -(-(high_row * stride - low) // 256) * 256
    high = min(low + size, total)
    return [(at, min(at + CHUNK, high)) for at in range(low, high, CHUNK)]


def cycle_kernel(rows, cols, length, last, sources, windows, *refs):
    (start_buf, hidden_buf, *taps, stack, mask, raw), refs = refs[-9:], refs[:-9]
    taps_first, taps_second = taps[0:2], taps[2:4]
    pair_refs, refs = refs[:sources], refs[sources:]
    row_ref, window_refs, refs = refs[0], refs[1 : 1 + windows], refs[1 + windows :]
    first_ref, second_ref, spread_row, spread_col, collect, place_ref, *outs = refs
    channels = row_ref.shape[0]
    stride = cols + 2 * HALO
    tall = rows + 2 * HALO
    total = tall * stride
    strip = GROUP * stride
    strips = tall // GROUP
    guard = LANES
    reach = 2 * stride
    far = -(-reach // LANES) * LANES
    rep = lax.axis_index("rep")
    row_index = lax.axis_index("row")
    chunk_index = lax.axis_index("col") * 2 + rep
    margin = 2 * CYCLES * 2 - (8 if not last else 4)
    spans_in = spans(margin, rows + 2 * HALO - margin, stride, total)
    spans_mid = spans(margin + 2, rows + 2 * HALO - margin - 2, stride, total)
    spans_out = spans(margin + 4, rows + 2 * HALO - margin - 4, stride, total)

    for k in range(strips):
        row_at = row_index * rows - HALO + k * GROUP + place_ref[0:1, :]
        col_at = chunk_index * cols - HALO + place_ref[1:2, :]
        inside = (row_at >= 0) & (row_at < length) & (col_at >= 0) & (col_at < length)
        mask[:, k * strip : (k + 1) * strip] = jnp.where(inside, 1.0, 0.0)

    turn = lax.rem(row_index, windows)
    for n, ref in enumerate((first_ref, second_ref)):
        lines = []
        for ti in (1, 0, 2):
            blocks = [ref[3 * ti + tj].astype(F32) for tj in range(3)]
            lines.append(jnp.concatenate(blocks, axis=1))
        stack[n] = jnp.concatenate(lines, axis=0).astype(BF16)

    ordered = []
    for offset in range(windows):
        value = window_refs[0][...]
        for t in range(1, windows):
            piece = lax.rem(t - turn + windows, windows)
            value = jnp.where(piece == offset, window_refs[t][...], value)
        low = 0 if offset == 0 else HALO
        high = rows + (2 * HALO if offset == windows - 1 else HALO)
        ordered.append(value[:, low:high].astype(F32))
    colval = jnp.concatenate(ordered, axis=1).astype(BF16)
    colval = jnp.dot(colval, spread_col[...], preferred_element_type=F32)
    col_flat, val_flat = colval[:channels], colval[channels:]

    for buf, edge, part in (
        (start_buf, guard, ((0, total),)), (hidden_buf, guard, spans_mid),
        (taps_first[1], far, spans_in), (taps_second[1], far, spans_mid),
    ):
        low, high = part[0][0], part[-1][1]
        fill = jnp.zeros((buf.shape[0], edge), buf.dtype)
        buf[:, low : low + edge] = fill
        buf[:, high + edge : high + 2 * edge] = fill

    if sources > 1:
        unpack((pair_refs[0:3], pair_refs[3:6]), pair_refs[6], raw, cols)

    def pair_strip(k):
        if sources > 1:
            return raw_strip(raw, k)
        return pair_refs[0][:, k * strip : (k + 1) * strip].astype(F32)

    def start_strip(k):
        row_flat = jnp.dot(
            row_ref[:, k * GROUP : (k + 1) * GROUP], spread_row[...], preferred_element_type=F32
        )
        value = pair_strip(k) + row_flat + col_flat
        value = jnp.where(mask[:, k * strip : (k + 1) * strip] > 0, value, 0.0)
        start_buf[:, guard + k * strip : guard + (k + 1) * strip] = value.astype(BF16)

    def spread(source, taps, n, low, high):
        window = source[:, low : high + 2 * guard]
        stacked = jnp.concatenate(
            [window[:, guard + d : guard + d + high - low] for d in (-2, 0, 2)], axis=0
        )
        result = jnp.dot(stack[n], stacked, preferred_element_type=F32)
        taps[0][:, low:high] = result[:channels]
        taps[1][:, far + low : far + high] = result[channels:].astype(BF16)

    def gather(taps, low, high):
        size = high - low
        value = taps[0][:, low:high]
        for part, lane in ((0, far + low - reach), (1, far + low + reach)):
            begin = lane // LANES * LANES
            end = -(-(lane + size) // LANES) * LANES
            window = taps[1][part * channels : (part + 1) * channels, begin:end]
            value = value + window[:, lane - begin : lane - begin + size].astype(F32)
        return jnp.maximum(value, 0.0)

    def first_span(low, high):
        spread(start_buf, taps_first, 0, low, high)

    def hidden_span(low, high):
        value = jnp.where(mask[:, low:high] > 0, gather(taps_first, low, high), 0.0)
        hidden_buf[:, guard + low : guard + high] = value.astype(BF16)

    def second_span(low, high):
        spread(hidden_buf, taps_second, 1, low, high)

    def pair_span(low, high):
        value = gather(taps_second, low, high)
        pair = start_buf[:, guard + low : guard + high].astype(F32) + value
        start_buf[:, guard + low : guard + high] = pair.astype(BF16)

    def gate_strip(k):
        pair = start_buf[:, guard + k * strip : guard + (k + 1) * strip]
        wide = pair.astype(F32)
        gate = jax.nn.sigmoid(wide).astype(BF16)
        product = (gate.astype(F32) * val_flat).astype(BF16)
        outs[0][:, k * GROUP : (k + 1) * GROUP] = jnp.dot(
            product, collect[...], preferred_element_type=F32
        )
        if not last:
            outs[1][:, k * strip : (k + 1) * strip] = pair
        else:
            for i in range(GROUP):
                for t in range(cols // LANES):
                    at = i * stride + HALO + t * LANES
                    flat = raw.at[t].reshape(channels * tall, LANES)
                    flat[pl.ds(k * GROUP + i, channels, stride=tall), :] = wide[:, at : at + LANES]

    strip_spans = [(k * strip, (k + 1) * strip) for k in range(strips)]
    stages = [
        (strip_spans, lambda low, high: start_strip(low // strip), 0),
        (spans_in, first_span, guard),
        (spans_mid, hidden_span, reach),
        (spans_mid, second_span, guard),
        (spans_out, pair_span, reach),
        (strip_spans, lambda low, high: gate_strip(low // strip), 0),
    ]
    done, made = [0] * len(stages), [0] * len(stages)

    def ready(n):
        parts, _, ahead = stages[n]
        if done[n] == len(parts):
            return False
        if n == 0 or done[n - 1] == len(stages[n - 1][0]):
            return True
        return parts[done[n]][1] + ahead <= made[n - 1]

    while any(done[n] < len(stages[n][0]) for n in range(len(stages))):
        for n in reversed(range(len(stages))):
            if ready(n):
                low, high = stages[n][0][done[n]]
                stages[n][1](low, high)
                done[n], made[n] = done[n] + 1, high

    if last:
        half = channels // 2
        for t in range(cols // LANES):
            lanes = slice(t * LANES, (t + 1) * LANES)
            for out, owner in ((outs[1], rep), (outs[2], 1 - rep)):
                value = raw[t, pl.ds(owner * half, half), HALO : HALO + rows, :]
                out[:, :, lanes] = value.astype(BF16)


def run_cycle(pieces, row_proj, windows, first, second, rows, cols, length, last):
    channels = row_proj.shape[0]
    stride = cols + 2 * HALO
    total = (rows + 2 * HALO) * stride
    strip = GROUP * stride
    lane = np.arange(strip)
    place = np.stack([lane // stride, lane % stride] + [0 * lane] * 6).astype(np.int32)
    spread_row = (place[0] == np.arange(GROUP)[:, None]).astype(BF16)
    spread_col = (place[1] == np.arange(stride)[:, None]).astype(BF16)
    inner = (place[1] >= HALO) & (place[1] < HALO + cols)
    collect = (spread_row.T.astype(np.float32) * inner[:, None]).astype(BF16)
    far = -(-2 * stride // LANES) * LANES
    sums = ((channels, rows + 2 * HALO), F32)
    half = ((channels // 2, rows, cols), BF16)
    outs = (sums, half, half) if last else (sums, ((channels, total), BF16))
    scratch = [
        pltpu.VMEM((channels, total + 2 * LANES), BF16),
        pltpu.VMEM((channels, total + 2 * LANES), BF16),
        pltpu.VMEM((channels, total), F32),
        pltpu.VMEM((2 * channels, total + 2 * far), BF16),
        pltpu.VMEM((channels, total), F32),
        pltpu.VMEM((2 * channels, total + 2 * far), BF16),
        pltpu.VMEM((2, 3 * channels, 3 * channels), BF16),
        pltpu.VMEM((1, total), F32),
        pltpu.VMEM((cols // LANES + 1, channels, rows + 2 * HALO, LANES), F32),
    ]
    kernel = functools.partial(cycle_kernel, rows, cols, length, last, len(pieces), len(windows))
    return call(
        kernel, outs, scratch, *pieces, row_proj, *windows, first, second,
        spread_row, spread_col, collect, place,
        limit=10 + total // 512, flops=40 * channels * channels * total,
    )


def on_device(seq_in, pair_in, w_row, w_col, w_value, conv_first, conv_second, w_out):
    rows, features = seq_in.shape
    channels = w_row.shape[1]
    half = channels // 2
    cols = pair_in.shape[2] // 2
    stride = cols + 2 * HALO
    tall = rows + 2 * HALO
    row_size, col_size = lax.axis_size("row"), lax.axis_size("col")
    chunks = 2 * col_size
    length = rows * row_size
    windows = cols // rows
    root = np.float32(np.sqrt(np.float32(length)))
    every = ("row", "col", "rep")
    weights = (w_row.T, w_col.T, w_value.T)
    swap = [(0, 1), (1, 0)]

    def pairs(begin, size):
        moves = []
        for i in range(begin, size - 1, 2):
            moves += [(i, i + 1), (i + 1, i)]
        return moves

    across = pairs(1, chunks)
    if chunks == 4:
        across += [(0, 3), (3, 0)]

    def to_columns(value):
        results = []
        for t in range(windows):
            moves = []
            for r in range(row_size):
                for q in range(chunks):
                    source = windows * q + (t - r) % windows
                    moves.append((source * chunks + r // windows, r * chunks + q))
            results.append(lax.ppermute(value, every, moves))
        return results

    def all_parts(value):
        if chunks & (chunks - 1):
            partners = [[(i, (i + b) % chunks) for i in range(chunks)] for b in range(1, chunks)]
        else:
            partners = [[(i, i ^ b) for i in range(chunks)] for b in range(1, chunks)]
        return [value] + [lax.ppermute(value, ("col", "rep"), moves) for moves in partners]

    far_pair = lax.ppermute(pair_in, "rep", swap)
    width = pair_in.shape[2]
    message = ((-(-GROUP * (half + features // width) // 16) * 16, width), BF16)
    first_out, second_out = call(
        strips_kernel, [message, message],
        [
            pltpu.VMEM((2, half, 2 * GROUP, width), BF16),
            pltpu.VMEM((2, 2 * GROUP, features), BF16),
            pltpu.SemaphoreType.DMA((4,)),
        ],
        pair_in, seq_in, space=pl.ANY, limit=56,
    )
    first = lax.ppermute(first_out, "row", pairs(0, row_size))
    second = lax.ppermute(second_out, "row", pairs(1, row_size))
    wide = [((tall, features), BF16), ((channels, tall), BF16), ((2 * channels, tall), BF16)]
    feats, row_proj, colval = call(
        functools.partial(project_kernel, half), wide, [],
        seq_in, first, second, *weights
    )
    col_windows = to_columns(colval)
    first_far = lax.ppermute(first, "rep", swap)
    second_far = lax.ppermute(second, "rep", swap)
    pieces = (pair_in, first, second, far_pair, first_far, second_far)
    (edge,) = call(
        edges_kernel, [((channels * GROUP, LANES), BF16)], [], *pieces
    )
    pieces += (lax.ppermute(edge, ("col", "rep"), across),)

    sums, pair = run_cycle(
        pieces, row_proj, col_windows, conv_first, conv_second, rows, cols, length, False
    )
    parts = all_parts(sums)
    feats, row_proj, colval = call(
        functools.partial(middle_kernel, root, chunks), wide, [],
        *parts, feats, w_out, *weights,
    )
    col_windows = to_columns(colval)
    sums, own, send = run_cycle(
        (pair,), row_proj, col_windows, conv_first, conv_second, rows, cols, length, True
    )
    parts = all_parts(sums)
    far_half = lax.ppermute(send, "rep", swap)
    return call(
        functools.partial(finish_kernel, root, chunks),
        [(seq_in.shape, BF16), (pair_in.shape, BF16)], [],
        *parts, feats, w_out, own, far_half,
    )


def solution(mesh):
    in_specs = (
        P(("grp", "row"), None),
        P(("grp", "rep"), "row", "col"),
        P(),
        P(),
        P(),
        P(),
        P(),
        P(),
    )
    out_specs = (P(("grp", "row"), None), P(("grp", "rep"), "row", "col"))
    return jax.shard_map(
        on_device, mesh=mesh, in_specs=in_specs, out_specs=out_specs, check_vma=False
    )
```

```python
import functools

import jax
import jax.numpy as jnp
import numpy as np
from jax import lax
from jax.experimental import pallas as pl
from jax.experimental.pallas import tpu as pltpu
from jax.sharding import PartitionSpec as P

CYCLES = 2
HALO = 8
GROUP = 8
LANES = 128
CHUNK = 3840
F32, BF16 = jnp.float32, jnp.bfloat16
def call(kernel, outs, scratch, *args, space=pltpu.VMEM, limit=16, flops=1 << 20):
    moved = sum(int(np.prod(x.shape)) * x.dtype.itemsize for x in args)
    return pl.pallas_call(
        kernel,
        out_shape=tuple(jax.ShapeDtypeStruct(shape, dtype) for shape, dtype in outs),
        in_specs=[pl.BlockSpec(memory_space=space)] * len(args),
        out_specs=(pl.BlockSpec(memory_space=pltpu.VMEM),) * len(outs),
        scratch_shapes=scratch,
        compiler_params=pltpu.CompilerParams(vmem_limit_bytes=limit << 20),
        cost_estimate=pl.CostEstimate(flops=flops, bytes_accessed=moved, transcendentals=0),
    )(*args)


def lane_ids(shape):
    return lax.broadcasted_iota(jnp.int32, shape, len(shape) - 1)


def is_even():
    return lax.rem(lax.axis_index("row"), 2) == 0


def strips_kernel(tile_ref, seq_ref, first_ref, second_ref, tile_ends, seq_ends, sems):
    half, rows, width = tile_ref.shape
    even = is_even()

    def message(pair, seq):
        pieces = [pair.reshape(half * GROUP, width)]
        pieces += [seq[:, at : at + width] for at in range(0, seq.shape[1], width)]
        rest = first_ref.shape[0] - GROUP * (half + len(pieces) - 1)
        if rest:
            pieces.append(jnp.zeros((rest, width), F32))
        return jnp.concatenate(pieces, axis=0)

    moves = []
    for n, at in enumerate((0, rows - 2 * GROUP)):
        lines = pl.ds(at, 2 * GROUP)
        moves += [
            pltpu.make_async_copy(tile_ref.at[:, lines, :], tile_ends.at[n], sems.at[2 * n]),
            pltpu.make_async_copy(seq_ref.at[lines, :], seq_ends.at[n], sems.at[2 * n + 1]),
        ]
    for move in moves:
        move.start()
    for move in moves:
        move.wait()
    top = message(
        tile_ends[0].astype(F32)[:, :GROUP], seq_ends[0].astype(F32)[:GROUP]
    )
    bottom = message(
        tile_ends[1].astype(F32)[:, GROUP:], seq_ends[1].astype(F32)[GROUP:]
    )
    first_ref[...] = jnp.where(even, bottom, top).astype(BF16)
    second_ref[...] = jnp.where(even, top, bottom).astype(BF16)


def received(first, second):
    even = is_even()
    return jnp.where(even, second, first), jnp.where(even, first, second)


def tile_pieces(tile_ref, first_ref, second_ref, at):
    half, rows, _ = tile_ref.shape
    middle = tile_ref[:, :, pl.ds(at, LANES)].astype(F32)
    above, below = received(
        *(
            ref[0 : half * GROUP, pl.ds(at, LANES)].astype(F32).reshape(half, GROUP, LANES)
            for ref in (first_ref, second_ref)
        )
    )
    middle = [middle[:, m * GROUP : (m + 1) * GROUP] for m in range(rows // GROUP)]
    return [above, *middle, below]


def edges_kernel(*refs):
    parts, out_ref = (refs[0:3], refs[3:6]), refs[6]
    rep = lax.axis_index("rep")
    half, _, width = refs[0].shape
    lane = lane_ids((half, GROUP, LANES))
    at = pl.multiple_of(jnp.where(rep == 0, 0, width - LANES), LANES)
    for part in range(2):
        packed = jnp.zeros((half, GROUP, LANES), F32)
        turn = jnp.where(rep == 0, 0, HALO)
        for g, piece in enumerate(tile_pieces(*parts[part], at)):
            moved = pltpu.roll(piece, turn + HALO * g, 2)
            packed = jnp.where((lane >= HALO * g) & (lane < HALO * (g + 1)), moved, packed)
        base = (rep if part == 0 else 1 - rep) * half * GROUP
        out_ref[pl.ds(pl.multiple_of(base, 2 * GROUP), half * GROUP), :] = packed.reshape(
            half * GROUP, LANES
        ).astype(BF16)


def unpack(parts, edge_ref, raw, cols):
    rep = lax.axis_index("rep")
    across = cols // LANES
    half = parts[0][0].shape[0]
    inner_at = pl.multiple_of(jnp.where(rep == 0, cols, cols - LANES), LANES)
    is_outer = (lane_ids((half, GROUP, LANES)) < HALO) == (rep == 0)
    for part in range(2):
        owner = pl.ds((rep if part == 0 else 1 - rep) * half, half)
        for t in range(across):
            at = pl.multiple_of(rep * cols + t * LANES, LANES)
            for g, piece in enumerate(tile_pieces(*parts[part], at)):
                raw[t, owner, g * GROUP : (g + 1) * GROUP, :] = piece
        base = (rep if part == 0 else 1 - rep) * half * GROUP
        edge = edge_ref[pl.ds(pl.multiple_of(base, 2 * GROUP), half * GROUP), :].astype(F32)
        edge = edge.reshape(half, GROUP, LANES)
        outer = pltpu.roll(edge, jnp.where(rep == 0, 0, HALO), 2)
        for g, piece in enumerate(tile_pieces(*parts[part], inner_at)):
            raw[across, owner, g * GROUP : (g + 1) * GROUP, :] = jnp.where(
                is_outer,
                pltpu.roll(outer, (-HALO * g) % LANES, 2),
                pltpu.roll(piece, HALO, 2),
            )


def raw_strip(raw, place):
    across, channels, rows, _ = raw.shape
    pieces = []
    for i in range(place * GROUP, (place + 1) * GROUP):
        tiles = [
            raw.at[t].reshape(channels * rows, LANES)[pl.ds(i, channels, stride=rows), :]
            for t in range(across)
        ]
        side = tiles.pop()
        pieces += [side[:, :HALO], *tiles, side[:, HALO : 2 * HALO]]
    return jnp.concatenate(pieces, axis=1)


def project(feats, weight_refs, row_ref, colval_ref):
    row, col, value = (
        lax.dot_general(ref[...], feats, (((1,), (1,)), ((), ())), preferred_element_type=F32)
        for ref in weight_refs
    )
    channels = row.shape[0]
    row_ref[...] = row.astype(BF16)
    colval_ref[0:channels] = col.astype(BF16)
    colval_ref[channels:] = value.astype(BF16)


def project_kernel(half, seq_ref, first_ref, second_ref, *refs):
    weight_refs, (feats_ref, row_ref, colval_ref) = refs[:3], refs[3:]
    width = first_ref.shape[1]
    split = seq_ref.shape[1] // width
    halos = []
    for ref in (first_ref, second_ref):
        tail = ref[half * GROUP :, :].astype(F32)
        pieces = [tail[j * GROUP : (j + 1) * GROUP] for j in range(split)]
        halos.append(jnp.concatenate(pieces, axis=1))
    above, below = received(*halos)
    feats = jnp.concatenate([above, seq_ref[...].astype(F32), below], axis=0).astype(BF16)
    feats_ref[...] = feats
    project(feats, weight_refs, row_ref, colval_ref)


def advance(sum_refs, feats_ref, out_ref, root):
    total = sum_refs[0][...]
    for ref in sum_refs[1:]:
        total = total + ref[...]
    gathered = (total / root).T.astype(BF16)
    change = jnp.dot(gathered, out_ref[...], preferred_element_type=F32)
    return feats_ref[...].astype(F32) + change


def middle_kernel(root, parts, *refs):
    sum_refs, refs = refs[:parts], refs[parts:]
    feats_in, out_w, weight_refs, (feats_ref, row_ref, colval_ref) = (
        refs[0], refs[1], refs[2:5], refs[5:]
    )
    feats = advance(sum_refs, feats_in, out_w, root).astype(BF16)
    feats_ref[...] = feats
    project(feats, weight_refs, row_ref, colval_ref)


def finish_kernel(root, parts, *refs):
    sum_refs, refs = refs[:parts], refs[parts:]
    feats_in, out_w, own_ref, far_ref, seq_ref, pair_ref = refs
    rep = lax.axis_index("rep")
    rows, cols = seq_ref.shape[0], own_ref.shape[2]
    seq_ref[...] = advance(sum_refs, feats_in, out_w, root)[HALO : HALO + rows].astype(BF16)
    pair_ref[:, :, pl.ds(pl.multiple_of(rep * cols, LANES), cols)] = own_ref[...]
    pair_ref[:, :, pl.ds(pl.multiple_of((1 - rep) * cols, LANES), cols)] = far_ref[...]


def spans(low_row, high_row, stride, total):
    low = low_row * stride // LANES * LANES
    size = -(-(high_row * stride - low) // 256) * 256
    high = min(low + size, total)
    return [(at, min(at + CHUNK, high)) for at in range(low, high, CHUNK)]


def cycle_kernel(rows, cols, length, last, sources, windows, *refs):
    (start_buf, hidden_buf, *taps, stack, mask, raw), refs = refs[-9:], refs[:-9]
    taps_first, taps_second = taps[0:2], taps[2:4]
    pair_refs, refs = refs[:sources], refs[sources:]
    row_ref, window_refs, refs = refs[0], refs[1 : 1 + windows], refs[1 + windows :]
    first_ref, second_ref, spread_row, spread_col, collect, place_ref, *outs = refs
    channels = row_ref.shape[0]
    stride = cols + 2 * HALO
    tall = rows + 2 * HALO
    total = tall * stride
    strip = GROUP * stride
    strips = tall // GROUP
    guard = LANES
    reach = 2 * stride
    far = -(-reach // LANES) * LANES
    rep = lax.axis_index("rep")
    row_index = lax.axis_index("row")
    chunk_index = lax.axis_index("col") * 2 + rep
    margin = 2 * CYCLES * 2 - (8 if not last else 4)
    spans_in = spans(margin, rows + 2 * HALO - margin, stride, total)
    spans_mid = spans(margin + 2, rows + 2 * HALO - margin - 2, stride, total)
    spans_out = spans(margin + 4, rows + 2 * HALO - margin - 4, stride, total)

    for k in range(strips):
        row_at = row_index * rows - HALO + k * GROUP + place_ref[0:1, :]
        col_at = chunk_index * cols - HALO + place_ref[1:2, :]
        inside = (row_at >= 0) & (row_at < length) & (col_at >= 0) & (col_at < length)
        mask[:, k * strip : (k + 1) * strip] = jnp.where(inside, 1.0, 0.0)

    turn = lax.rem(row_index, windows)
    for n, ref in enumerate((first_ref, second_ref)):
        lines = []
        for ti in (1, 0, 2):
            blocks = [ref[3 * ti + tj].astype(F32) for tj in range(3)]
            lines.append(jnp.concatenate(blocks, axis=1))
        stack[n] = jnp.concatenate(lines, axis=0).astype(BF16)

    ordered = []
    for offset in range(windows):
        value = window_refs[0][...]
        for t in range(1, windows):
            piece = lax.rem(t - turn + windows, windows)
            value = jnp.where(piece == offset, window_refs[t][...], value)
        low = 0 if offset == 0 else HALO
        high = rows + (2 * HALO if offset == windows - 1 else HALO)
        ordered.append(value[:, low:high].astype(F32))
    colval = jnp.concatenate(ordered, axis=1).astype(BF16)
    colval = jnp.dot(colval, spread_col[...], preferred_element_type=F32)
    col_flat, val_flat = colval[:channels], colval[channels:]

    for buf, edge, part in (
        (start_buf, guard, ((0, total),)), (hidden_buf, guard, spans_mid),
        (taps_first[1], far, spans_in), (taps_second[1], far, spans_mid),
    ):
        low, high = part[0][0], part[-1][1]
        fill = jnp.zeros((buf.shape[0], edge), buf.dtype)
        buf[:, low : low + edge] = fill
        buf[:, high + edge : high + 2 * edge] = fill

    if sources > 1:
        unpack((pair_refs[0:3], pair_refs[3:6]), pair_refs[6], raw, cols)

    def pair_strip(k):
        if sources > 1:
            return raw_strip(raw, k)
        return pair_refs[0][:, k * strip : (k + 1) * strip].astype(F32)

    def start_strip(k):
        row_flat = jnp.dot(
            row_ref[:, k * GROUP : (k + 1) * GROUP], spread_row[...], preferred_element_type=F32
        )
        value = pair_strip(k) + row_flat + col_flat
        value = jnp.where(mask[:, k * strip : (k + 1) * strip] > 0, value, 0.0)
        start_buf[:, guard + k * strip : guard + (k + 1) * strip] = value.astype(BF16)

    def spread(source, taps, n, low, high):
        window = source[:, low : high + 2 * guard]
        stacked = jnp.concatenate(
            [window[:, guard + d : guard + d + high - low] for d in (-2, 0, 2)], axis=0
        )
        result = jnp.dot(stack[n], stacked, preferred_element_type=F32)
        taps[0][:, low:high] = result[:channels]
        taps[1][:, far + low : far + high] = result[channels:].astype(BF16)

    def gather(taps, low, high):
        size = high - low
        value = taps[0][:, low:high]
        for part, lane in ((0, far + low - reach), (1, far + low + reach)):
            begin = lane // LANES * LANES
            end = -(-(lane + size) // LANES) * LANES
            window = taps[1][part * channels : (part + 1) * channels, begin:end]
            value = value + window[:, lane - begin : lane - begin + size].astype(F32)
        return jnp.maximum(value, 0.0)

    def first_span(low, high):
        spread(start_buf, taps_first, 0, low, high)

    def hidden_span(low, high):
        value = jnp.where(mask[:, low:high] > 0, gather(taps_first, low, high), 0.0)
        hidden_buf[:, guard + low : guard + high] = value.astype(BF16)

    def second_span(low, high):
        spread(hidden_buf, taps_second, 1, low, high)

    def pair_span(low, high):
        value = gather(taps_second, low, high)
        pair = start_buf[:, guard + low : guard + high].astype(F32) + value
        start_buf[:, guard + low : guard + high] = pair.astype(BF16)

    def gate_strip(k):
        pair = start_buf[:, guard + k * strip : guard + (k + 1) * strip]
        wide = pair.astype(F32)
        gate = jax.nn.sigmoid(wide).astype(BF16)
        product = (gate.astype(F32) * val_flat).astype(BF16)
        outs[0][:, k * GROUP : (k + 1) * GROUP] = jnp.dot(
            product, collect[...], preferred_element_type=F32
        )
        if not last:
            outs[1][:, k * strip : (k + 1) * strip] = pair
        else:
            for i in range(GROUP):
                for t in range(cols // LANES):
                    at = i * stride + HALO + t * LANES
                    flat = raw.at[t].reshape(channels * tall, LANES)
                    flat[pl.ds(k * GROUP + i, channels, stride=tall), :] = wide[:, at : at + LANES]

    strip_spans = [(k * strip, (k + 1) * strip) for k in range(strips)]
    stages = [
        (strip_spans, lambda low, high: start_strip(low // strip), 0),
        (spans_in, first_span, guard),
        (spans_mid, hidden_span, reach),
        (spans_mid, second_span, guard),
        (spans_out, pair_span, reach),
        (strip_spans, lambda low, high: gate_strip(low // strip), 0),
    ]
    done, made = [0] * len(stages), [0] * len(stages)

    def ready(n):
        parts, _, ahead = stages[n]
        if done[n] == len(parts):
            return False
        if n == 0 or done[n - 1] == len(stages[n - 1][0]):
            return True
        return parts[done[n]][1] + ahead <= made[n - 1]

    while any(done[n] < len(stages[n][0]) for n in range(len(stages))):
        for n in reversed(range(len(stages))):
            if ready(n):
                low, high = stages[n][0][done[n]]
                stages[n][1](low, high)
                done[n], made[n] = done[n] + 1, high

    if last:
        half = channels // 2
        for t in range(cols // LANES):
            lanes = slice(t * LANES, (t + 1) * LANES)
            for out, owner in ((outs[1], rep), (outs[2], 1 - rep)):
                value = raw[t, pl.ds(owner * half, half), HALO : HALO + rows, :]
                out[:, :, lanes] = value.astype(BF16)


def run_cycle(pieces, row_proj, windows, first, second, rows, cols, length, last):
    channels = row_proj.shape[0]
    stride = cols + 2 * HALO
    total = (rows + 2 * HALO) * stride
    strip = GROUP * stride
    lane = np.arange(strip)
    place = np.stack([lane // stride, lane % stride] + [0 * lane] * 6).astype(np.int32)
    spread_row = (place[0] == np.arange(GROUP)[:, None]).astype(BF16)
    spread_col = (place[1] == np.arange(stride)[:, None]).astype(BF16)
    inner = (place[1] >= HALO) & (place[1] < HALO + cols)
    collect = (spread_row.T.astype(np.float32) * inner[:, None]).astype(BF16)
    far = -(-2 * stride // LANES) * LANES
    sums = ((channels, rows + 2 * HALO), F32)
    half = ((channels // 2, rows, cols), BF16)
    outs = (sums, half, half) if last else (sums, ((channels, total), BF16))
    scratch = [
        pltpu.VMEM((channels, total + 2 * LANES), BF16),
        pltpu.VMEM((channels, total + 2 * LANES), BF16),
        pltpu.VMEM((channels, total), F32),
        pltpu.VMEM((2 * channels, total + 2 * far), BF16),
        pltpu.VMEM((channels, total), F32),
        pltpu.VMEM((2 * channels, total + 2 * far), BF16),
        pltpu.VMEM((2, 3 * channels, 3 * channels), BF16),
        pltpu.VMEM((1, total), F32),
        pltpu.VMEM((cols // LANES + 1, channels, rows + 2 * HALO, LANES), F32),
    ]
    kernel = functools.partial(cycle_kernel, rows, cols, length, last, len(pieces), len(windows))
    return call(
        kernel, outs, scratch, *pieces, row_proj, *windows, first, second,
        spread_row, spread_col, collect, place,
        limit=10 + total // 512, flops=40 * channels * channels * total,
    )


def on_device(seq_in, pair_in, w_row, w_col, w_value, conv_first, conv_second, w_out):
    rows, features = seq_in.shape
    channels = w_row.shape[1]
    half = channels // 2
    cols = pair_in.shape[2] // 2
    stride = cols + 2 * HALO
    tall = rows + 2 * HALO
    row_size, col_size = lax.axis_size("row"), lax.axis_size("col")
    chunks = 2 * col_size
    length = rows * row_size
    windows = cols // rows
    root = np.float32(np.sqrt(np.float32(length)))
    every = ("row", "col", "rep")
    weights = (w_row.T, w_col.T, w_value.T)
    swap = [(0, 1), (1, 0)]

    def pairs(begin, size):
        moves = []
        for i in range(begin, size - 1, 2):
            moves += [(i, i + 1), (i + 1, i)]
        return moves

    across = pairs(1, chunks)
    if chunks == 4:
        across += [(0, 3), (3, 0)]

    def to_columns(value):
        results = []
        for t in range(windows):
            moves = []
            for r in range(row_size):
                for q in range(chunks):
                    source = windows * q + (t - r) % windows
                    replica = (r // windows) ^ (chunks // 2)
                    moves.append((source * chunks + replica, r * chunks + q))
            results.append(lax.ppermute(value, every, moves))
        return results

    def all_parts(value):
        if chunks & (chunks - 1):
            partners = [[(i, (i + b) % chunks) for i in range(chunks)] for b in range(1, chunks)]
        else:
            partners = [[(i, i ^ b) for i in range(chunks)] for b in range(1, chunks)]
        return [value] + [lax.ppermute(value, ("col", "rep"), moves) for moves in partners]

    far_pair = lax.ppermute(pair_in, "rep", swap)
    width = pair_in.shape[2]
    message = ((-(-GROUP * (half + features // width) // 16) * 16, width), BF16)
    first_out, second_out = call(
        strips_kernel, [message, message],
        [
            pltpu.VMEM((2, half, 2 * GROUP, width), BF16),
            pltpu.VMEM((2, 2 * GROUP, features), BF16),
            pltpu.SemaphoreType.DMA((4,)),
        ],
        pair_in, seq_in, space=pl.ANY, limit=56,
    )
    second = lax.ppermute(second_out, "row", pairs(1, row_size))
    first = lax.ppermute(first_out, "row", pairs(0, row_size))
    wide = [((tall, features), BF16), ((channels, tall), BF16), ((2 * channels, tall), BF16)]
    feats, row_proj, colval = call(
        functools.partial(project_kernel, half), wide, [],
        seq_in, first, second, *weights
    )
    col_windows = to_columns(colval)
    first_far = lax.ppermute(first, "rep", swap)
    second_far = lax.ppermute(second, "rep", swap)
    pieces = (pair_in, first, second, far_pair, first_far, second_far)
    (edge,) = call(
        edges_kernel, [((channels * GROUP, LANES), BF16)], [], *pieces
    )
    pieces += (lax.ppermute(edge, ("col", "rep"), across),)

    sums, pair = run_cycle(
        pieces, row_proj, col_windows, conv_first, conv_second, rows, cols, length, False
    )
    parts = all_parts(sums)
    feats, row_proj, colval = call(
        functools.partial(middle_kernel, root, chunks), wide, [],
        *parts, feats, w_out, *weights,
    )
    col_windows = to_columns(colval)
    sums, own, send = run_cycle(
        (pair,), row_proj, col_windows, conv_first, conv_second, rows, cols, length, True
    )
    parts = all_parts(sums)
    far_half = lax.ppermute(send, "rep", swap)
    return call(
        functools.partial(finish_kernel, root, chunks),
        [(seq_in.shape, BF16), (pair_in.shape, BF16)], [],
        *parts, feats, w_out, own, far_half,
    )


def solution(mesh):
    in_specs = (
        P(("grp", "row"), None),
        P(("grp", "rep"), "row", "col"),
        P(),
        P(),
        P(),
        P(),
        P(),
        P(),
    )
    out_specs = (P(("grp", "row"), None), P(("grp", "rep"), "row", "col"))
    return jax.shard_map(
        on_device, mesh=mesh, in_specs=in_specs, out_specs=out_specs, check_vma=False
    )
```

```python
import functools

import jax
import jax.numpy as jnp
import numpy as np
from jax import lax
from jax.experimental import pallas as pl
from jax.experimental.pallas import tpu as pltpu
from jax.sharding import PartitionSpec as P

CYCLES = 2
HALO = 8
GROUP = 8
LANES = 128
CHUNK = 3840
F32, BF16 = jnp.float32, jnp.bfloat16
def call(kernel, outs, scratch, *args, space=pltpu.VMEM, limit=16, flops=1 << 20):
    moved = sum(int(np.prod(x.shape)) * x.dtype.itemsize for x in args)
    return pl.pallas_call(
        kernel,
        out_shape=tuple(jax.ShapeDtypeStruct(shape, dtype) for shape, dtype in outs),
        in_specs=[pl.BlockSpec(memory_space=space)] * len(args),
        out_specs=(pl.BlockSpec(memory_space=pltpu.VMEM),) * len(outs),
        scratch_shapes=scratch,
        compiler_params=pltpu.CompilerParams(vmem_limit_bytes=limit << 20),
        cost_estimate=pl.CostEstimate(flops=flops, bytes_accessed=moved, transcendentals=0),
    )(*args)


def lane_ids(shape):
    return lax.broadcasted_iota(jnp.int32, shape, len(shape) - 1)


def is_even():
    return lax.rem(lax.axis_index("row"), 2) == 0


def strips_kernel(tile_ref, seq_ref, first_ref, second_ref, tile_ends, seq_ends, sems):
    half, rows, width = tile_ref.shape
    even = is_even()

    def message(pair, seq):
        pieces = [pair.reshape(half * GROUP, width)]
        pieces += [seq[:, at : at + width] for at in range(0, seq.shape[1], width)]
        rest = first_ref.shape[0] - GROUP * (half + len(pieces) - 1)
        if rest:
            pieces.append(jnp.zeros((rest, width), F32))
        return jnp.concatenate(pieces, axis=0)

    moves = []
    for n, at in enumerate((0, rows - 2 * GROUP)):
        lines = pl.ds(at, 2 * GROUP)
        moves += [
            pltpu.make_async_copy(tile_ref.at[:, lines, :], tile_ends.at[n], sems.at[2 * n]),
            pltpu.make_async_copy(seq_ref.at[lines, :], seq_ends.at[n], sems.at[2 * n + 1]),
        ]
    for move in moves:
        move.start()
    for move in moves:
        move.wait()
    top = message(
        tile_ends[0].astype(F32)[:, :GROUP], seq_ends[0].astype(F32)[:GROUP]
    )
    bottom = message(
        tile_ends[1].astype(F32)[:, GROUP:], seq_ends[1].astype(F32)[GROUP:]
    )
    first_ref[...] = jnp.where(even, bottom, top).astype(BF16)
    second_ref[...] = jnp.where(even, top, bottom).astype(BF16)


def received(first, second):
    even = is_even()
    return jnp.where(even, first, second), jnp.where(even, second, first)


def tile_pieces(tile_ref, first_ref, second_ref, at):
    half, rows, _ = tile_ref.shape
    middle = tile_ref[:, :, pl.ds(at, LANES)].astype(F32)
    above, below = received(
        *(
            ref[0 : half * GROUP, pl.ds(at, LANES)].astype(F32).reshape(half, GROUP, LANES)
            for ref in (first_ref, second_ref)
        )
    )
    middle = [middle[:, m * GROUP : (m + 1) * GROUP] for m in range(rows // GROUP)]
    return [above, *middle, below]


def edges_kernel(*refs):
    parts, out_ref = (refs[0:3], refs[3:6]), refs[6]
    rep = lax.axis_index("rep")
    half, _, width = refs[0].shape
    lane = lane_ids((half, GROUP, LANES))
    at = pl.multiple_of(jnp.where(rep == 0, 0, width - LANES), LANES)
    for part in range(2):
        packed = jnp.zeros((half, GROUP, LANES), F32)
        turn = jnp.where(rep == 0, 0, HALO)
        for g, piece in enumerate(tile_pieces(*parts[part], at)):
            moved = pltpu.roll(piece, turn + HALO * g, 2)
            packed = jnp.where((lane >= HALO * g) & (lane < HALO * (g + 1)), moved, packed)
        base = (rep if part == 0 else 1 - rep) * half * GROUP
        out_ref[pl.ds(pl.multiple_of(base, 2 * GROUP), half * GROUP), :] = packed.reshape(
            half * GROUP, LANES
        ).astype(BF16)


def unpack(parts, edge_ref, raw, cols):
    rep = lax.axis_index("rep")
    across = cols // LANES
    half = parts[0][0].shape[0]
    inner_at = pl.multiple_of(jnp.where(rep == 0, cols, cols - LANES), LANES)
    is_outer = (lane_ids((half, GROUP, LANES)) < HALO) == (rep == 0)
    for part in range(2):
        owner = pl.ds((rep if part == 0 else 1 - rep) * half, half)
        for t in range(across):
            at = pl.multiple_of(rep * cols + t * LANES, LANES)
            for g, piece in enumerate(tile_pieces(*parts[part], at)):
                raw[t, owner, g * GROUP : (g + 1) * GROUP, :] = piece
        base = (rep if part == 0 else 1 - rep) * half * GROUP
        edge = edge_ref[pl.ds(pl.multiple_of(base, 2 * GROUP), half * GROUP), :].astype(F32)
        edge = edge.reshape(half, GROUP, LANES)
        outer = pltpu.roll(edge, jnp.where(rep == 0, 0, HALO), 2)
        for g, piece in enumerate(tile_pieces(*parts[part], inner_at)):
            raw[across, owner, g * GROUP : (g + 1) * GROUP, :] = jnp.where(
                is_outer,
                pltpu.roll(outer, (-HALO * g) % LANES, 2),
                pltpu.roll(piece, HALO, 2),
            )


def assemble_kernel(cols, *refs):
    parts, edge_ref, out_ref, raw = (refs[0:3], refs[3:6]), refs[6], refs[7], refs[8]
    unpack(parts, edge_ref, raw, cols)
    strip = GROUP * (cols + 2 * HALO)
    for k in range(raw.shape[2] // GROUP):
        out_ref[:, k * strip : (k + 1) * strip] = raw_strip(raw, k).astype(BF16)


def raw_strip(raw, place):
    across, channels, rows, _ = raw.shape
    pieces = []
    for i in range(place * GROUP, (place + 1) * GROUP):
        tiles = [
            raw.at[t].reshape(channels * rows, LANES)[pl.ds(i, channels, stride=rows), :]
            for t in range(across)
        ]
        side = tiles.pop()
        pieces += [side[:, :HALO], *tiles, side[:, HALO : 2 * HALO]]
    return jnp.concatenate(pieces, axis=1)


def project(feats, weight_refs, row_ref, colval_ref):
    row, col, value = (
        lax.dot_general(ref[...], feats, (((1,), (1,)), ((), ())), preferred_element_type=F32)
        for ref in weight_refs
    )
    channels = row.shape[0]
    row_ref[...] = row.astype(BF16)
    colval_ref[0:channels] = col.astype(BF16)
    colval_ref[channels:] = value.astype(BF16)


def project_kernel(half, seq_ref, first_ref, second_ref, *refs):
    weight_refs, (feats_ref, row_ref, colval_ref) = refs[:3], refs[3:]
    width = first_ref.shape[1]
    split = seq_ref.shape[1] // width
    halos = []
    for ref in (first_ref, second_ref):
        tail = ref[half * GROUP :, :].astype(F32)
        pieces = [tail[j * GROUP : (j + 1) * GROUP] for j in range(split)]
        halos.append(jnp.concatenate(pieces, axis=1))
    above, below = received(*halos)
    feats = jnp.concatenate([above, seq_ref[...].astype(F32), below], axis=0).astype(BF16)
    feats_ref[...] = feats
    project(feats, weight_refs, row_ref, colval_ref)


def advance(sum_refs, feats_ref, out_ref, root):
    total = sum_refs[0][...]
    for ref in sum_refs[1:]:
        total = total + ref[...]
    gathered = (total / root).T.astype(BF16)
    change = jnp.dot(gathered, out_ref[...], preferred_element_type=F32)
    return feats_ref[...].astype(F32) + change


def middle_kernel(root, parts, *refs):
    sum_refs, refs = refs[:parts], refs[parts:]
    feats_in, out_w, weight_refs, (feats_ref, row_ref, colval_ref) = (
        refs[0], refs[1], refs[2:5], refs[5:]
    )
    feats = advance(sum_refs, feats_in, out_w, root).astype(BF16)
    feats_ref[...] = feats
    project(feats, weight_refs, row_ref, colval_ref)


def finish_kernel(root, parts, *refs):
    sum_refs, refs = refs[:parts], refs[parts:]
    feats_in, out_w, own_ref, far_ref, seq_ref, pair_ref = refs
    rep = lax.axis_index("rep")
    rows, cols = seq_ref.shape[0], own_ref.shape[2]
    seq_ref[...] = advance(sum_refs, feats_in, out_w, root)[HALO : HALO + rows].astype(BF16)
    pair_ref[:, :, pl.ds(pl.multiple_of(rep * cols, LANES), cols)] = own_ref[...]
    pair_ref[:, :, pl.ds(pl.multiple_of((1 - rep) * cols, LANES), cols)] = far_ref[...]


def spans(low_row, high_row, stride, total):
    low = low_row * stride // LANES * LANES
    size = -(-(high_row * stride - low) // 256) * 256
    high = min(low + size, total)
    return [(at, min(at + CHUNK, high)) for at in range(low, high, CHUNK)]


def cycle_kernel(rows, cols, length, last, windows, *refs):
    (start_buf, hidden_buf, *taps, stack, mask, raw), refs = refs[-9:], refs[:-9]
    taps_first, taps_second = taps[0:2], taps[2:4]
    pair_ref, refs = refs[0], refs[1:]
    row_ref, window_refs, refs = refs[0], refs[1 : 1 + windows], refs[1 + windows :]
    first_ref, second_ref, spread_row, spread_col, collect, place_ref, *outs = refs
    channels = row_ref.shape[0]
    stride = cols + 2 * HALO
    tall = rows + 2 * HALO
    total = tall * stride
    strip = GROUP * stride
    strips = tall // GROUP
    guard = LANES
    reach = 2 * stride
    far = -(-reach // LANES) * LANES
    rep = lax.axis_index("rep")
    row_index = lax.axis_index("row")
    chunk_index = lax.axis_index("col") * 2 + rep
    margin = 2 * CYCLES * 2 - (8 if not last else 4)
    spans_in = spans(margin, rows + 2 * HALO - margin, stride, total)
    spans_mid = spans(margin + 2, rows + 2 * HALO - margin - 2, stride, total)
    spans_out = spans(margin + 4, rows + 2 * HALO - margin - 4, stride, total)

    for k in range(strips):
        row_at = row_index * rows - HALO + k * GROUP + place_ref[0:1, :]
        col_at = chunk_index * cols - HALO + place_ref[1:2, :]
        inside = (row_at >= 0) & (row_at < length) & (col_at >= 0) & (col_at < length)
        mask[:, k * strip : (k + 1) * strip] = jnp.where(inside, 1.0, 0.0)

    turn = lax.rem(row_index, windows)
    for n, ref in enumerate((first_ref, second_ref)):
        lines = []
        for ti in (1, 0, 2):
            blocks = [ref[3 * ti + tj].astype(F32) for tj in range(3)]
            lines.append(jnp.concatenate(blocks, axis=1))
        stack[n] = jnp.concatenate(lines, axis=0).astype(BF16)

    ordered = []
    for offset in range(windows):
        value = window_refs[0][...]
        for t in range(1, windows):
            piece = lax.rem(t - turn + windows, windows)
            value = jnp.where(piece == offset, window_refs[t][...], value)
        low = 0 if offset == 0 else HALO
        high = rows + (2 * HALO if offset == windows - 1 else HALO)
        ordered.append(value[:, low:high].astype(F32))
    colval = jnp.concatenate(ordered, axis=1).astype(BF16)
    colval = jnp.dot(colval, spread_col[...], preferred_element_type=F32)
    col_flat, val_flat = colval[:channels], colval[channels:]

    for buf, edge, part in (
        (start_buf, guard, ((0, total),)), (hidden_buf, guard, spans_mid),
        (taps_first[1], far, spans_in), (taps_second[1], far, spans_mid),
    ):
        low, high = part[0][0], part[-1][1]
        fill = jnp.zeros((buf.shape[0], edge), buf.dtype)
        buf[:, low : low + edge] = fill
        buf[:, high + edge : high + 2 * edge] = fill

    def start_strip(k):
        row_flat = jnp.dot(
            row_ref[:, k * GROUP : (k + 1) * GROUP], spread_row[...], preferred_element_type=F32
        )
        pair = pair_ref[:, k * strip : (k + 1) * strip].astype(F32)
        value = pair + row_flat + col_flat
        value = jnp.where(mask[:, k * strip : (k + 1) * strip] > 0, value, 0.0)
        start_buf[:, guard + k * strip : guard + (k + 1) * strip] = value.astype(BF16)

    def spread(source, taps, n, low, high):
        window = source[:, low : high + 2 * guard]
        stacked = jnp.concatenate(
            [window[:, guard + d : guard + d + high - low] for d in (-2, 0, 2)], axis=0
        )
        result = jnp.dot(stack[n], stacked, preferred_element_type=F32)
        taps[0][:, low:high] = result[:channels]
        taps[1][:, far + low : far + high] = result[channels:].astype(BF16)

    def gather(taps, low, high):
        size = high - low
        value = taps[0][:, low:high]
        for part, lane in ((0, far + low - reach), (1, far + low + reach)):
            begin = lane // LANES * LANES
            end = -(-(lane + size) // LANES) * LANES
            window = taps[1][part * channels : (part + 1) * channels, begin:end]
            value = value + window[:, lane - begin : lane - begin + size].astype(F32)
        return jnp.maximum(value, 0.0)

    def first_span(low, high):
        spread(start_buf, taps_first, 0, low, high)

    def hidden_span(low, high):
        value = jnp.where(mask[:, low:high] > 0, gather(taps_first, low, high), 0.0)
        hidden_buf[:, guard + low : guard + high] = value.astype(BF16)

    def second_span(low, high):
        spread(hidden_buf, taps_second, 1, low, high)

    def pair_span(low, high):
        value = gather(taps_second, low, high)
        pair = start_buf[:, guard + low : guard + high].astype(F32) + value
        start_buf[:, guard + low : guard + high] = pair.astype(BF16)

    def gate_strip(k):
        pair = start_buf[:, guard + k * strip : guard + (k + 1) * strip]
        wide = pair.astype(F32)
        gate = jax.nn.sigmoid(wide).astype(BF16)
        product = (gate.astype(F32) * val_flat).astype(BF16)
        outs[0][:, k * GROUP : (k + 1) * GROUP] = jnp.dot(
            product, collect[...], preferred_element_type=F32
        )
        if not last:
            outs[1][:, k * strip : (k + 1) * strip] = pair
        else:
            for i in range(GROUP):
                for t in range(cols // LANES):
                    at = i * stride + HALO + t * LANES
                    flat = raw.at[t].reshape(channels * tall, LANES)
                    flat[pl.ds(k * GROUP + i, channels, stride=tall), :] = wide[:, at : at + LANES]

    strip_spans = [(k * strip, (k + 1) * strip) for k in range(strips)]
    stages = [
        (strip_spans, lambda low, high: start_strip(low // strip), 0),
        (spans_in, first_span, guard),
        (spans_mid, hidden_span, reach),
        (spans_mid, second_span, guard),
        (spans_out, pair_span, reach),
        (strip_spans, lambda low, high: gate_strip(low // strip), 0),
    ]
    done, made = [0] * len(stages), [0] * len(stages)

    def ready(n):
        parts, _, ahead = stages[n]
        if done[n] == len(parts):
            return False
        if n == 0 or done[n - 1] == len(stages[n - 1][0]):
            return True
        return parts[done[n]][1] + ahead <= made[n - 1]

    while any(done[n] < len(stages[n][0]) for n in range(len(stages))):
        for n in reversed(range(len(stages))):
            if ready(n):
                low, high = stages[n][0][done[n]]
                stages[n][1](low, high)
                done[n], made[n] = done[n] + 1, high

    if last:
        half = channels // 2
        for t in range(cols // LANES):
            lanes = slice(t * LANES, (t + 1) * LANES)
            for out, owner in ((outs[1], rep), (outs[2], 1 - rep)):
                value = raw[t, pl.ds(owner * half, half), HALO : HALO + rows, :]
                out[:, :, lanes] = value.astype(BF16)


def run_cycle(pair, row_proj, windows, first, second, rows, cols, length, last):
    channels = row_proj.shape[0]
    stride = cols + 2 * HALO
    total = (rows + 2 * HALO) * stride
    strip = GROUP * stride
    lane = np.arange(strip)
    place = np.stack([lane // stride, lane % stride] + [0 * lane] * 6).astype(np.int32)
    spread_row = (place[0] == np.arange(GROUP)[:, None]).astype(BF16)
    spread_col = (place[1] == np.arange(stride)[:, None]).astype(BF16)
    inner = (place[1] >= HALO) & (place[1] < HALO + cols)
    collect = (spread_row.T.astype(np.float32) * inner[:, None]).astype(BF16)
    far = -(-2 * stride // LANES) * LANES
    sums = ((channels, rows + 2 * HALO), F32)
    half = ((channels // 2, rows, cols), BF16)
    outs = (sums, half, half) if last else (sums, ((channels, total), BF16))
    scratch = [
        pltpu.VMEM((channels, total + 2 * LANES), BF16),
        pltpu.VMEM((channels, total + 2 * LANES), BF16),
        pltpu.VMEM((channels, total), F32),
        pltpu.VMEM((2 * channels, total + 2 * far), BF16),
        pltpu.VMEM((channels, total), F32),
        pltpu.VMEM((2 * channels, total + 2 * far), BF16),
        pltpu.VMEM((2, 3 * channels, 3 * channels), BF16),
        pltpu.VMEM((1, total), F32),
        pltpu.VMEM((cols // LANES, channels, rows + 2 * HALO, LANES), F32),
    ]
    kernel = functools.partial(cycle_kernel, rows, cols, length, last, len(windows))
    return call(
        kernel, outs, scratch, pair, row_proj, *windows, first, second,
        spread_row, spread_col, collect, place,
        limit=10 + total // 512, flops=40 * channels * channels * total,
    )


def on_device(seq_in, pair_in, w_row, w_col, w_value, conv_first, conv_second, w_out):
    rows, features = seq_in.shape
    channels = w_row.shape[1]
    half = channels // 2
    cols = pair_in.shape[2] // 2
    stride = cols + 2 * HALO
    tall = rows + 2 * HALO
    row_size, col_size = lax.axis_size("row"), lax.axis_size("col")
    chunks = 2 * col_size
    length = rows * row_size
    windows = cols // rows
    root = np.float32(np.sqrt(np.float32(length)))
    every = ("row", "col", "rep")
    weights = (w_row.T, w_col.T, w_value.T)
    swap = [(0, 1), (1, 0)]

    def pairs(begin, size):
        moves = []
        for i in range(begin, size - 1, 2):
            moves += [(i, i + 1), (i + 1, i)]
        return moves

    across = pairs(1, chunks)
    if chunks == 4:
        across += [(0, 3), (3, 0)]

    def to_columns(value):
        results = []
        for t in range(windows):
            moves = []
            for r in range(row_size):
                for q in range(chunks):
                    source = windows * q + (t - r) % windows
                    replica = (r // windows) ^ (chunks // 2)
                    moves.append((source * chunks + replica, r * chunks + q))
            results.append(lax.ppermute(value, every, moves))
        return results

    def all_parts(value):
        if chunks & (chunks - 1):
            partners = [[(i, (i + b) % chunks) for i in range(chunks)] for b in range(1, chunks)]
        else:
            partners = [[(i, i ^ b) for i in range(chunks)] for b in range(1, chunks)]
        return [value] + [lax.ppermute(value, ("col", "rep"), moves) for moves in partners]

    far_pair = lax.ppermute(pair_in, "rep", swap)
    width = pair_in.shape[2]
    message = ((-(-GROUP * (half + features // width) // 16) * 16, width), BF16)
    first_out, second_out = call(
        strips_kernel, [message, message],
        [
            pltpu.VMEM((2, half, 2 * GROUP, width), BF16),
            pltpu.VMEM((2, 2 * GROUP, features), BF16),
            pltpu.SemaphoreType.DMA((4,)),
        ],
        pair_in, seq_in, space=pl.ANY, limit=56,
    )
    second = lax.ppermute(second_out, "row", pairs(1, row_size))
    first = lax.ppermute(first_out, "row", pairs(0, row_size))
    wide = [((tall, features), BF16), ((channels, tall), BF16), ((2 * channels, tall), BF16)]
    feats, row_proj, colval = call(
        functools.partial(project_kernel, half), wide, [],
        seq_in, second, first, *weights
    )
    col_windows = to_columns(colval)
    second_far = lax.ppermute(second, "rep", swap)
    first_far = lax.ppermute(first, "rep", swap)
    pieces = (pair_in, second, first, far_pair, second_far, first_far)
    (edge,) = call(edges_kernel, [((channels * GROUP, LANES), BF16)], [], *pieces)
    pieces += (lax.ppermute(edge, ("col", "rep"), across),)
    (pair,) = call(
        functools.partial(assemble_kernel, cols), [((channels, tall * stride), BF16)],
        [pltpu.VMEM((cols // LANES + 1, channels, tall, LANES), F32)],
        *pieces, limit=24, flops=1 << 30,
    )

    sums, pair = run_cycle(
        pair, row_proj, col_windows, conv_first, conv_second, rows, cols, length, False
    )
    parts = all_parts(sums)
    feats, row_proj, colval = call(
        functools.partial(middle_kernel, root, chunks), wide, [],
        *parts, feats, w_out, *weights,
    )
    col_windows = to_columns(colval)
    sums, own, send = run_cycle(
        pair, row_proj, col_windows, conv_first, conv_second, rows, cols, length, True
    )
    parts = all_parts(sums)
    far_half = lax.ppermute(send, "rep", swap)
    return call(
        functools.partial(finish_kernel, root, chunks),
        [(seq_in.shape, BF16), (pair_in.shape, BF16)], [],
        *parts, feats, w_out, own, far_half,
    )


def solution(mesh):
    in_specs = (
        P(("grp", "row"), None),
        P(("grp", "rep"), "row", "col"),
        P(),
        P(),
        P(),
        P(),
        P(),
        P(),
    )
    out_specs = (P(("grp", "row"), None), P(("grp", "rep"), "row", "col"))
    return jax.shard_map(
        on_device, mesh=mesh, in_specs=in_specs, out_specs=out_specs, check_vma=False
    )
```

```python
import functools

import jax
import jax.numpy as jnp
import numpy as np
from jax import lax
from jax.experimental import pallas as pl
from jax.experimental.pallas import tpu as pltpu
from jax.sharding import PartitionSpec as P

CYCLES = 2
HALO = 8
GROUP = 8
LANES = 128
CHUNK = 3840
F32, BF16 = jnp.float32, jnp.bfloat16
def call(kernel, outs, scratch, *args, space=pltpu.VMEM, limit=16, flops=1 << 20):
    moved = sum(int(np.prod(x.shape)) * x.dtype.itemsize for x in args)
    return pl.pallas_call(
        kernel,
        out_shape=tuple(jax.ShapeDtypeStruct(shape, dtype) for shape, dtype in outs),
        in_specs=[pl.BlockSpec(memory_space=space)] * len(args),
        out_specs=(pl.BlockSpec(memory_space=pltpu.VMEM),) * len(outs),
        scratch_shapes=scratch,
        compiler_params=pltpu.CompilerParams(vmem_limit_bytes=limit << 20),
        cost_estimate=pl.CostEstimate(flops=flops, bytes_accessed=moved, transcendentals=0),
    )(*args)


def lane_ids(shape):
    return lax.broadcasted_iota(jnp.int32, shape, len(shape) - 1)


def is_even():
    return lax.rem(lax.axis_index("row"), 2) == 0


def strips_kernel(tile_ref, seq_ref, first_ref, second_ref, tile_ends, seq_ends, sems):
    half, rows, width = tile_ref.shape
    even = is_even()

    def message(pair, seq):
        pieces = [pair.reshape(half * GROUP, width)]
        pieces += [seq[:, at : at + width] for at in range(0, seq.shape[1], width)]
        rest = first_ref.shape[0] - GROUP * (half + len(pieces) - 1)
        if rest:
            pieces.append(jnp.zeros((rest, width), F32))
        return jnp.concatenate(pieces, axis=0)

    moves = []
    for n, at in enumerate((0, rows - 2 * GROUP)):
        lines = pl.ds(at, 2 * GROUP)
        moves += [
            pltpu.make_async_copy(tile_ref.at[:, lines, :], tile_ends.at[n], sems.at[2 * n]),
            pltpu.make_async_copy(seq_ref.at[lines, :], seq_ends.at[n], sems.at[2 * n + 1]),
        ]
    for move in moves:
        move.start()
    for move in moves:
        move.wait()
    top = message(
        tile_ends[0].astype(F32)[:, :GROUP], seq_ends[0].astype(F32)[:GROUP]
    )
    bottom = message(
        tile_ends[1].astype(F32)[:, GROUP:], seq_ends[1].astype(F32)[GROUP:]
    )
    first_ref[...] = jnp.where(even, bottom, top).astype(BF16)
    second_ref[...] = jnp.where(even, top, bottom).astype(BF16)


def received(first, second):
    even = is_even()
    return jnp.where(even, second, first), jnp.where(even, first, second)


def tile_pieces(tile_ref, first_ref, second_ref, at):
    half, rows, _ = tile_ref.shape
    middle = tile_ref[:, :, pl.ds(at, LANES)].astype(F32)
    above, below = received(
        *(
            ref[0 : half * GROUP, pl.ds(at, LANES)].astype(F32).reshape(half, GROUP, LANES)
            for ref in (first_ref, second_ref)
        )
    )
    middle = [middle[:, m * GROUP : (m + 1) * GROUP] for m in range(rows // GROUP)]
    return [above, *middle, below]


def edges_kernel(*refs):
    parts, out_ref = (refs[0:3], refs[3:6]), refs[6]
    rep = lax.axis_index("rep")
    half, _, width = refs[0].shape
    lane = lane_ids((half, GROUP, LANES))
    at = pl.multiple_of(jnp.where(rep == 0, 0, width - LANES), LANES)
    for part in range(2):
        packed = jnp.zeros((half, GROUP, LANES), F32)
        turn = jnp.where(rep == 0, 0, HALO)
        for g, piece in enumerate(tile_pieces(*parts[part], at)):
            moved = pltpu.roll(piece, turn + HALO * g, 2)
            packed = jnp.where((lane >= HALO * g) & (lane < HALO * (g + 1)), moved, packed)
        base = (rep if part == 0 else 1 - rep) * half * GROUP
        out_ref[pl.ds(pl.multiple_of(base, 2 * GROUP), half * GROUP), :] = packed.reshape(
            half * GROUP, LANES
        ).astype(BF16)


def unpack(parts, edge_ref, raw, cols):
    rep = lax.axis_index("rep")
    across = cols // LANES
    half = parts[0][0].shape[0]
    inner_at = pl.multiple_of(jnp.where(rep == 0, cols, cols - LANES), LANES)
    is_outer = (lane_ids((half, GROUP, LANES)) < HALO) == (rep == 0)
    for part in range(2):
        owner = pl.ds((rep if part == 0 else 1 - rep) * half, half)
        for t in range(across):
            at = pl.multiple_of(rep * cols + t * LANES, LANES)
            for g, piece in enumerate(tile_pieces(*parts[part], at)):
                raw[t, owner, g * GROUP : (g + 1) * GROUP, :] = piece
        base = (rep if part == 0 else 1 - rep) * half * GROUP
        edge = edge_ref[pl.ds(pl.multiple_of(base, 2 * GROUP), half * GROUP), :].astype(F32)
        edge = edge.reshape(half, GROUP, LANES)
        outer = pltpu.roll(edge, jnp.where(rep == 0, 0, HALO), 2)
        for g, piece in enumerate(tile_pieces(*parts[part], inner_at)):
            raw[across, owner, g * GROUP : (g + 1) * GROUP, :] = jnp.where(
                is_outer,
                pltpu.roll(outer, (-HALO * g) % LANES, 2),
                pltpu.roll(piece, HALO, 2),
            )


def assemble_kernel(cols, *refs):
    parts, edge_ref, out_ref, raw = (refs[0:3], refs[3:6]), refs[6], refs[7], refs[8]
    unpack(parts, edge_ref, raw, cols)
    strip = GROUP * (cols + 2 * HALO)
    for k in range(raw.shape[2] // GROUP):
        out_ref[:, k * strip : (k + 1) * strip] = raw_strip(raw, k).astype(BF16)


def raw_strip(raw, place):
    across, channels, rows, _ = raw.shape
    pieces = []
    for i in range(place * GROUP, (place + 1) * GROUP):
        tiles = [
            raw.at[t].reshape(channels * rows, LANES)[pl.ds(i, channels, stride=rows), :]
            for t in range(across)
        ]
        side = tiles.pop()
        pieces += [side[:, :HALO], *tiles, side[:, HALO : 2 * HALO]]
    return jnp.concatenate(pieces, axis=1)


def project(feats, weight_refs, row_ref, colval_ref):
    row, col, value = (
        lax.dot_general(ref[...], feats, (((1,), (1,)), ((), ())), preferred_element_type=F32)
        for ref in weight_refs
    )
    channels = row.shape[0]
    row_ref[...] = row.astype(BF16)
    colval_ref[0:channels] = col.astype(BF16)
    colval_ref[channels:] = value.astype(BF16)


def project_kernel(half, seq_ref, first_ref, second_ref, *refs):
    weight_refs, (feats_ref, row_ref, colval_ref) = refs[:3], refs[3:]
    width = first_ref.shape[1]
    split = seq_ref.shape[1] // width
    halos = []
    for ref in (first_ref, second_ref):
        tail = ref[half * GROUP :, :].astype(F32)
        pieces = [tail[j * GROUP : (j + 1) * GROUP] for j in range(split)]
        halos.append(jnp.concatenate(pieces, axis=1))
    above, below = received(*halos)
    feats = jnp.concatenate([above, seq_ref[...].astype(F32), below], axis=0).astype(BF16)
    feats_ref[...] = feats
    project(feats, weight_refs, row_ref, colval_ref)


def advance(sum_refs, feats_ref, out_ref, root):
    total = sum_refs[0][...]
    for ref in sum_refs[1:]:
        total = total + ref[...]
    gathered = (total / root).T.astype(BF16)
    change = jnp.dot(gathered, out_ref[...], preferred_element_type=F32)
    return feats_ref[...].astype(F32) + change


def middle_kernel(root, parts, *refs):
    sum_refs, refs = refs[:parts], refs[parts:]
    feats_in, out_w, weight_refs, (feats_ref, row_ref, colval_ref) = (
        refs[0], refs[1], refs[2:5], refs[5:]
    )
    feats = advance(sum_refs, feats_in, out_w, root).astype(BF16)
    feats_ref[...] = feats
    project(feats, weight_refs, row_ref, colval_ref)


def finish_kernel(root, parts, *refs):
    sum_refs, refs = refs[:parts], refs[parts:]
    feats_in, out_w, own_ref, far_ref, seq_ref, pair_ref = refs
    rep = lax.axis_index("rep")
    rows, cols = seq_ref.shape[0], own_ref.shape[2]
    seq_ref[...] = advance(sum_refs, feats_in, out_w, root)[HALO : HALO + rows].astype(BF16)
    pair_ref[:, :, pl.ds(pl.multiple_of(rep * cols, LANES), cols)] = own_ref[...]
    pair_ref[:, :, pl.ds(pl.multiple_of((1 - rep) * cols, LANES), cols)] = far_ref[...]


def spans(low_row, high_row, stride, total):
    low = low_row * stride // LANES * LANES
    size = -(-(high_row * stride - low) // 256) * 256
    high = min(low + size, total)
    return [(at, min(at + CHUNK, high)) for at in range(low, high, CHUNK)]


def cycle_kernel(rows, cols, length, last, windows, *refs):
    (start_buf, hidden_buf, *taps, stack, mask, raw), refs = refs[-9:], refs[:-9]
    taps_first, taps_second = taps[0:2], taps[2:4]
    pair_ref, refs = refs[0], refs[1:]
    row_ref, window_refs, refs = refs[0], refs[1 : 1 + windows], refs[1 + windows :]
    first_ref, second_ref, spread_row, spread_col, collect, place_ref, *outs = refs
    channels = row_ref.shape[0]
    stride = cols + 2 * HALO
    tall = rows + 2 * HALO
    total = tall * stride
    strip = GROUP * stride
    strips = tall // GROUP
    guard = LANES
    reach = 2 * stride
    far = -(-reach // LANES) * LANES
    rep = lax.axis_index("rep")
    row_index = lax.axis_index("row")
    chunk_index = lax.axis_index("col") * 2 + rep
    margin = 2 * CYCLES * 2 - (8 if not last else 4)
    spans_in = spans(margin, rows + 2 * HALO - margin, stride, total)
    spans_mid = spans(margin + 2, rows + 2 * HALO - margin - 2, stride, total)
    spans_out = spans(margin + 4, rows + 2 * HALO - margin - 4, stride, total)

    for k in range(strips):
        row_at = row_index * rows - HALO + k * GROUP + place_ref[0:1, :]
        col_at = chunk_index * cols - HALO + place_ref[1:2, :]
        inside = (row_at >= 0) & (row_at < length) & (col_at >= 0) & (col_at < length)
        mask[:, k * strip : (k + 1) * strip] = jnp.where(inside, 1.0, 0.0)

    turn = lax.rem(row_index, windows)
    for n, ref in enumerate((first_ref, second_ref)):
        lines = []
        for ti in (1, 0, 2):
            blocks = [ref[3 * ti + tj].astype(F32) for tj in range(3)]
            lines.append(jnp.concatenate(blocks, axis=1))
        stack[n] = jnp.concatenate(lines, axis=0).astype(BF16)

    ordered = []
    for offset in range(windows):
        value = window_refs[0][...]
        for t in range(1, windows):
            piece = lax.rem(t - turn + windows, windows)
            value = jnp.where(piece == offset, window_refs[t][...], value)
        low = 0 if offset == 0 else HALO
        high = rows + (2 * HALO if offset == windows - 1 else HALO)
        ordered.append(value[:, low:high].astype(F32))
    colval = jnp.concatenate(ordered, axis=1).astype(BF16)
    colval = jnp.dot(colval, spread_col[...], preferred_element_type=F32)
    col_flat, val_flat = colval[:channels], colval[channels:]

    for buf, edge, part in (
        (start_buf, guard, ((0, total),)), (hidden_buf, guard, spans_mid),
        (taps_first[1], far, spans_in), (taps_second[1], far, spans_mid),
    ):
        low, high = part[0][0], part[-1][1]
        fill = jnp.zeros((buf.shape[0], edge), buf.dtype)
        buf[:, low : low + edge] = fill
        buf[:, high + edge : high + 2 * edge] = fill

    def start_strip(k):
        row_flat = jnp.dot(
            row_ref[:, k * GROUP : (k + 1) * GROUP], spread_row[...], preferred_element_type=F32
        )
        pair = pair_ref[:, k * strip : (k + 1) * strip].astype(F32)
        value = pair + row_flat + col_flat
        value = jnp.where(mask[:, k * strip : (k + 1) * strip] > 0, value, 0.0)
        start_buf[:, guard + k * strip : guard + (k + 1) * strip] = value.astype(BF16)

    def spread(source, taps, n, low, high):
        window = source[:, low : high + 2 * guard]
        stacked = jnp.concatenate(
            [window[:, guard + d : guard + d + high - low] for d in (-2, 0, 2)], axis=0
        )
        result = jnp.dot(stack[n], stacked, preferred_element_type=F32)
        taps[0][:, low:high] = result[:channels]
        taps[1][:, far + low : far + high] = result[channels:].astype(BF16)

    def gather(taps, low, high):
        size = high - low
        value = taps[0][:, low:high]
        for part, lane in ((0, far + low - reach), (1, far + low + reach)):
            begin = lane // LANES * LANES
            end = -(-(lane + size) // LANES) * LANES
            window = taps[1][part * channels : (part + 1) * channels, begin:end]
            value = value + window[:, lane - begin : lane - begin + size].astype(F32)
        return jnp.maximum(value, 0.0)

    def first_span(low, high):
        spread(start_buf, taps_first, 0, low, high)

    def hidden_span(low, high):
        value = jnp.where(mask[:, low:high] > 0, gather(taps_first, low, high), 0.0)
        hidden_buf[:, guard + low : guard + high] = value.astype(BF16)

    def second_span(low, high):
        spread(hidden_buf, taps_second, 1, low, high)

    def pair_span(low, high):
        value = gather(taps_second, low, high)
        pair = start_buf[:, guard + low : guard + high].astype(F32) + value
        start_buf[:, guard + low : guard + high] = pair.astype(BF16)

    def gate_strip(k):
        pair = start_buf[:, guard + k * strip : guard + (k + 1) * strip]
        wide = pair.astype(F32)
        gate = jax.nn.sigmoid(wide).astype(BF16)
        product = (gate.astype(F32) * val_flat).astype(BF16)
        outs[0][:, k * GROUP : (k + 1) * GROUP] = jnp.dot(
            product, collect[...], preferred_element_type=F32
        )
        if not last:
            outs[1][:, k * strip : (k + 1) * strip] = pair
        else:
            for i in range(GROUP):
                for t in range(cols // LANES):
                    at = i * stride + HALO + t * LANES
                    flat = raw.at[t].reshape(channels * tall, LANES)
                    flat[pl.ds(k * GROUP + i, channels, stride=tall), :] = wide[:, at : at + LANES]

    strip_spans = [(k * strip, (k + 1) * strip) for k in range(strips)]
    stages = [
        (strip_spans, lambda low, high: start_strip(low // strip), 0),
        (spans_in, first_span, guard),
        (spans_mid, hidden_span, reach),
        (spans_mid, second_span, guard),
        (spans_out, pair_span, reach),
        (strip_spans, lambda low, high: gate_strip(low // strip), 0),
    ]
    done, made = [0] * len(stages), [0] * len(stages)

    def ready(n):
        parts, _, ahead = stages[n]
        if done[n] == len(parts):
            return False
        if n == 0 or done[n - 1] == len(stages[n - 1][0]):
            return True
        return parts[done[n]][1] + ahead <= made[n - 1]

    while any(done[n] < len(stages[n][0]) for n in range(len(stages))):
        for n in reversed(range(len(stages))):
            if ready(n):
                low, high = stages[n][0][done[n]]
                stages[n][1](low, high)
                done[n], made[n] = done[n] + 1, high

    if last:
        half = channels // 2
        for t in range(cols // LANES):
            lanes = slice(t * LANES, (t + 1) * LANES)
            for out, owner in ((outs[1], rep), (outs[2], 1 - rep)):
                value = raw[t, pl.ds(owner * half, half), HALO : HALO + rows, :]
                out[:, :, lanes] = value.astype(BF16)


def run_cycle(pair, row_proj, windows, first, second, rows, cols, length, last):
    channels = row_proj.shape[0]
    stride = cols + 2 * HALO
    total = (rows + 2 * HALO) * stride
    strip = GROUP * stride
    lane = np.arange(strip)
    place = np.stack([lane // stride, lane % stride] + [0 * lane] * 6).astype(np.int32)
    spread_row = (place[0] == np.arange(GROUP)[:, None]).astype(BF16)
    spread_col = (place[1] == np.arange(stride)[:, None]).astype(BF16)
    inner = (place[1] >= HALO) & (place[1] < HALO + cols)
    collect = (spread_row.T.astype(np.float32) * inner[:, None]).astype(BF16)
    far = -(-2 * stride // LANES) * LANES
    sums = ((channels, rows + 2 * HALO), F32)
    half = ((channels // 2, rows, cols), BF16)
    outs = (sums, half, half) if last else (sums, ((channels, total), BF16))
    scratch = [
        pltpu.VMEM((channels, total + 2 * LANES), BF16),
        pltpu.VMEM((channels, total + 2 * LANES), BF16),
        pltpu.VMEM((channels, total), F32),
        pltpu.VMEM((2 * channels, total + 2 * far), BF16),
        pltpu.VMEM((channels, total), F32),
        pltpu.VMEM((2 * channels, total + 2 * far), BF16),
        pltpu.VMEM((2, 3 * channels, 3 * channels), BF16),
        pltpu.VMEM((1, total), F32),
        pltpu.VMEM((cols // LANES, channels, rows + 2 * HALO, LANES), F32),
    ]
    kernel = functools.partial(cycle_kernel, rows, cols, length, last, len(windows))
    return call(
        kernel, outs, scratch, pair, row_proj, *windows, first, second,
        spread_row, spread_col, collect, place,
        limit=10 + total // 512, flops=40 * channels * channels * total,
    )


def on_device(seq_in, pair_in, w_row, w_col, w_value, conv_first, conv_second, w_out):
    rows, features = seq_in.shape
    channels = w_row.shape[1]
    half = channels // 2
    cols = pair_in.shape[2] // 2
    stride = cols + 2 * HALO
    tall = rows + 2 * HALO
    row_size, col_size = lax.axis_size("row"), lax.axis_size("col")
    chunks = 2 * col_size
    length = rows * row_size
    windows = cols // rows
    root = np.float32(np.sqrt(np.float32(length)))
    every = ("row", "col", "rep")
    weights = (w_row.T, w_col.T, w_value.T)
    swap = [(0, 1), (1, 0)]

    def pairs(begin, size):
        moves = []
        for i in range(begin, size - 1, 2):
            moves += [(i, i + 1), (i + 1, i)]
        return moves

    across = pairs(1, chunks)
    if chunks == 4:
        across += [(0, 3), (3, 0)]

    def to_columns(value):
        results = []
        for t in range(windows):
            moves = []
            for r in range(row_size):
                for q in range(chunks):
                    source = windows * q + (t - r) % windows
                    replica = (r // windows) ^ (chunks // 2)
                    moves.append((source * chunks + replica, r * chunks + q))
            results.append(lax.ppermute(value, every, moves))
        return results

    def all_parts(value):
        if chunks & (chunks - 1):
            partners = [[(i, (i + b) % chunks) for i in range(chunks)] for b in range(1, chunks)]
        else:
            partners = [[(i, i ^ b) for i in range(chunks)] for b in range(1, chunks)]
        return [value] + [lax.ppermute(value, ("col", "rep"), moves) for moves in partners]

    far_pair = lax.ppermute(pair_in, "rep", swap)
    width = pair_in.shape[2]
    message = ((-(-GROUP * (half + features // width) // 16) * 16, width), BF16)
    first_out, second_out = call(
        strips_kernel, [message, message],
        [
            pltpu.VMEM((2, half, 2 * GROUP, width), BF16),
            pltpu.VMEM((2, 2 * GROUP, features), BF16),
            pltpu.SemaphoreType.DMA((4,)),
        ],
        pair_in, seq_in, space=pl.ANY, limit=56,
    )
    first = lax.ppermute(first_out, "row", pairs(0, row_size))
    second = lax.ppermute(second_out, "row", pairs(1, row_size))
    wide = [((tall, features), BF16), ((channels, tall), BF16), ((2 * channels, tall), BF16)]
    feats, row_proj, colval = call(
        functools.partial(project_kernel, half), wide, [],
        seq_in, first, second, *weights
    )
    col_windows = to_columns(colval)
    first_far = lax.ppermute(first, "rep", swap)
    second_far = lax.ppermute(second, "rep", swap)
    pieces = (pair_in, first, second, far_pair, first_far, second_far)
    (edge,) = call(edges_kernel, [((channels * GROUP, LANES), BF16)], [], *pieces)
    pieces += (lax.ppermute(edge, ("col", "rep"), across),)
    (pair,) = call(
        functools.partial(assemble_kernel, cols), [((channels, tall * stride), BF16)],
        [pltpu.VMEM((cols // LANES + 1, channels, tall, LANES), F32)],
        *pieces, limit=24, flops=1 << 30,
    )

    sums, pair = run_cycle(
        pair, row_proj, col_windows, conv_first, conv_second, rows, cols, length, False
    )
    parts = all_parts(sums)
    feats, row_proj, colval = call(
        functools.partial(middle_kernel, root, chunks), wide, [],
        *parts, feats, w_out, *weights,
    )
    col_windows = to_columns(colval)
    sums, own, send = run_cycle(
        pair, row_proj, col_windows, conv_first, conv_second, rows, cols, length, True
    )
    parts = all_parts(sums)
    far_half = lax.ppermute(send, "rep", swap)
    return call(
        functools.partial(finish_kernel, root, chunks),
        [(seq_in.shape, BF16), (pair_in.shape, BF16)], [],
        *parts, feats, w_out, own, far_half,
    )


def solution(mesh):
    in_specs = (
        P(("grp", "row"), None),
        P(("grp", "rep"), "row", "col"),
        P(),
        P(),
        P(),
        P(),
        P(),
        P(),
    )
    out_specs = (P(("grp", "row"), None), P(("grp", "rep"), "row", "col"))
    return jax.shard_map(
        on_device, mesh=mesh, in_specs=in_specs, out_specs=out_specs, check_vma=False
    )
```

```python
import functools

import jax
import jax.numpy as jnp
import numpy as np
from jax import lax
from jax.experimental import pallas as pl
from jax.experimental.pallas import tpu as pltpu
from jax.sharding import PartitionSpec as P

CYCLES = 2
HALO = 8
GROUP = 8
LANES = 128
CHUNK = 3840
F32, BF16 = jnp.float32, jnp.bfloat16
def call(kernel, outs, scratch, *args, space=pltpu.VMEM, limit=16, flops=1 << 20):
    moved = sum(int(np.prod(x.shape)) * x.dtype.itemsize for x in args)
    return pl.pallas_call(
        kernel,
        out_shape=tuple(jax.ShapeDtypeStruct(shape, dtype) for shape, dtype in outs),
        in_specs=[pl.BlockSpec(memory_space=space)] * len(args),
        out_specs=(pl.BlockSpec(memory_space=pltpu.VMEM),) * len(outs),
        scratch_shapes=scratch,
        compiler_params=pltpu.CompilerParams(vmem_limit_bytes=limit << 20),
        cost_estimate=pl.CostEstimate(flops=flops, bytes_accessed=moved, transcendentals=0),
    )(*args)


def lane_ids(shape):
    return lax.broadcasted_iota(jnp.int32, shape, len(shape) - 1)


def is_even():
    return lax.rem(lax.axis_index("row"), 2) == 0


def strips_kernel(tile_ref, seq_ref, first_ref, second_ref, tile_ends, seq_ends, sems):
    half, rows, width = tile_ref.shape
    even = is_even()

    def message(pair, seq):
        pieces = [pair.reshape(half * GROUP, width)]
        pieces += [seq[:, at : at + width] for at in range(0, seq.shape[1], width)]
        rest = first_ref.shape[0] - GROUP * (half + len(pieces) - 1)
        if rest:
            pieces.append(jnp.zeros((rest, width), F32))
        return jnp.concatenate(pieces, axis=0)

    moves = []
    for n, at in enumerate((0, rows - 2 * GROUP)):
        lines = pl.ds(at, 2 * GROUP)
        moves += [
            pltpu.make_async_copy(tile_ref.at[:, lines, :], tile_ends.at[n], sems.at[2 * n]),
            pltpu.make_async_copy(seq_ref.at[lines, :], seq_ends.at[n], sems.at[2 * n + 1]),
        ]
    for move in moves:
        move.start()
    for move in moves:
        move.wait()
    top = message(
        tile_ends[0].astype(F32)[:, :GROUP], seq_ends[0].astype(F32)[:GROUP]
    )
    bottom = message(
        tile_ends[1].astype(F32)[:, GROUP:], seq_ends[1].astype(F32)[GROUP:]
    )
    first_ref[...] = jnp.where(even, bottom, top).astype(BF16)
    second_ref[...] = jnp.where(even, top, bottom).astype(BF16)


def received(first, second):
    even = is_even()
    return jnp.where(even, second, first), jnp.where(even, first, second)


def tile_pieces(tile_ref, first_ref, second_ref, at):
    half, rows, _ = tile_ref.shape
    middle = tile_ref[:, :, pl.ds(at, LANES)].astype(F32)
    above, below = received(
        *(
            ref[0 : half * GROUP, pl.ds(at, LANES)].astype(F32).reshape(half, GROUP, LANES)
            for ref in (first_ref, second_ref)
        )
    )
    middle = [middle[:, m * GROUP : (m + 1) * GROUP] for m in range(rows // GROUP)]
    return [above, *middle, below]


def edges_kernel(*refs):
    parts, out_ref = (refs[0:3], refs[3:6]), refs[6]
    rep = lax.axis_index("rep")
    half, _, width = refs[0].shape
    lane = lane_ids((half, GROUP, LANES))
    at = pl.multiple_of(jnp.where(rep == 0, 0, width - LANES), LANES)
    for part in range(2):
        packed = jnp.zeros((half, GROUP, LANES), F32)
        turn = jnp.where(rep == 0, 0, HALO)
        for g, piece in enumerate(tile_pieces(*parts[part], at)):
            moved = pltpu.roll(piece, turn + HALO * g, 2)
            packed = jnp.where((lane >= HALO * g) & (lane < HALO * (g + 1)), moved, packed)
        base = (rep if part == 0 else 1 - rep) * half * GROUP
        out_ref[pl.ds(pl.multiple_of(base, 2 * GROUP), half * GROUP), :] = packed.reshape(
            half * GROUP, LANES
        ).astype(BF16)


def unpack(parts, edge_ref, raw, cols):
    rep = lax.axis_index("rep")
    across = cols // LANES
    half = parts[0][0].shape[0]
    inner_at = pl.multiple_of(jnp.where(rep == 0, cols, cols - LANES), LANES)
    is_outer = (lane_ids((half, GROUP, LANES)) < HALO) == (rep == 0)
    for part in range(2):
        owner = pl.ds((rep if part == 0 else 1 - rep) * half, half)
        for t in range(across):
            at = pl.multiple_of(rep * cols + t * LANES, LANES)
            for g, piece in enumerate(tile_pieces(*parts[part], at)):
                raw[t, owner, g * GROUP : (g + 1) * GROUP, :] = piece
        base = (rep if part == 0 else 1 - rep) * half * GROUP
        edge = edge_ref[pl.ds(pl.multiple_of(base, 2 * GROUP), half * GROUP), :].astype(F32)
        edge = edge.reshape(half, GROUP, LANES)
        outer = pltpu.roll(edge, jnp.where(rep == 0, 0, HALO), 2)
        for g, piece in enumerate(tile_pieces(*parts[part], inner_at)):
            raw[across, owner, g * GROUP : (g + 1) * GROUP, :] = jnp.where(
                is_outer,
                pltpu.roll(outer, (-HALO * g) % LANES, 2),
                pltpu.roll(piece, HALO, 2),
            )


def assemble_kernel(cols, *refs):
    parts, edge_ref, out_ref, raw = (refs[0:3], refs[3:6]), refs[6], refs[7], refs[8]
    unpack(parts, edge_ref, raw, cols)
    strip = GROUP * (cols + 2 * HALO)
    for k in range(raw.shape[2] // GROUP):
        out_ref[:, k * strip : (k + 1) * strip] = raw_strip(raw, k).astype(BF16)


def raw_strip(raw, place):
    across, channels, rows, _ = raw.shape
    pieces = []
    for i in range(place * GROUP, (place + 1) * GROUP):
        tiles = [
            raw.at[t].reshape(channels * rows, LANES)[pl.ds(i, channels, stride=rows), :]
            for t in range(across)
        ]
        side = tiles.pop()
        pieces += [side[:, :HALO], *tiles, side[:, HALO : 2 * HALO]]
    return jnp.concatenate(pieces, axis=1)


def project(feats, weight_refs, row_ref, colval_ref):
    row, col, value = (
        lax.dot_general(ref[...], feats, (((1,), (1,)), ((), ())), preferred_element_type=F32)
        for ref in weight_refs
    )
    channels = row.shape[0]
    row_ref[...] = row.astype(BF16)
    colval_ref[0:channels] = col.astype(BF16)
    colval_ref[channels:] = value.astype(BF16)


def project_kernel(half, seq_ref, first_ref, second_ref, *refs):
    weight_refs, (feats_ref, row_ref, colval_ref) = refs[:3], refs[3:]
    width = first_ref.shape[1]
    split = seq_ref.shape[1] // width
    halos = []
    for ref in (first_ref, second_ref):
        tail = ref[half * GROUP :, :].astype(F32)
        pieces = [tail[j * GROUP : (j + 1) * GROUP] for j in range(split)]
        halos.append(jnp.concatenate(pieces, axis=1))
    above, below = received(*halos)
    feats = jnp.concatenate([above, seq_ref[...].astype(F32), below], axis=0).astype(BF16)
    feats_ref[...] = feats
    project(feats, weight_refs, row_ref, colval_ref)


def advance(sum_refs, feats_ref, out_ref, root):
    total = sum_refs[0][...]
    for ref in sum_refs[1:]:
        total = total + ref[...]
    gathered = (total / root).T.astype(BF16)
    change = jnp.dot(gathered, out_ref[...], preferred_element_type=F32)
    return feats_ref[...].astype(F32) + change


def middle_kernel(root, parts, *refs):
    sum_refs, refs = refs[:parts], refs[parts:]
    feats_in, out_w, weight_refs, (feats_ref, row_ref, colval_ref) = (
        refs[0], refs[1], refs[2:5], refs[5:]
    )
    feats = advance(sum_refs, feats_in, out_w, root).astype(BF16)
    feats_ref[...] = feats
    project(feats, weight_refs, row_ref, colval_ref)


def finish_kernel(root, parts, *refs):
    sum_refs, refs = refs[:parts], refs[parts:]
    feats_in, out_w, own_ref, far_ref, seq_ref, pair_ref = refs
    rep = lax.axis_index("rep")
    rows, cols = seq_ref.shape[0], own_ref.shape[2]
    seq_ref[...] = advance(sum_refs, feats_in, out_w, root)[HALO : HALO + rows].astype(BF16)
    pair_ref[:, :, pl.ds(pl.multiple_of(rep * cols, LANES), cols)] = own_ref[...]
    pair_ref[:, :, pl.ds(pl.multiple_of((1 - rep) * cols, LANES), cols)] = far_ref[...]


def spans(low_row, high_row, stride, total):
    low = low_row * stride // LANES * LANES
    size = -(-(high_row * stride - low) // 256) * 256
    high = min(low + size, total)
    return [(at, min(at + CHUNK, high)) for at in range(low, high, CHUNK)]


def cycle_kernel(rows, cols, length, last, windows, *refs):
    (start_buf, hidden_buf, *taps, stack, mask, raw), refs = refs[-9:], refs[:-9]
    taps_first, taps_second = taps[0:2], taps[2:4]
    pair_ref, refs = refs[0], refs[1:]
    row_ref, window_refs, refs = refs[0], refs[1 : 1 + windows], refs[1 + windows :]
    first_ref, second_ref, spread_row, spread_col, collect, place_ref, *outs = refs
    channels = row_ref.shape[0]
    stride = cols + 2 * HALO
    tall = rows + 2 * HALO
    total = tall * stride
    strip = GROUP * stride
    strips = tall // GROUP
    guard = LANES
    reach = 2 * stride
    far = -(-reach // LANES) * LANES
    rep = lax.axis_index("rep")
    row_index = lax.axis_index("row")
    chunk_index = lax.axis_index("col") * 2 + rep
    margin = 2 * CYCLES * 2 - (8 if not last else 4)
    spans_in = spans(margin, rows + 2 * HALO - margin, stride, total)
    spans_mid = spans(margin + 2, rows + 2 * HALO - margin - 2, stride, total)
    spans_out = spans(margin + 4, rows + 2 * HALO - margin - 4, stride, total)

    for k in range(strips):
        row_at = row_index * rows - HALO + k * GROUP + place_ref[0:1, :]
        col_at = chunk_index * cols - HALO + place_ref[1:2, :]
        inside = (row_at >= 0) & (row_at < length) & (col_at >= 0) & (col_at < length)
        mask[:, k * strip : (k + 1) * strip] = jnp.where(inside, 1.0, 0.0)

    turn = lax.rem(row_index, windows)
    for n, ref in enumerate((first_ref, second_ref)):
        lines = []
        for ti in (1, 0, 2):
            blocks = [ref[3 * ti + tj].astype(F32) for tj in range(3)]
            lines.append(jnp.concatenate(blocks, axis=1))
        stack[n] = jnp.concatenate(lines, axis=0).astype(BF16)

    ordered = []
    for offset in range(windows):
        value = window_refs[0][...]
        for t in range(1, windows):
            piece = lax.rem(t - turn + windows, windows)
            value = jnp.where(piece == offset, window_refs[t][...], value)
        low = 0 if offset == 0 else HALO
        high = rows + (2 * HALO if offset == windows - 1 else HALO)
        ordered.append(value[:, low:high].astype(F32))
    colval = jnp.concatenate(ordered, axis=1).astype(BF16)
    colval = jnp.dot(colval, spread_col[...], preferred_element_type=F32)
    col_flat, val_flat = colval[:channels], colval[channels:]

    for buf, edge, part in (
        (start_buf, guard, ((0, total),)), (hidden_buf, guard, spans_mid),
        (taps_first[1], far, spans_in), (taps_second[1], far, spans_mid),
    ):
        low, high = part[0][0], part[-1][1]
        fill = jnp.zeros((buf.shape[0], edge), buf.dtype)
        buf[:, low : low + edge] = fill
        buf[:, high + edge : high + 2 * edge] = fill

    def start_strip(k):
        row_flat = jnp.dot(
            row_ref[:, k * GROUP : (k + 1) * GROUP], spread_row[...], preferred_element_type=F32
        )
        pair = pair_ref[:, k * strip : (k + 1) * strip].astype(F32)
        value = pair + row_flat + col_flat
        value = jnp.where(mask[:, k * strip : (k + 1) * strip] > 0, value, 0.0)
        start_buf[:, guard + k * strip : guard + (k + 1) * strip] = value.astype(BF16)

    lane = lane_ids((channels, LANES))
    turned = {}

    def shifted(key, load, at, low, high):
        tiles = []
        for tile in range(low // LANES, high // LANES):
            first, off = divmod(tile * LANES + at, LANES)
            pair = []
            for place in (first, first + 1):
                if (key, at, place) not in turned:
                    turned[key, at, place] = pltpu.roll(load(place), LANES - off, 1)
                pair.append(turned[key, at, place])
            tiles.append(jnp.where(lane < LANES - off, *pair))
        return jnp.concatenate(tiles, axis=1)

    def spread(source, taps, n, low, high):
        def load(tile):
            return source[:, guard + tile * LANES : guard + (tile + 1) * LANES]

        stacked = [
            shifted((n, 0), load, -2, low, high),
            source[:, guard + low : guard + high],
            shifted((n, 0), load, 2, low, high),
        ]
        stacked = jnp.concatenate(stacked, axis=0)
        result = jnp.dot(stack[n], stacked, preferred_element_type=F32)
        taps[0][:, low:high] = result[:channels]
        taps[1][:, far + low : far + high] = result[channels:].astype(BF16)

    def gather(n, taps, low, high):
        value = taps[0][:, low:high]
        for part, at in ((0, -reach), (1, reach)):

            def load(tile):
                lanes = slice(far + tile * LANES, far + (tile + 1) * LANES)
                return taps[1][part * channels : (part + 1) * channels, lanes]

            value = value + shifted((n, 1), load, at, low, high).astype(F32)
        return jnp.maximum(value, 0.0)

    def first_span(low, high):
        spread(start_buf, taps_first, 0, low, high)

    def hidden_span(low, high):
        value = jnp.where(mask[:, low:high] > 0, gather(0, taps_first, low, high), 0.0)
        hidden_buf[:, guard + low : guard + high] = value.astype(BF16)

    def second_span(low, high):
        spread(hidden_buf, taps_second, 1, low, high)

    def pair_span(low, high):
        value = gather(1, taps_second, low, high)
        pair = start_buf[:, guard + low : guard + high].astype(F32) + value
        start_buf[:, guard + low : guard + high] = pair.astype(BF16)

    def gate_strip(k):
        pair = start_buf[:, guard + k * strip : guard + (k + 1) * strip]
        wide = pair.astype(F32)
        gate = jax.nn.sigmoid(wide).astype(BF16)
        product = (gate.astype(F32) * val_flat).astype(BF16)
        outs[0][:, k * GROUP : (k + 1) * GROUP] = jnp.dot(
            product, collect[...], preferred_element_type=F32
        )
        if not last:
            outs[1][:, k * strip : (k + 1) * strip] = pair
        else:
            for i in range(GROUP):
                for t in range(cols // LANES):
                    at = i * stride + HALO + t * LANES
                    flat = raw.at[t].reshape(channels * tall, LANES)
                    flat[pl.ds(k * GROUP + i, channels, stride=tall), :] = wide[:, at : at + LANES]

    strip_spans = [(k * strip, (k + 1) * strip) for k in range(strips)]
    stages = [
        (strip_spans, lambda low, high: start_strip(low // strip), 0),
        (spans_in, first_span, guard),
        (spans_mid, hidden_span, reach),
        (spans_mid, second_span, guard),
        (spans_out, pair_span, reach),
        (strip_spans, lambda low, high: gate_strip(low // strip), 0),
    ]
    done, made = [0] * len(stages), [0] * len(stages)

    def ready(n):
        parts, _, ahead = stages[n]
        if done[n] == len(parts):
            return False
        if n == 0 or done[n - 1] == len(stages[n - 1][0]):
            return True
        return parts[done[n]][1] + ahead <= made[n - 1]

    while any(done[n] < len(stages[n][0]) for n in range(len(stages))):
        for n in reversed(range(len(stages))):
            if ready(n):
                low, high = stages[n][0][done[n]]
                stages[n][1](low, high)
                done[n], made[n] = done[n] + 1, high

    if last:
        half = channels // 2
        for t in range(cols // LANES):
            lanes = slice(t * LANES, (t + 1) * LANES)
            for out, owner in ((outs[1], rep), (outs[2], 1 - rep)):
                value = raw[t, pl.ds(owner * half, half), HALO : HALO + rows, :]
                out[:, :, lanes] = value.astype(BF16)


def run_cycle(pair, row_proj, windows, first, second, rows, cols, length, last):
    channels = row_proj.shape[0]
    stride = cols + 2 * HALO
    total = (rows + 2 * HALO) * stride
    strip = GROUP * stride
    lane = np.arange(strip)
    place = np.stack([lane // stride, lane % stride] + [0 * lane] * 6).astype(np.int32)
    spread_row = (place[0] == np.arange(GROUP)[:, None]).astype(BF16)
    spread_col = (place[1] == np.arange(stride)[:, None]).astype(BF16)
    inner = (place[1] >= HALO) & (place[1] < HALO + cols)
    collect = (spread_row.T.astype(np.float32) * inner[:, None]).astype(BF16)
    far = -(-2 * stride // LANES) * LANES
    sums = ((channels, rows + 2 * HALO), F32)
    half = ((channels // 2, rows, cols), BF16)
    outs = (sums, half, half) if last else (sums, ((channels, total), BF16))
    scratch = [
        pltpu.VMEM((channels, total + 2 * LANES), BF16),
        pltpu.VMEM((channels, total + 2 * LANES), BF16),
        pltpu.VMEM((channels, total), F32),
        pltpu.VMEM((2 * channels, total + 2 * far), BF16),
        pltpu.VMEM((channels, total), F32),
        pltpu.VMEM((2 * channels, total + 2 * far), BF16),
        pltpu.VMEM((2, 3 * channels, 3 * channels), BF16),
        pltpu.VMEM((1, total), F32),
        pltpu.VMEM((cols // LANES, channels, rows + 2 * HALO, LANES), F32),
    ]
    kernel = functools.partial(cycle_kernel, rows, cols, length, last, len(windows))
    return call(
        kernel, outs, scratch, pair, row_proj, *windows, first, second,
        spread_row, spread_col, collect, place,
        limit=10 + total // 512, flops=40 * channels * channels * total,
    )


def on_device(seq_in, pair_in, w_row, w_col, w_value, conv_first, conv_second, w_out):
    rows, features = seq_in.shape
    channels = w_row.shape[1]
    half = channels // 2
    cols = pair_in.shape[2] // 2
    stride = cols + 2 * HALO
    tall = rows + 2 * HALO
    row_size, col_size = lax.axis_size("row"), lax.axis_size("col")
    chunks = 2 * col_size
    length = rows * row_size
    windows = cols // rows
    root = np.float32(np.sqrt(np.float32(length)))
    every = ("row", "col", "rep")
    weights = (w_row.T, w_col.T, w_value.T)
    swap = [(0, 1), (1, 0)]

    def pairs(begin, size):
        moves = []
        for i in range(begin, size - 1, 2):
            moves += [(i, i + 1), (i + 1, i)]
        return moves

    across = pairs(1, chunks)
    if chunks == 4:
        across += [(0, 3), (3, 0)]

    def to_columns(value):
        results = []
        for t in range(windows):
            moves = []
            for r in range(row_size):
                for q in range(chunks):
                    source = windows * q + (t - r) % windows
                    replica = (r // windows) ^ (chunks // 2)
                    moves.append((source * chunks + replica, r * chunks + q))
            results.append(lax.ppermute(value, every, moves))
        return results

    def all_parts(value):
        if chunks & (chunks - 1):
            partners = [[(i, (i + b) % chunks) for i in range(chunks)] for b in range(1, chunks)]
        else:
            partners = [[(i, i ^ b) for i in range(chunks)] for b in range(1, chunks)]
        return [value] + [lax.ppermute(value, ("col", "rep"), moves) for moves in partners]

    far_pair = lax.ppermute(pair_in, "rep", swap)
    width = pair_in.shape[2]
    message = ((-(-GROUP * (half + features // width) // 16) * 16, width), BF16)
    first_out, second_out = call(
        strips_kernel, [message, message],
        [
            pltpu.VMEM((2, half, 2 * GROUP, width), BF16),
            pltpu.VMEM((2, 2 * GROUP, features), BF16),
            pltpu.SemaphoreType.DMA((4,)),
        ],
        pair_in, seq_in, space=pl.ANY, limit=56,
    )
    first = lax.ppermute(first_out, "row", pairs(0, row_size))
    second = lax.ppermute(second_out, "row", pairs(1, row_size))
    wide = [((tall, features), BF16), ((channels, tall), BF16), ((2 * channels, tall), BF16)]
    feats, row_proj, colval = call(
        functools.partial(project_kernel, half), wide, [],
        seq_in, first, second, *weights
    )
    col_windows = to_columns(colval)
    first_far = lax.ppermute(first, "rep", swap)
    second_far = lax.ppermute(second, "rep", swap)
    pieces = (pair_in, first, second, far_pair, first_far, second_far)
    (edge,) = call(edges_kernel, [((channels * GROUP, LANES), BF16)], [], *pieces)
    pieces += (lax.ppermute(edge, ("col", "rep"), across),)
    (pair,) = call(
        functools.partial(assemble_kernel, cols), [((channels, tall * stride), BF16)],
        [pltpu.VMEM((cols // LANES + 1, channels, tall, LANES), F32)],
        *pieces, limit=24, flops=1 << 30,
    )

    sums, pair = run_cycle(
        pair, row_proj, col_windows, conv_first, conv_second, rows, cols, length, False
    )
    parts = all_parts(sums)
    feats, row_proj, colval = call(
        functools.partial(middle_kernel, root, chunks), wide, [],
        *parts, feats, w_out, *weights,
    )
    col_windows = to_columns(colval)
    sums, own, send = run_cycle(
        pair, row_proj, col_windows, conv_first, conv_second, rows, cols, length, True
    )
    parts = all_parts(sums)
    far_half = lax.ppermute(send, "rep", swap)
    return call(
        functools.partial(finish_kernel, root, chunks),
        [(seq_in.shape, BF16), (pair_in.shape, BF16)], [],
        *parts, feats, w_out, own, far_half,
    )


def solution(mesh):
    in_specs = (
        P(("grp", "row"), None),
        P(("grp", "rep"), "row", "col"),
        P(),
        P(),
        P(),
        P(),
        P(),
        P(),
    )
    out_specs = (P(("grp", "row"), None), P(("grp", "rep"), "row", "col"))
    return jax.shard_map(
        on_device, mesh=mesh, in_specs=in_specs, out_specs=out_specs, check_vma=False
    )
```

```python
import functools

import jax
import jax.numpy as jnp
import numpy as np
from jax import lax
from jax.experimental import pallas as pl
from jax.experimental.pallas import tpu as pltpu
from jax.sharding import PartitionSpec as P

CYCLES = 2
HALO = 8
GROUP = 8
LANES = 128
CHUNK = 3840
F32, BF16 = jnp.float32, jnp.bfloat16
def call(kernel, outs, scratch, *args, space=pltpu.VMEM, limit=16, flops=1 << 20):
    moved = sum(int(np.prod(x.shape)) * x.dtype.itemsize for x in args)
    return pl.pallas_call(
        kernel,
        out_shape=tuple(jax.ShapeDtypeStruct(shape, dtype) for shape, dtype in outs),
        in_specs=[pl.BlockSpec(memory_space=space)] * len(args),
        out_specs=(pl.BlockSpec(memory_space=pltpu.VMEM),) * len(outs),
        scratch_shapes=scratch,
        compiler_params=pltpu.CompilerParams(vmem_limit_bytes=limit << 20),
        cost_estimate=pl.CostEstimate(flops=flops, bytes_accessed=moved, transcendentals=0),
    )(*args)


def lane_ids(shape):
    return lax.broadcasted_iota(jnp.int32, shape, len(shape) - 1)


def is_even():
    return lax.rem(lax.axis_index("row"), 2) == 0


def strips_kernel(tile_ref, seq_ref, first_ref, second_ref, tile_ends, seq_ends, sems):
    half, rows, width = tile_ref.shape
    even = is_even()

    def message(pair, seq):
        pieces = [pair.reshape(half * GROUP, width)]
        pieces += [seq[:, at : at + width] for at in range(0, seq.shape[1], width)]
        rest = first_ref.shape[0] - GROUP * (half + len(pieces) - 1)
        if rest:
            pieces.append(jnp.zeros((rest, width), F32))
        return jnp.concatenate(pieces, axis=0)

    moves = []
    for n, at in enumerate((0, rows - 2 * GROUP)):
        lines = pl.ds(at, 2 * GROUP)
        moves += [
            pltpu.make_async_copy(tile_ref.at[:, lines, :], tile_ends.at[n], sems.at[2 * n]),
            pltpu.make_async_copy(seq_ref.at[lines, :], seq_ends.at[n], sems.at[2 * n + 1]),
        ]
    for move in moves:
        move.start()
    for move in moves:
        move.wait()
    top = message(
        tile_ends[0].astype(F32)[:, :GROUP], seq_ends[0].astype(F32)[:GROUP]
    )
    bottom = message(
        tile_ends[1].astype(F32)[:, GROUP:], seq_ends[1].astype(F32)[GROUP:]
    )
    first_ref[...] = jnp.where(even, bottom, top).astype(BF16)
    second_ref[...] = jnp.where(even, top, bottom).astype(BF16)


def received(first, second):
    even = is_even()
    return jnp.where(even, second, first), jnp.where(even, first, second)


def tile_pieces(tile_ref, first_ref, second_ref, at):
    half, rows, _ = tile_ref.shape
    middle = tile_ref[:, :, pl.ds(at, LANES)].astype(F32)
    above, below = received(
        *(
            ref[0 : half * GROUP, pl.ds(at, LANES)].astype(F32).reshape(half, GROUP, LANES)
            for ref in (first_ref, second_ref)
        )
    )
    middle = [middle[:, m * GROUP : (m + 1) * GROUP] for m in range(rows // GROUP)]
    return [above, *middle, below]


def edges_kernel(*refs):
    parts, out_ref = (refs[0:3], refs[3:6]), refs[6]
    rep = lax.axis_index("rep")
    half, _, width = refs[0].shape
    lane = lane_ids((half, GROUP, LANES))
    at = pl.multiple_of(jnp.where(rep == 0, 0, width - LANES), LANES)
    for part in range(2):
        packed = jnp.zeros((half, GROUP, LANES), F32)
        turn = jnp.where(rep == 0, 0, HALO)
        for g, piece in enumerate(tile_pieces(*parts[part], at)):
            moved = pltpu.roll(piece, turn + HALO * g, 2)
            packed = jnp.where((lane >= HALO * g) & (lane < HALO * (g + 1)), moved, packed)
        base = (rep if part == 0 else 1 - rep) * half * GROUP
        out_ref[pl.ds(pl.multiple_of(base, 2 * GROUP), half * GROUP), :] = packed.reshape(
            half * GROUP, LANES
        ).astype(BF16)


def unpack(parts, edge_ref, raw, cols):
    rep = lax.axis_index("rep")
    across = cols // LANES
    half = parts[0][0].shape[0]
    inner_at = pl.multiple_of(jnp.where(rep == 0, cols, cols - LANES), LANES)
    is_outer = (lane_ids((half, GROUP, LANES)) < HALO) == (rep == 0)
    for part in range(2):
        owner = pl.ds((rep if part == 0 else 1 - rep) * half, half)
        for t in range(across):
            at = pl.multiple_of(rep * cols + t * LANES, LANES)
            for g, piece in enumerate(tile_pieces(*parts[part], at)):
                raw[t, owner, g * GROUP : (g + 1) * GROUP, :] = piece
        base = (rep if part == 0 else 1 - rep) * half * GROUP
        edge = edge_ref[pl.ds(pl.multiple_of(base, 2 * GROUP), half * GROUP), :].astype(F32)
        edge = edge.reshape(half, GROUP, LANES)
        outer = pltpu.roll(edge, jnp.where(rep == 0, 0, HALO), 2)
        for g, piece in enumerate(tile_pieces(*parts[part], inner_at)):
            raw[across, owner, g * GROUP : (g + 1) * GROUP, :] = jnp.where(
                is_outer,
                pltpu.roll(outer, (-HALO * g) % LANES, 2),
                pltpu.roll(piece, HALO, 2),
            )


def assemble_kernel(cols, *refs):
    parts, edge_ref, out_ref, raw = (refs[0:3], refs[3:6]), refs[6], refs[7], refs[8]
    unpack(parts, edge_ref, raw, cols)
    strip = GROUP * (cols + 2 * HALO)
    for k in range(raw.shape[2] // GROUP):
        out_ref[:, k * strip : (k + 1) * strip] = raw_strip(raw, k)


def raw_strip(raw, place):
    across, channels, rows, _ = raw.shape
    pieces = []
    for i in range(place * GROUP, (place + 1) * GROUP):
        tiles = [
            raw.at[t].reshape(channels * rows, LANES)[pl.ds(i, channels, stride=rows), :].astype(BF16)
            for t in range(across)
        ]
        side = tiles.pop()
        pieces += [side[:, :HALO], *tiles, side[:, HALO : 2 * HALO]]
    return jnp.concatenate(pieces, axis=1)


def project(feats, weight_refs, row_ref, colval_ref):
    row, col, value = (
        lax.dot_general(ref[...], feats, (((1,), (1,)), ((), ())), preferred_element_type=F32)
        for ref in weight_refs
    )
    channels = row.shape[0]
    row_ref[...] = row.astype(BF16)
    colval_ref[0:channels] = col.astype(BF16)
    colval_ref[channels:] = value.astype(BF16)


def project_kernel(half, seq_ref, first_ref, second_ref, *refs):
    weight_refs, (feats_ref, row_ref, colval_ref) = refs[:3], refs[3:]
    width = first_ref.shape[1]
    split = seq_ref.shape[1] // width
    halos = []
    for ref in (first_ref, second_ref):
        tail = ref[half * GROUP :, :].astype(F32)
        pieces = [tail[j * GROUP : (j + 1) * GROUP] for j in range(split)]
        halos.append(jnp.concatenate(pieces, axis=1))
    above, below = received(*halos)
    feats = jnp.concatenate([above, seq_ref[...].astype(F32), below], axis=0).astype(BF16)
    feats_ref[...] = feats
    project(feats, weight_refs, row_ref, colval_ref)


def advance(sum_refs, feats_ref, out_ref, root):
    total = sum_refs[0][...]
    for ref in sum_refs[1:]:
        total = total + ref[...]
    gathered = (total / root).T.astype(BF16)
    change = jnp.dot(gathered, out_ref[...], preferred_element_type=F32)
    return feats_ref[...].astype(F32) + change


def middle_kernel(root, parts, *refs):
    sum_refs, refs = refs[:parts], refs[parts:]
    feats_in, out_w, weight_refs, (feats_ref, row_ref, colval_ref) = (
        refs[0], refs[1], refs[2:5], refs[5:]
    )
    feats = advance(sum_refs, feats_in, out_w, root).astype(BF16)
    feats_ref[...] = feats
    project(feats, weight_refs, row_ref, colval_ref)


def finish_kernel(root, parts, *refs):
    sum_refs, refs = refs[:parts], refs[parts:]
    feats_in, out_w, own_ref, far_ref, seq_ref, pair_ref = refs
    rep = lax.axis_index("rep")
    rows, cols = seq_ref.shape[0], own_ref.shape[2]
    seq_ref[...] = advance(sum_refs, feats_in, out_w, root)[HALO : HALO + rows].astype(BF16)
    pair_ref[:, :, pl.ds(pl.multiple_of(rep * cols, LANES), cols)] = own_ref[...]
    pair_ref[:, :, pl.ds(pl.multiple_of((1 - rep) * cols, LANES), cols)] = far_ref[...]


def spans(low_row, high_row, stride, total):
    low = low_row * stride // LANES * LANES
    size = -(-(high_row * stride - low) // 256) * 256
    high = min(low + size, total)
    return [(at, min(at + CHUNK, high)) for at in range(low, high, CHUNK)]


def cycle_kernel(rows, cols, length, last, windows, *refs):
    (start_buf, hidden_buf, *taps, stack, mask, raw), refs = refs[-9:], refs[:-9]
    taps_first, taps_second = taps[0:2], taps[2:4]
    pair_ref, refs = refs[0], refs[1:]
    row_ref, window_refs, refs = refs[0], refs[1 : 1 + windows], refs[1 + windows :]
    first_ref, second_ref, spread_row, spread_col, collect, place_ref, *outs = refs
    channels = row_ref.shape[0]
    stride = cols + 2 * HALO
    tall = rows + 2 * HALO
    total = tall * stride
    strip = GROUP * stride
    strips = tall // GROUP
    guard = LANES
    reach = 2 * stride
    far = -(-reach // LANES) * LANES
    rep = lax.axis_index("rep")
    row_index = lax.axis_index("row")
    chunk_index = lax.axis_index("col") * 2 + rep
    margin = 2 * CYCLES * 2 - (8 if not last else 4)
    spans_in = spans(margin, rows + 2 * HALO - margin, stride, total)
    spans_mid = spans(margin + 2, rows + 2 * HALO - margin - 2, stride, total)
    spans_out = spans(margin + 4, rows + 2 * HALO - margin - 4, stride, total)

    for k in range(strips):
        row_at = row_index * rows - HALO + k * GROUP + place_ref[0:1, :]
        col_at = chunk_index * cols - HALO + place_ref[1:2, :]
        inside = (row_at >= 0) & (row_at < length) & (col_at >= 0) & (col_at < length)
        mask[:, k * strip : (k + 1) * strip] = jnp.where(inside, 1.0, 0.0)

    turn = lax.rem(row_index, windows)
    for n, ref in enumerate((first_ref, second_ref)):
        lines = []
        for ti in (1, 0, 2):
            blocks = [ref[3 * ti + tj].astype(F32) for tj in range(3)]
            lines.append(jnp.concatenate(blocks, axis=1))
        stack[n] = jnp.concatenate(lines, axis=0).astype(BF16)

    ordered = []
    for offset in range(windows):
        value = window_refs[0][...]
        for t in range(1, windows):
            piece = lax.rem(t - turn + windows, windows)
            value = jnp.where(piece == offset, window_refs[t][...], value)
        low = 0 if offset == 0 else HALO
        high = rows + (2 * HALO if offset == windows - 1 else HALO)
        ordered.append(value[:, low:high].astype(F32))
    colval = jnp.concatenate(ordered, axis=1).astype(BF16)
    colval = jnp.dot(colval, spread_col[...], preferred_element_type=F32)
    col_flat, val_flat = colval[:channels], colval[channels:]

    for buf, edge, part in (
        (start_buf, guard, ((0, total),)), (hidden_buf, guard, spans_mid),
        (taps_first[1], far, spans_in), (taps_second[1], far, spans_mid),
    ):
        low, high = part[0][0], part[-1][1]
        fill = jnp.zeros((buf.shape[0], edge), buf.dtype)
        buf[:, low : low + edge] = fill
        buf[:, high + edge : high + 2 * edge] = fill

    def start_strip(k):
        row_flat = jnp.dot(
            row_ref[:, k * GROUP : (k + 1) * GROUP], spread_row[...], preferred_element_type=F32
        )
        pair = pair_ref[:, k * strip : (k + 1) * strip].astype(F32)
        value = pair + row_flat + col_flat
        value = jnp.where(mask[:, k * strip : (k + 1) * strip] > 0, value, 0.0)
        start_buf[:, guard + k * strip : guard + (k + 1) * strip] = value.astype(BF16)

    lane = lane_ids((channels, LANES))
    turned = {}

    def shifted(key, load, at, low, high):
        tiles = []
        for tile in range(low // LANES, high // LANES):
            first, off = divmod(tile * LANES + at, LANES)
            pair = []
            for place in (first, first + 1):
                if (key, at, place) not in turned:
                    turned[key, at, place] = pltpu.roll(load(place), LANES - off, 1)
                pair.append(turned[key, at, place])
            tiles.append(jnp.where(lane < LANES - off, *pair))
        return jnp.concatenate(tiles, axis=1)

    def spread(source, taps, n, low, high):
        def load(tile):
            return source[:, guard + tile * LANES : guard + (tile + 1) * LANES]

        stacked = [
            shifted((n, 0), load, -2, low, high),
            source[:, guard + low : guard + high],
            shifted((n, 0), load, 2, low, high),
        ]
        stacked = jnp.concatenate(stacked, axis=0)
        result = jnp.dot(stack[n], stacked, preferred_element_type=F32)
        taps[0][:, low:high] = result[:channels]
        taps[1][:, far + low : far + high] = result[channels:].astype(BF16)

    def gather(n, taps, low, high):
        value = taps[0][:, low:high]
        for part, at in ((0, -reach), (1, reach)):

            def load(tile):
                lanes = slice(far + tile * LANES, far + (tile + 1) * LANES)
                return taps[1][part * channels : (part + 1) * channels, lanes]

            value = value + shifted((n, 1), load, at, low, high).astype(F32)
        return jnp.maximum(value, 0.0)

    def first_span(low, high):
        spread(start_buf, taps_first, 0, low, high)

    def hidden_span(low, high):
        value = jnp.where(mask[:, low:high] > 0, gather(0, taps_first, low, high), 0.0)
        hidden_buf[:, guard + low : guard + high] = value.astype(BF16)

    def second_span(low, high):
        spread(hidden_buf, taps_second, 1, low, high)

    def pair_span(low, high):
        value = gather(1, taps_second, low, high)
        pair = start_buf[:, guard + low : guard + high].astype(F32) + value
        start_buf[:, guard + low : guard + high] = pair.astype(BF16)

    def gate_strip(k):
        if last and k in (0, strips - 1):
            outs[0][:, k * GROUP : (k + 1) * GROUP] = jnp.zeros((channels, GROUP), F32)
            return
        pair = start_buf[:, guard + k * strip : guard + (k + 1) * strip]
        wide = pair.astype(F32)
        gate = jax.nn.sigmoid(wide).astype(BF16)
        product = (gate.astype(F32) * val_flat).astype(BF16)
        outs[0][:, k * GROUP : (k + 1) * GROUP] = jnp.dot(
            product, collect[...], preferred_element_type=F32
        )
        if not last:
            outs[1][:, k * strip : (k + 1) * strip] = pair
        else:
            for i in range(GROUP):
                for t in range(cols // LANES):
                    at = i * stride + HALO + t * LANES
                    flat = raw.at[t].reshape(channels * tall, LANES)
                    piece = pair[:, at : at + LANES].astype(F32)
                    flat[pl.ds(k * GROUP + i, channels, stride=tall), :] = piece

    strip_spans = [(k * strip, (k + 1) * strip) for k in range(strips)]
    stages = [
        (strip_spans, lambda low, high: start_strip(low // strip), 0),
        (spans_in, first_span, guard),
        (spans_mid, hidden_span, reach),
        (spans_mid, second_span, guard),
        (spans_out, pair_span, reach),
        (strip_spans, lambda low, high: gate_strip(low // strip), 0),
    ]
    done, made = [0] * len(stages), [0] * len(stages)

    def ready(n):
        parts, _, ahead = stages[n]
        if done[n] == len(parts):
            return False
        if n == 0 or done[n - 1] == len(stages[n - 1][0]):
            return True
        return parts[done[n]][1] + ahead <= made[n - 1]

    while any(done[n] < len(stages[n][0]) for n in range(len(stages))):
        for n in reversed(range(len(stages))):
            if ready(n):
                low, high = stages[n][0][done[n]]
                stages[n][1](low, high)
                done[n], made[n] = done[n] + 1, high

    if last:
        half = channels // 2
        for t in range(cols // LANES):
            lanes = slice(t * LANES, (t + 1) * LANES)
            for out, owner in ((outs[1], rep), (outs[2], 1 - rep)):
                value = raw[t, pl.ds(owner * half, half), HALO : HALO + rows, :]
                out[:, :, lanes] = value.astype(BF16)


def run_cycle(pair, row_proj, windows, first, second, rows, cols, length, last):
    channels = row_proj.shape[0]
    stride = cols + 2 * HALO
    total = (rows + 2 * HALO) * stride
    strip = GROUP * stride
    lane = np.arange(strip)
    place = np.stack([lane // stride, lane % stride] + [0 * lane] * 6).astype(np.int32)
    spread_row = (place[0] == np.arange(GROUP)[:, None]).astype(BF16)
    spread_col = (place[1] == np.arange(stride)[:, None]).astype(BF16)
    inner = (place[1] >= HALO) & (place[1] < HALO + cols)
    collect = (spread_row.T.astype(np.float32) * inner[:, None]).astype(BF16)
    far = -(-2 * stride // LANES) * LANES
    sums = ((channels, rows + 2 * HALO), F32)
    half = ((channels // 2, rows, cols), BF16)
    outs = (sums, half, half) if last else (sums, ((channels, total), BF16))
    scratch = [
        pltpu.VMEM((channels, total + 2 * LANES), BF16),
        pltpu.VMEM((channels, total + 2 * LANES), BF16),
        pltpu.VMEM((channels, total), F32),
        pltpu.VMEM((2 * channels, total + 2 * far), BF16),
        pltpu.VMEM((channels, total), F32),
        pltpu.VMEM((2 * channels, total + 2 * far), BF16),
        pltpu.VMEM((2, 3 * channels, 3 * channels), BF16),
        pltpu.VMEM((1, total), F32),
        pltpu.VMEM((cols // LANES, channels, rows + 2 * HALO, LANES), F32),
    ]
    kernel = functools.partial(cycle_kernel, rows, cols, length, last, len(windows))
    return call(
        kernel, outs, scratch, pair, row_proj, *windows, first, second,
        spread_row, spread_col, collect, place,
        limit=10 + total // 512, flops=40 * channels * channels * total,
    )


def on_device(seq_in, pair_in, w_row, w_col, w_value, conv_first, conv_second, w_out):
    rows, features = seq_in.shape
    channels = w_row.shape[1]
    half = channels // 2
    cols = pair_in.shape[2] // 2
    stride = cols + 2 * HALO
    tall = rows + 2 * HALO
    row_size, col_size = lax.axis_size("row"), lax.axis_size("col")
    chunks = 2 * col_size
    length = rows * row_size
    windows = cols // rows
    root = np.float32(np.sqrt(np.float32(length)))
    every = ("row", "col", "rep")
    weights = (w_row.T, w_col.T, w_value.T)
    swap = [(0, 1), (1, 0)]

    def pairs(begin, size):
        moves = []
        for i in range(begin, size - 1, 2):
            moves += [(i, i + 1), (i + 1, i)]
        return moves

    across = pairs(1, chunks)
    if chunks == 4:
        across += [(0, 3), (3, 0)]

    def to_columns(value):
        results = []
        for t in range(windows):
            moves = []
            for r in range(row_size):
                for q in range(chunks):
                    source = windows * q + (t - r) % windows
                    replica = (r // windows) ^ ((chunks // 2 + t % 2) % chunks)
                    moves.append((source * chunks + replica, r * chunks + q))
            results.append(lax.ppermute(value, every, moves))
        return results

    def all_parts(value):
        if chunks & (chunks - 1):
            partners = [[(i, (i + b) % chunks) for i in range(chunks)] for b in range(1, chunks)]
        else:
            partners = [[(i, i ^ b) for i in range(chunks)] for b in range(1, chunks)]
        return [value] + [lax.ppermute(value, ("col", "rep"), moves) for moves in partners]

    far_pair = lax.ppermute(pair_in, "rep", swap)
    width = pair_in.shape[2]
    message = ((-(-GROUP * (half + features // width) // 16) * 16, width), BF16)
    first_out, second_out = call(
        strips_kernel, [message, message],
        [
            pltpu.VMEM((2, half, 2 * GROUP, width), BF16),
            pltpu.VMEM((2, 2 * GROUP, features), BF16),
            pltpu.SemaphoreType.DMA((4,)),
        ],
        pair_in, seq_in, space=pl.ANY, limit=56,
    )
    first = lax.ppermute(first_out, "row", pairs(0, row_size))
    second = lax.ppermute(second_out, "row", pairs(1, row_size))
    wide = [((tall, features), BF16), ((channels, tall), BF16), ((2 * channels, tall), BF16)]
    feats, row_proj, colval = call(
        functools.partial(project_kernel, half), wide, [],
        seq_in, first, second, *weights
    )
    col_windows = to_columns(colval)
    first_far = lax.ppermute(first, "rep", swap)
    second_far = lax.ppermute(second, "rep", swap)
    pieces = (pair_in, first, second, far_pair, first_far, second_far)
    (edge,) = call(edges_kernel, [((channels * GROUP, LANES), BF16)], [], *pieces)
    pieces += (lax.ppermute(edge, ("col", "rep"), across),)
    (pair,) = call(
        functools.partial(assemble_kernel, cols), [((channels, tall * stride), BF16)],
        [pltpu.VMEM((cols // LANES + 1, channels, tall, LANES), F32)],
        *pieces, limit=24, flops=1 << 30,
    )

    sums, pair = run_cycle(
        pair, row_proj, col_windows, conv_first, conv_second, rows, cols, length, False
    )
    parts = all_parts(sums)
    feats, row_proj, colval = call(
        functools.partial(middle_kernel, root, chunks), wide, [],
        *parts, feats, w_out, *weights,
    )
    col_windows = to_columns(colval)
    sums, own, send = run_cycle(
        pair, row_proj, col_windows, conv_first, conv_second, rows, cols, length, True
    )
    parts = all_parts(sums)
    far_half = lax.ppermute(send, "rep", swap)
    return call(
        functools.partial(finish_kernel, root, chunks),
        [(seq_in.shape, BF16), (pair_in.shape, BF16)], [],
        *parts, feats, w_out, own, far_half,
    )


def solution(mesh):
    in_specs = (
        P(("grp", "row"), None),
        P(("grp", "rep"), "row", "col"),
        P(),
        P(),
        P(),
        P(),
        P(),
        P(),
    )
    out_specs = (P(("grp", "row"), None), P(("grp", "rep"), "row", "col"))
    return jax.shard_map(
        on_device, mesh=mesh, in_specs=in_specs, out_specs=out_specs, check_vma=False
    )
```

```python
import functools

import jax
import jax.numpy as jnp
import numpy as np
from jax import lax
from jax.experimental import pallas as pl
from jax.experimental.pallas import tpu as pltpu
from jax.sharding import PartitionSpec as P

CYCLES = 2
HALO = 8
GROUP = 8
LANES = 128
CHUNK = 3840
F32, BF16 = jnp.float32, jnp.bfloat16
def call(kernel, outs, scratch, *args, space=pltpu.VMEM, limit=16, flops=1 << 20):
    moved = sum(int(np.prod(x.shape)) * x.dtype.itemsize for x in args)
    return pl.pallas_call(
        kernel,
        out_shape=tuple(jax.ShapeDtypeStruct(shape, dtype) for shape, dtype in outs),
        in_specs=[pl.BlockSpec(memory_space=space)] * len(args),
        out_specs=(pl.BlockSpec(memory_space=pltpu.VMEM),) * len(outs),
        scratch_shapes=scratch,
        compiler_params=pltpu.CompilerParams(vmem_limit_bytes=limit << 20),
        cost_estimate=pl.CostEstimate(flops=flops, bytes_accessed=moved, transcendentals=0),
    )(*args)


def lane_ids(shape):
    return lax.broadcasted_iota(jnp.int32, shape, len(shape) - 1)


def is_even():
    return lax.rem(lax.axis_index("row"), 2) == 0


def strips_kernel(tile_ref, seq_ref, first_ref, second_ref, tile_ends, seq_ends, sems):
    half, rows, width = tile_ref.shape
    even = is_even()

    def message(pair, seq):
        pieces = [pair.reshape(half * GROUP, width)]
        pieces += [seq[:, at : at + width] for at in range(0, seq.shape[1], width)]
        rest = first_ref.shape[0] - GROUP * (half + len(pieces) - 1)
        if rest:
            pieces.append(jnp.zeros((rest, width), F32))
        return jnp.concatenate(pieces, axis=0)

    moves = []
    for n, at in enumerate((0, rows - 2 * GROUP)):
        lines = pl.ds(at, 2 * GROUP)
        moves += [
            pltpu.make_async_copy(tile_ref.at[:, lines, :], tile_ends.at[n], sems.at[2 * n]),
            pltpu.make_async_copy(seq_ref.at[lines, :], seq_ends.at[n], sems.at[2 * n + 1]),
        ]
    for move in moves:
        move.start()
    for move in moves:
        move.wait()
    top = message(
        tile_ends[0].astype(F32)[:, :GROUP], seq_ends[0].astype(F32)[:GROUP]
    )
    bottom = message(
        tile_ends[1].astype(F32)[:, GROUP:], seq_ends[1].astype(F32)[GROUP:]
    )
    first_ref[...] = jnp.where(even, bottom, top).astype(BF16)
    second_ref[...] = jnp.where(even, top, bottom).astype(BF16)


def received(first, second):
    even = is_even()
    return jnp.where(even, second, first), jnp.where(even, first, second)


def tile_pieces(tile_ref, first_ref, second_ref, at):
    half, rows, _ = tile_ref.shape
    middle = tile_ref[:, :, pl.ds(at, LANES)].astype(F32)
    above, below = received(
        *(
            ref[0 : half * GROUP, pl.ds(at, LANES)].astype(F32).reshape(half, GROUP, LANES)
            for ref in (first_ref, second_ref)
        )
    )
    middle = [middle[:, m * GROUP : (m + 1) * GROUP] for m in range(rows // GROUP)]
    return [above, *middle, below]


def edges_kernel(*refs):
    parts, out_ref = (refs[0:3], refs[3:6]), refs[6]
    rep = lax.axis_index("rep")
    half, _, width = refs[0].shape
    lane = lane_ids((half, GROUP, LANES))
    at = pl.multiple_of(jnp.where(rep == 0, 0, width - LANES), LANES)
    for part in range(2):
        packed = jnp.zeros((half, GROUP, LANES), F32)
        turn = jnp.where(rep == 0, 0, HALO)
        for g, piece in enumerate(tile_pieces(*parts[part], at)):
            moved = pltpu.roll(piece, turn + HALO * g, 2)
            packed = jnp.where((lane >= HALO * g) & (lane < HALO * (g + 1)), moved, packed)
        base = (rep if part == 0 else 1 - rep) * half * GROUP
        out_ref[pl.ds(pl.multiple_of(base, 2 * GROUP), half * GROUP), :] = packed.reshape(
            half * GROUP, LANES
        ).astype(BF16)


def unpack(parts, edge_ref, raw, cols):
    rep = lax.axis_index("rep")
    across = cols // LANES
    half = parts[0][0].shape[0]
    inner_at = pl.multiple_of(jnp.where(rep == 0, cols, cols - LANES), LANES)
    is_outer = (lane_ids((half, GROUP, LANES)) < HALO) == (rep == 0)
    for part in range(2):
        owner = pl.ds((rep if part == 0 else 1 - rep) * half, half)
        for t in range(across):
            at = pl.multiple_of(rep * cols + t * LANES, LANES)
            for g, piece in enumerate(tile_pieces(*parts[part], at)):
                raw[t, owner, g * GROUP : (g + 1) * GROUP, :] = piece
        base = (rep if part == 0 else 1 - rep) * half * GROUP
        edge = edge_ref[pl.ds(pl.multiple_of(base, 2 * GROUP), half * GROUP), :].astype(F32)
        edge = edge.reshape(half, GROUP, LANES)
        outer = pltpu.roll(edge, jnp.where(rep == 0, 0, HALO), 2)
        for g, piece in enumerate(tile_pieces(*parts[part], inner_at)):
            raw[across, owner, g * GROUP : (g + 1) * GROUP, :] = jnp.where(
                is_outer,
                pltpu.roll(outer, (-HALO * g) % LANES, 2),
                pltpu.roll(piece, HALO, 2),
            )


def assemble_kernel(cols, *refs):
    parts, edge_ref, out_ref, raw = (refs[0:3], refs[3:6]), refs[6], refs[7], refs[8]
    unpack(parts, edge_ref, raw, cols)
    strip = GROUP * (cols + 2 * HALO)
    for k in range(raw.shape[2] // GROUP):
        out_ref[:, k * strip : (k + 1) * strip] = raw_strip(raw, k)


def raw_strip(raw, place):
    across, channels, rows, _ = raw.shape
    pieces = []
    for i in range(place * GROUP, (place + 1) * GROUP):
        tiles = [
            raw.at[t].reshape(channels * rows, LANES)[pl.ds(i, channels, stride=rows), :].astype(BF16)
            for t in range(across)
        ]
        side = tiles.pop()
        pieces += [side[:, :HALO], *tiles, side[:, HALO : 2 * HALO]]
    return jnp.concatenate(pieces, axis=1)


def project(feats, weight_refs, row_ref, colval_ref):
    row, col, value = (
        lax.dot_general(ref[...], feats, (((1,), (1,)), ((), ())), preferred_element_type=F32)
        for ref in weight_refs
    )
    channels = row.shape[0]
    row_ref[...] = row.astype(BF16)
    colval_ref[0:channels] = col.astype(BF16)
    colval_ref[channels:] = value.astype(BF16)


def project_kernel(half, seq_ref, first_ref, second_ref, *refs):
    weight_refs, (feats_ref, row_ref, colval_ref) = refs[:3], refs[3:]
    width = first_ref.shape[1]
    split = seq_ref.shape[1] // width
    halos = []
    for ref in (first_ref, second_ref):
        tail = ref[half * GROUP :, :].astype(F32)
        pieces = [tail[j * GROUP : (j + 1) * GROUP] for j in range(split)]
        halos.append(jnp.concatenate(pieces, axis=1))
    above, below = received(*halos)
    feats = jnp.concatenate([above, seq_ref[...].astype(F32), below], axis=0).astype(BF16)
    feats_ref[...] = feats
    project(feats, weight_refs, row_ref, colval_ref)


def advance(sum_refs, feats_ref, out_ref, root):
    total = sum_refs[0][...]
    for ref in sum_refs[1:]:
        total = total + ref[...]
    gathered = (total / root).T.astype(BF16)
    change = jnp.dot(gathered, out_ref[...], preferred_element_type=F32)
    return feats_ref[...].astype(F32) + change


def middle_kernel(root, parts, *refs):
    sum_refs, refs = refs[:parts], refs[parts:]
    feats_in, out_w, weight_refs, (feats_ref, row_ref, colval_ref) = (
        refs[0], refs[1], refs[2:5], refs[5:]
    )
    feats = advance(sum_refs, feats_in, out_w, root).astype(BF16)
    feats_ref[...] = feats
    project(feats, weight_refs, row_ref, colval_ref)


def finish_kernel(root, parts, *refs):
    sum_refs, refs = refs[:parts], refs[parts:]
    feats_in, out_w, own_ref, far_ref, seq_ref, pair_ref = refs
    rep = lax.axis_index("rep")
    rows, cols = seq_ref.shape[0], own_ref.shape[2]
    seq_ref[...] = advance(sum_refs, feats_in, out_w, root)[HALO : HALO + rows].astype(BF16)
    pair_ref[:, :, pl.ds(pl.multiple_of(rep * cols, LANES), cols)] = own_ref[...]
    pair_ref[:, :, pl.ds(pl.multiple_of((1 - rep) * cols, LANES), cols)] = far_ref[...]


def spans(low_row, high_row, stride, total):
    low = low_row * stride // LANES * LANES
    size = -(-(high_row * stride - low) // 256) * 256
    high = min(low + size, total)
    return [(at, min(at + CHUNK, high)) for at in range(low, high, CHUNK)]


def cycle_kernel(rows, cols, length, last, windows, *refs):
    (start_buf, hidden_buf, *taps, stack, mask, raw), refs = refs[-9:], refs[:-9]
    taps_first, taps_second = taps[0:2], taps[2:4]
    pair_ref, refs = refs[0], refs[1:]
    row_ref, window_refs, refs = refs[0], refs[1 : 1 + windows], refs[1 + windows :]
    first_ref, second_ref, spread_row, spread_col, collect, place_ref, *outs = refs
    channels = row_ref.shape[0]
    stride = cols + 2 * HALO
    tall = rows + 2 * HALO
    total = tall * stride
    strip = GROUP * stride
    strips = tall // GROUP
    guard = LANES
    reach = 2 * stride
    far = -(-reach // LANES) * LANES
    rep = lax.axis_index("rep")
    row_index = lax.axis_index("row")
    chunk_index = lax.axis_index("col") * 2 + rep
    margin = 2 * CYCLES * 2 - (8 if not last else 4)
    spans_in = spans(margin, rows + 2 * HALO - margin, stride, total)
    spans_mid = spans(margin + 2, rows + 2 * HALO - margin - 2, stride, total)
    spans_out = spans(margin + 4, rows + 2 * HALO - margin - 4, stride, total)

    for k in range(strips):
        row_at = row_index * rows - HALO + k * GROUP + place_ref[0:1, :]
        col_at = chunk_index * cols - HALO + place_ref[1:2, :]
        inside = (row_at >= 0) & (row_at < length) & (col_at >= 0) & (col_at < length)
        mask[:, k * strip : (k + 1) * strip] = jnp.where(inside, 1.0, 0.0)

    turn = lax.rem(row_index, windows)
    for n, ref in enumerate((first_ref, second_ref)):
        lines = []
        for ti in (1, 0, 2):
            blocks = [ref[3 * ti + tj].astype(F32) for tj in range(3)]
            lines.append(jnp.concatenate(blocks, axis=1))
        stack[n] = jnp.concatenate(lines, axis=0).astype(BF16)

    ordered = []
    for offset in range(windows):
        value = window_refs[0][...]
        for t in range(1, windows):
            piece = lax.rem(t + 1 - turn + windows, windows)
            value = jnp.where(piece == offset, window_refs[t][...], value)
        low = 0 if offset == 0 else HALO
        high = rows + (2 * HALO if offset == windows - 1 else HALO)
        ordered.append(value[:, low:high].astype(F32))
    colval = jnp.concatenate(ordered, axis=1).astype(BF16)
    colval = jnp.dot(colval, spread_col[...], preferred_element_type=F32)
    col_flat, val_flat = colval[:channels], colval[channels:]

    for buf, edge, part in (
        (start_buf, guard, ((0, total),)), (hidden_buf, guard, spans_mid),
        (taps_first[1], far, spans_in), (taps_second[1], far, spans_mid),
    ):
        low, high = part[0][0], part[-1][1]
        fill = jnp.zeros((buf.shape[0], edge), buf.dtype)
        buf[:, low : low + edge] = fill
        buf[:, high + edge : high + 2 * edge] = fill

    def start_strip(k):
        row_flat = jnp.dot(
            row_ref[:, k * GROUP : (k + 1) * GROUP], spread_row[...], preferred_element_type=F32
        )
        pair = pair_ref[:, k * strip : (k + 1) * strip].astype(F32)
        value = pair + row_flat + col_flat
        value = jnp.where(mask[:, k * strip : (k + 1) * strip] > 0, value, 0.0)
        start_buf[:, guard + k * strip : guard + (k + 1) * strip] = value.astype(BF16)

    lane = lane_ids((channels, LANES))
    turned = {}

    def shifted(key, load, at, low, high):
        tiles = []
        for tile in range(low // LANES, high // LANES):
            first, off = divmod(tile * LANES + at, LANES)
            pair = []
            for place in (first, first + 1):
                if (key, at, place) not in turned:
                    turned[key, at, place] = pltpu.roll(load(place), LANES - off, 1)
                pair.append(turned[key, at, place])
            tiles.append(jnp.where(lane < LANES - off, *pair))
        return jnp.concatenate(tiles, axis=1)

    def spread(source, taps, n, low, high):
        def load(tile):
            return source[:, guard + tile * LANES : guard + (tile + 1) * LANES]

        stacked = [
            shifted((n, 0), load, -2, low, high),
            source[:, guard + low : guard + high],
            shifted((n, 0), load, 2, low, high),
        ]
        stacked = jnp.concatenate(stacked, axis=0)
        result = jnp.dot(stack[n], stacked, preferred_element_type=F32)
        taps[0][:, low:high] = result[:channels]
        taps[1][:, far + low : far + high] = result[channels:].astype(BF16)

    def gather(n, taps, low, high):
        value = taps[0][:, low:high]
        for part, at in ((0, -reach), (1, reach)):

            def load(tile):
                lanes = slice(far + tile * LANES, far + (tile + 1) * LANES)
                return taps[1][part * channels : (part + 1) * channels, lanes]

            value = value + shifted((n, 1), load, at, low, high).astype(F32)
        return jnp.maximum(value, 0.0)

    def first_span(low, high):
        spread(start_buf, taps_first, 0, low, high)

    def hidden_span(low, high):
        value = jnp.where(mask[:, low:high] > 0, gather(0, taps_first, low, high), 0.0)
        hidden_buf[:, guard + low : guard + high] = value.astype(BF16)

    def second_span(low, high):
        spread(hidden_buf, taps_second, 1, low, high)

    def pair_span(low, high):
        value = gather(1, taps_second, low, high)
        pair = start_buf[:, guard + low : guard + high].astype(F32) + value
        start_buf[:, guard + low : guard + high] = pair.astype(BF16)

    def gate_strip(k):
        if last and k in (0, strips - 1):
            outs[0][:, k * GROUP : (k + 1) * GROUP] = jnp.zeros((channels, GROUP), F32)
            return
        pair = start_buf[:, guard + k * strip : guard + (k + 1) * strip]
        wide = pair.astype(F32)
        gate = jax.nn.sigmoid(wide).astype(BF16)
        product = (gate.astype(F32) * val_flat).astype(BF16)
        outs[0][:, k * GROUP : (k + 1) * GROUP] = jnp.dot(
            product, collect[...], preferred_element_type=F32
        )
        if not last:
            outs[1][:, k * strip : (k + 1) * strip] = pair
        else:
            for i in range(GROUP):
                for t in range(cols // LANES):
                    at = i * stride + HALO + t * LANES
                    flat = raw.at[t].reshape(channels * tall, LANES)
                    piece = pair[:, at : at + LANES].astype(F32)
                    flat[pl.ds(k * GROUP + i, channels, stride=tall), :] = piece

    strip_spans = [(k * strip, (k + 1) * strip) for k in range(strips)]
    stages = [
        (strip_spans, lambda low, high: start_strip(low // strip), 0),
        (spans_in, first_span, guard),
        (spans_mid, hidden_span, reach),
        (spans_mid, second_span, guard),
        (spans_out, pair_span, reach),
        (strip_spans, lambda low, high: gate_strip(low // strip), 0),
    ]
    done, made = [0] * len(stages), [0] * len(stages)

    def ready(n):
        parts, _, ahead = stages[n]
        if done[n] == len(parts):
            return False
        if n == 0 or done[n - 1] == len(stages[n - 1][0]):
            return True
        return parts[done[n]][1] + ahead <= made[n - 1]

    while any(done[n] < len(stages[n][0]) for n in range(len(stages))):
        for n in reversed(range(len(stages))):
            if ready(n):
                low, high = stages[n][0][done[n]]
                stages[n][1](low, high)
                done[n], made[n] = done[n] + 1, high

    if last:
        half = channels // 2
        for t in range(cols // LANES):
            lanes = slice(t * LANES, (t + 1) * LANES)
            for out, owner in ((outs[1], rep), (outs[2], 1 - rep)):
                value = raw[t, pl.ds(owner * half, half), HALO : HALO + rows, :]
                out[:, :, lanes] = value.astype(BF16)


def run_cycle(pair, row_proj, windows, first, second, rows, cols, length, last):
    channels = row_proj.shape[0]
    stride = cols + 2 * HALO
    total = (rows + 2 * HALO) * stride
    strip = GROUP * stride
    lane = np.arange(strip)
    place = np.stack([lane // stride, lane % stride] + [0 * lane] * 6).astype(np.int32)
    spread_row = (place[0] == np.arange(GROUP)[:, None]).astype(BF16)
    spread_col = (place[1] == np.arange(stride)[:, None]).astype(BF16)
    inner = (place[1] >= HALO) & (place[1] < HALO + cols)
    collect = (spread_row.T.astype(np.float32) * inner[:, None]).astype(BF16)
    far = -(-2 * stride // LANES) * LANES
    sums = ((channels, rows + 2 * HALO), F32)
    half = ((channels // 2, rows, cols), BF16)
    outs = (sums, half, half) if last else (sums, ((channels, total), BF16))
    scratch = [
        pltpu.VMEM((channels, total + 2 * LANES), BF16),
        pltpu.VMEM((channels, total + 2 * LANES), BF16),
        pltpu.VMEM((channels, total), F32),
        pltpu.VMEM((2 * channels, total + 2 * far), BF16),
        pltpu.VMEM((channels, total), F32),
        pltpu.VMEM((2 * channels, total + 2 * far), BF16),
        pltpu.VMEM((2, 3 * channels, 3 * channels), BF16),
        pltpu.VMEM((1, total), F32),
        pltpu.VMEM((cols // LANES, channels, rows + 2 * HALO, LANES), F32),
    ]
    kernel = functools.partial(cycle_kernel, rows, cols, length, last, len(windows))
    return call(
        kernel, outs, scratch, pair, row_proj, *windows, first, second,
        spread_row, spread_col, collect, place,
        limit=10 + total // 512, flops=40 * channels * channels * total,
    )


def on_device(seq_in, pair_in, w_row, w_col, w_value, conv_first, conv_second, w_out):
    rows, features = seq_in.shape
    channels = w_row.shape[1]
    half = channels // 2
    cols = pair_in.shape[2] // 2
    stride = cols + 2 * HALO
    tall = rows + 2 * HALO
    row_size, col_size = lax.axis_size("row"), lax.axis_size("col")
    chunks = 2 * col_size
    length = rows * row_size
    windows = cols // rows
    root = np.float32(np.sqrt(np.float32(length)))
    every = ("row", "col", "rep")
    weights = (w_row.T, w_col.T, w_value.T)
    swap = [(0, 1), (1, 0)]

    def pairs(begin, size):
        moves = []
        for i in range(begin, size - 1, 2):
            moves += [(i, i + 1), (i + 1, i)]
        return moves

    across = pairs(1, chunks)
    if chunks == 4:
        across += [(0, 3), (3, 0)]

    def to_columns(value):
        results = []
        for t in range(windows):
            moves = []
            for r in range(row_size):
                for q in range(chunks):
                    source = windows * q + (t + 1 - r) % windows
                    replica = (r // windows) ^ ((chunks // 2 + (t + 1) % 2) % chunks)
                    moves.append((source * chunks + replica, r * chunks + q))
            results.append(lax.ppermute(value, every, moves))
        return results

    def all_parts(value):
        if chunks & (chunks - 1):
            partners = [[(i, (i + b) % chunks) for i in range(chunks)] for b in range(1, chunks)]
        else:
            partners = [[(i, i ^ b) for i in range(chunks)] for b in range(1, chunks)]
        return [value] + [lax.ppermute(value, ("col", "rep"), moves) for moves in partners]

    far_pair = lax.ppermute(pair_in, "rep", swap)
    width = pair_in.shape[2]
    message = ((-(-GROUP * (half + features // width) // 16) * 16, width), BF16)
    first_out, second_out = call(
        strips_kernel, [message, message],
        [
            pltpu.VMEM((2, half, 2 * GROUP, width), BF16),
            pltpu.VMEM((2, 2 * GROUP, features), BF16),
            pltpu.SemaphoreType.DMA((4,)),
        ],
        pair_in, seq_in, space=pl.ANY, limit=56,
    )
    first = lax.ppermute(first_out, "row", pairs(0, row_size))
    second = lax.ppermute(second_out, "row", pairs(1, row_size))
    wide = [((tall, features), BF16), ((channels, tall), BF16), ((2 * channels, tall), BF16)]
    feats, row_proj, colval = call(
        functools.partial(project_kernel, half), wide, [],
        seq_in, first, second, *weights
    )
    col_windows = to_columns(colval)
    first_far = lax.ppermute(first, "rep", swap)
    second_far = lax.ppermute(second, "rep", swap)
    pieces = (pair_in, first, second, far_pair, first_far, second_far)
    (edge,) = call(edges_kernel, [((channels * GROUP, LANES), BF16)], [], *pieces)
    pieces += (lax.ppermute(edge, ("col", "rep"), across),)
    (pair,) = call(
        functools.partial(assemble_kernel, cols), [((channels, tall * stride), BF16)],
        [pltpu.VMEM((cols // LANES + 1, channels, tall, LANES), F32)],
        *pieces, limit=24, flops=1 << 30,
    )

    sums, pair = run_cycle(
        pair, row_proj, col_windows, conv_first, conv_second, rows, cols, length, False
    )
    parts = all_parts(sums)
    feats, row_proj, colval = call(
        functools.partial(middle_kernel, root, chunks), wide, [],
        *parts, feats, w_out, *weights,
    )
    col_windows = to_columns(colval)
    sums, own, send = run_cycle(
        pair, row_proj, col_windows, conv_first, conv_second, rows, cols, length, True
    )
    parts = all_parts(sums)
    far_half = lax.ppermute(send, "rep", swap)
    return call(
        functools.partial(finish_kernel, root, chunks),
        [(seq_in.shape, BF16), (pair_in.shape, BF16)], [],
        *parts, feats, w_out, own, far_half,
    )


def solution(mesh):
    in_specs = (
        P(("grp", "row"), None),
        P(("grp", "rep"), "row", "col"),
        P(),
        P(),
        P(),
        P(),
        P(),
        P(),
    )
    out_specs = (P(("grp", "row"), None), P(("grp", "rep"), "row", "col"))
    return jax.shard_map(
        on_device, mesh=mesh, in_specs=in_specs, out_specs=out_specs, check_vma=False
    )
```

```python
import functools

import jax
import jax.numpy as jnp
import numpy as np
from jax import lax
from jax.experimental import pallas as pl
from jax.experimental.pallas import tpu as pltpu
from jax.sharding import PartitionSpec as P

CYCLES = 2
HALO = 8
GROUP = 8
LANES = 128
CHUNK = 5760
F32, BF16 = jnp.float32, jnp.bfloat16
def call(kernel, outs, scratch, *args, space=pltpu.VMEM, limit=16, flops=1 << 20):
    moved = sum(int(np.prod(x.shape)) * x.dtype.itemsize for x in args)
    return pl.pallas_call(
        kernel,
        out_shape=tuple(jax.ShapeDtypeStruct(shape, dtype) for shape, dtype in outs),
        in_specs=[pl.BlockSpec(memory_space=space)] * len(args),
        out_specs=(pl.BlockSpec(memory_space=pltpu.VMEM),) * len(outs),
        scratch_shapes=scratch,
        compiler_params=pltpu.CompilerParams(vmem_limit_bytes=limit << 20),
        cost_estimate=pl.CostEstimate(flops=flops, bytes_accessed=moved, transcendentals=0),
    )(*args)


def lane_ids(shape):
    return lax.broadcasted_iota(jnp.int32, shape, len(shape) - 1)


def is_even():
    return lax.rem(lax.axis_index("row"), 2) == 0


def strips_kernel(tile_ref, seq_ref, first_ref, second_ref, tile_ends, seq_ends, sems):
    half, rows, width = tile_ref.shape
    even = is_even()

    def message(pair, seq):
        pieces = [pair.reshape(half * GROUP, width)]
        pieces += [seq[:, at : at + width] for at in range(0, seq.shape[1], width)]
        rest = first_ref.shape[0] - GROUP * (half + len(pieces) - 1)
        if rest:
            pieces.append(jnp.zeros((rest, width), F32))
        return jnp.concatenate(pieces, axis=0)

    moves = []
    for n, at in enumerate((0, rows - 2 * GROUP)):
        lines = pl.ds(at, 2 * GROUP)
        moves += [
            pltpu.make_async_copy(tile_ref.at[:, lines, :], tile_ends.at[n], sems.at[2 * n]),
            pltpu.make_async_copy(seq_ref.at[lines, :], seq_ends.at[n], sems.at[2 * n + 1]),
        ]
    for move in moves:
        move.start()
    for move in moves:
        move.wait()
    top = message(
        tile_ends[0].astype(F32)[:, :GROUP], seq_ends[0].astype(F32)[:GROUP]
    )
    bottom = message(
        tile_ends[1].astype(F32)[:, GROUP:], seq_ends[1].astype(F32)[GROUP:]
    )
    first_ref[...] = jnp.where(even, bottom, top).astype(BF16)
    second_ref[...] = jnp.where(even, top, bottom).astype(BF16)


def received(first, second):
    even = is_even()
    return jnp.where(even, second, first), jnp.where(even, first, second)


def tile_pieces(tile_ref, first_ref, second_ref, at):
    half, rows, _ = tile_ref.shape
    middle = tile_ref[:, :, pl.ds(at, LANES)].astype(F32)
    above, below = received(
        *(
            ref[0 : half * GROUP, pl.ds(at, LANES)].astype(F32).reshape(half, GROUP, LANES)
            for ref in (first_ref, second_ref)
        )
    )
    middle = [middle[:, m * GROUP : (m + 1) * GROUP] for m in range(rows // GROUP)]
    return [above, *middle, below]


def edges_kernel(*refs):
    parts, out_ref = (refs[0:3], refs[3:6]), refs[6]
    rep = lax.axis_index("rep")
    half, _, width = refs[0].shape
    lane = lane_ids((half, GROUP, LANES))
    at = pl.multiple_of(jnp.where(rep == 0, 0, width - LANES), LANES)
    for part in range(2):
        packed = jnp.zeros((half, GROUP, LANES), F32)
        turn = jnp.where(rep == 0, 0, HALO)
        for g, piece in enumerate(tile_pieces(*parts[part], at)):
            moved = pltpu.roll(piece, turn + HALO * g, 2)
            packed = jnp.where((lane >= HALO * g) & (lane < HALO * (g + 1)), moved, packed)
        base = (rep if part == 0 else 1 - rep) * half * GROUP
        out_ref[pl.ds(pl.multiple_of(base, 2 * GROUP), half * GROUP), :] = packed.reshape(
            half * GROUP, LANES
        ).astype(BF16)


def unpack(parts, edge_ref, raw, cols):
    rep = lax.axis_index("rep")
    across = cols // LANES
    half = parts[0][0].shape[0]
    inner_at = pl.multiple_of(jnp.where(rep == 0, cols, cols - LANES), LANES)
    is_outer = (lane_ids((half, GROUP, LANES)) < HALO) == (rep == 0)
    for part in range(2):
        owner = pl.ds((rep if part == 0 else 1 - rep) * half, half)
        for t in range(across):
            at = pl.multiple_of(rep * cols + t * LANES, LANES)
            for g, piece in enumerate(tile_pieces(*parts[part], at)):
                raw[t, owner, g * GROUP : (g + 1) * GROUP, :] = piece
        base = (rep if part == 0 else 1 - rep) * half * GROUP
        edge = edge_ref[pl.ds(pl.multiple_of(base, 2 * GROUP), half * GROUP), :].astype(F32)
        edge = edge.reshape(half, GROUP, LANES)
        outer = pltpu.roll(edge, jnp.where(rep == 0, 0, HALO), 2)
        for g, piece in enumerate(tile_pieces(*parts[part], inner_at)):
            raw[across, owner, g * GROUP : (g + 1) * GROUP, :] = jnp.where(
                is_outer,
                pltpu.roll(outer, (-HALO * g) % LANES, 2),
                pltpu.roll(piece, HALO, 2),
            )


def assemble_kernel(cols, *refs):
    parts, edge_ref, out_ref, raw = (refs[0:3], refs[3:6]), refs[6], refs[7], refs[8]
    unpack(parts, edge_ref, raw, cols)
    strip = GROUP * (cols + 2 * HALO)
    for k in range(raw.shape[2] // GROUP):
        out_ref[:, k * strip : (k + 1) * strip] = raw_strip(raw, k)


def raw_strip(raw, place):
    across, channels, rows, _ = raw.shape
    pieces = []
    for i in range(place * GROUP, (place + 1) * GROUP):
        tiles = [
            raw.at[t].reshape(channels * rows, LANES)[pl.ds(i, channels, stride=rows), :].astype(BF16)
            for t in range(across)
        ]
        side = tiles.pop()
        pieces += [side[:, :HALO], *tiles, side[:, HALO : 2 * HALO]]
    return jnp.concatenate(pieces, axis=1)


def project(feats, weight_refs, row_ref, colval_ref):
    row, col, value = (
        lax.dot_general(ref[...], feats, (((1,), (1,)), ((), ())), preferred_element_type=F32)
        for ref in weight_refs
    )
    channels = row.shape[0]
    row_ref[...] = row.astype(BF16)
    colval_ref[0:channels] = col.astype(BF16)
    colval_ref[channels:] = value.astype(BF16)


def project_kernel(half, seq_ref, first_ref, second_ref, *refs):
    weight_refs, (feats_ref, row_ref, colval_ref) = refs[:3], refs[3:]
    width = first_ref.shape[1]
    split = seq_ref.shape[1] // width
    halos = []
    for ref in (first_ref, second_ref):
        tail = ref[half * GROUP :, :].astype(F32)
        pieces = [tail[j * GROUP : (j + 1) * GROUP] for j in range(split)]
        halos.append(jnp.concatenate(pieces, axis=1))
    above, below = received(*halos)
    feats = jnp.concatenate([above, seq_ref[...].astype(F32), below], axis=0).astype(BF16)
    feats_ref[...] = feats
    project(feats, weight_refs, row_ref, colval_ref)


def advance(sum_refs, feats_ref, out_ref, root):
    total = sum_refs[0][...]
    for ref in sum_refs[1:]:
        total = total + ref[...]
    gathered = (total / root).T.astype(BF16)
    change = jnp.dot(gathered, out_ref[...], preferred_element_type=F32)
    return feats_ref[...].astype(F32) + change


def middle_kernel(root, parts, *refs):
    sum_refs, refs = refs[:parts], refs[parts:]
    feats_in, out_w, weight_refs, (feats_ref, row_ref, colval_ref) = (
        refs[0], refs[1], refs[2:5], refs[5:]
    )
    feats = advance(sum_refs, feats_in, out_w, root).astype(BF16)
    feats_ref[...] = feats
    project(feats, weight_refs, row_ref, colval_ref)


def finish_kernel(root, parts, *refs):
    sum_refs, refs = refs[:parts], refs[parts:]
    feats_in, out_w, own_ref, far_ref, seq_ref, pair_ref = refs
    rep = lax.axis_index("rep")
    rows, cols = seq_ref.shape[0], own_ref.shape[2]
    seq_ref[...] = advance(sum_refs, feats_in, out_w, root)[HALO : HALO + rows].astype(BF16)
    pair_ref[:, :, pl.ds(pl.multiple_of(rep * cols, LANES), cols)] = own_ref[...]
    pair_ref[:, :, pl.ds(pl.multiple_of((1 - rep) * cols, LANES), cols)] = far_ref[...]


def spans(low_row, high_row, stride, total):
    low = low_row * stride // LANES * LANES
    size = -(-(high_row * stride - low) // 256) * 256
    high = min(low + size, total)
    return [(at, min(at + CHUNK, high)) for at in range(low, high, CHUNK)]


def cycle_kernel(rows, cols, length, last, windows, *refs):
    (start_buf, hidden_buf, *taps, stack, mask, raw), refs = refs[-9:], refs[:-9]
    taps_first, taps_second = taps[0:2], taps[2:4]
    pair_ref, refs = refs[0], refs[1:]
    row_ref, window_refs, refs = refs[0], refs[1 : 1 + windows], refs[1 + windows :]
    first_ref, second_ref, spread_row, spread_col, collect, place_ref, *outs = refs
    channels = row_ref.shape[0]
    stride = cols + 2 * HALO
    tall = rows + 2 * HALO
    total = tall * stride
    strip = GROUP * stride
    strips = tall // GROUP
    guard = LANES
    reach = 2 * stride
    far = -(-reach // LANES) * LANES
    rep = lax.axis_index("rep")
    row_index = lax.axis_index("row")
    chunk_index = lax.axis_index("col") * 2 + rep
    margin = 2 * CYCLES * 2 - (8 if not last else 4)
    spans_in = spans(margin, rows + 2 * HALO - margin, stride, total)
    spans_mid = spans(margin + 2, rows + 2 * HALO - margin - 2, stride, total)
    spans_out = spans(margin + 4, rows + 2 * HALO - margin - 4, stride, total)

    for k in range(strips):
        row_at = row_index * rows - HALO + k * GROUP + place_ref[0:1, :]
        col_at = chunk_index * cols - HALO + place_ref[1:2, :]
        inside = (row_at >= 0) & (row_at < length) & (col_at >= 0) & (col_at < length)
        mask[:, k * strip : (k + 1) * strip] = jnp.where(inside, 1.0, 0.0)

    turn = lax.rem(row_index, windows)
    for n, ref in enumerate((first_ref, second_ref)):
        lines = []
        for ti in (1, 0, 2):
            blocks = [ref[3 * ti + tj].astype(F32) for tj in range(3)]
            lines.append(jnp.concatenate(blocks, axis=1))
        stack[n] = jnp.concatenate(lines, axis=0).astype(BF16)

    ordered = []
    for offset in range(windows):
        value = window_refs[0][...]
        for t in range(1, windows):
            piece = lax.rem(t + 1 - turn + windows, windows)
            value = jnp.where(piece == offset, window_refs[t][...], value)
        low = 0 if offset == 0 else HALO
        high = rows + (2 * HALO if offset == windows - 1 else HALO)
        ordered.append(value[:, low:high].astype(F32))
    colval = jnp.concatenate(ordered, axis=1).astype(BF16)
    colval = jnp.dot(colval, spread_col[...], preferred_element_type=F32)
    col_flat, val_flat = colval[:channels], colval[channels:]

    for buf, edge, part in (
        (start_buf, guard, ((0, total),)), (hidden_buf, guard, spans_mid),
        (taps_first[1], far, spans_in), (taps_second[1], far, spans_mid),
    ):
        low, high = part[0][0], part[-1][1]
        fill = jnp.zeros((buf.shape[0], edge), buf.dtype)
        buf[:, low : low + edge] = fill
        buf[:, high + edge : high + 2 * edge] = fill

    def start_strip(k):
        row_flat = jnp.dot(
            row_ref[:, k * GROUP : (k + 1) * GROUP], spread_row[...], preferred_element_type=F32
        )
        pair = pair_ref[:, k * strip : (k + 1) * strip].astype(F32)
        value = pair + row_flat + col_flat
        value = jnp.where(mask[:, k * strip : (k + 1) * strip] > 0, value, 0.0)
        start_buf[:, guard + k * strip : guard + (k + 1) * strip] = value.astype(BF16)

    lane = lane_ids((channels, LANES))
    turned = {}

    def shifted(key, load, at, low, high):
        tiles = []
        for tile in range(low // LANES, high // LANES):
            first, off = divmod(tile * LANES + at, LANES)
            pair = []
            for place in (first, first + 1):
                if (key, at, place) not in turned:
                    turned[key, at, place] = pltpu.roll(load(place), LANES - off, 1)
                pair.append(turned[key, at, place])
            tiles.append(jnp.where(lane < LANES - off, *pair))
        return jnp.concatenate(tiles, axis=1)

    def spread(source, taps, n, low, high):
        def load(tile):
            return source[:, guard + tile * LANES : guard + (tile + 1) * LANES]

        stacked = [
            shifted((n, 0), load, -2, low, high),
            source[:, guard + low : guard + high],
            shifted((n, 0), load, 2, low, high),
        ]
        stacked = jnp.concatenate(stacked, axis=0)
        result = jnp.dot(stack[n], stacked, preferred_element_type=F32)
        taps[0][:, low:high] = result[:channels]
        taps[1][:, far + low : far + high] = result[channels:].astype(BF16)

    def gather(n, taps, low, high):
        value = taps[0][:, low:high]
        for part, at in ((0, -reach), (1, reach)):

            def load(tile):
                lanes = slice(far + tile * LANES, far + (tile + 1) * LANES)
                return taps[1][part * channels : (part + 1) * channels, lanes]

            value = value + shifted((n, 1), load, at, low, high).astype(F32)
        return jnp.maximum(value, 0.0)

    def first_span(low, high):
        spread(start_buf, taps_first, 0, low, high)

    def hidden_span(low, high):
        value = jnp.where(mask[:, low:high] > 0, gather(0, taps_first, low, high), 0.0)
        hidden_buf[:, guard + low : guard + high] = value.astype(BF16)

    def second_span(low, high):
        spread(hidden_buf, taps_second, 1, low, high)

    def pair_span(low, high):
        value = gather(1, taps_second, low, high)
        pair = start_buf[:, guard + low : guard + high].astype(F32) + value
        start_buf[:, guard + low : guard + high] = pair.astype(BF16)

    def gate_strip(k):
        if last and k in (0, strips - 1):
            outs[0][:, k * GROUP : (k + 1) * GROUP] = jnp.zeros((channels, GROUP), F32)
            return
        pair = start_buf[:, guard + k * strip : guard + (k + 1) * strip]
        wide = pair.astype(F32)
        gate = jax.nn.sigmoid(wide).astype(BF16)
        product = (gate.astype(F32) * val_flat).astype(BF16)
        outs[0][:, k * GROUP : (k + 1) * GROUP] = jnp.dot(
            product, collect[...], preferred_element_type=F32
        )
        if not last:
            outs[1][:, k * strip : (k + 1) * strip] = pair
        else:
            for i in range(GROUP):
                for t in range(cols // LANES):
                    at = i * stride + HALO + t * LANES
                    flat = raw.at[t].reshape(channels * tall, LANES)
                    piece = pair[:, at : at + LANES].astype(F32)
                    flat[pl.ds(k * GROUP + i, channels, stride=tall), :] = piece

    strip_spans = [(k * strip, (k + 1) * strip) for k in range(strips)]
    stages = [
        (strip_spans, lambda low, high: start_strip(low // strip), 0),
        (spans_in, first_span, guard),
        (spans_mid, hidden_span, reach),
        (spans_mid, second_span, guard),
        (spans_out, pair_span, reach),
        (strip_spans, lambda low, high: gate_strip(low // strip), 0),
    ]
    done, made = [0] * len(stages), [0] * len(stages)

    def ready(n):
        parts, _, ahead = stages[n]
        if done[n] == len(parts):
            return False
        if n == 0 or done[n - 1] == len(stages[n - 1][0]):
            return True
        return parts[done[n]][1] + ahead <= made[n - 1]

    while any(done[n] < len(stages[n][0]) for n in range(len(stages))):
        for n in reversed(range(len(stages))):
            if ready(n):
                low, high = stages[n][0][done[n]]
                stages[n][1](low, high)
                done[n], made[n] = done[n] + 1, high

    if last:
        half = channels // 2
        for t in range(cols // LANES):
            lanes = slice(t * LANES, (t + 1) * LANES)
            for out, owner in ((outs[1], rep), (outs[2], 1 - rep)):
                value = raw[t, pl.ds(owner * half, half), HALO : HALO + rows, :]
                out[:, :, lanes] = value.astype(BF16)


def run_cycle(pair, row_proj, windows, first, second, rows, cols, length, last):
    channels = row_proj.shape[0]
    stride = cols + 2 * HALO
    total = (rows + 2 * HALO) * stride
    strip = GROUP * stride
    lane = np.arange(strip)
    place = np.stack([lane // stride, lane % stride] + [0 * lane] * 6).astype(np.int32)
    spread_row = (place[0] == np.arange(GROUP)[:, None]).astype(BF16)
    spread_col = (place[1] == np.arange(stride)[:, None]).astype(BF16)
    inner = (place[1] >= HALO) & (place[1] < HALO + cols)
    collect = (spread_row.T.astype(np.float32) * inner[:, None]).astype(BF16)
    far = -(-2 * stride // LANES) * LANES
    sums = ((channels, rows + 2 * HALO), F32)
    half = ((channels // 2, rows, cols), BF16)
    outs = (sums, half, half) if last else (sums, ((channels, total), BF16))
    scratch = [
        pltpu.VMEM((channels, total + 2 * LANES), BF16),
        pltpu.VMEM((channels, total + 2 * LANES), BF16),
        pltpu.VMEM((channels, total), F32),
        pltpu.VMEM((2 * channels, total + 2 * far), BF16),
        pltpu.VMEM((channels, total), F32),
        pltpu.VMEM((2 * channels, total + 2 * far), BF16),
        pltpu.VMEM((2, 3 * channels, 3 * channels), BF16),
        pltpu.VMEM((1, total), F32),
        pltpu.VMEM((cols // LANES, channels, rows + 2 * HALO, LANES), F32),
    ]
    kernel = functools.partial(cycle_kernel, rows, cols, length, last, len(windows))
    return call(
        kernel, outs, scratch, pair, row_proj, *windows, first, second,
        spread_row, spread_col, collect, place,
        limit=10 + total // 512, flops=40 * channels * channels * total,
    )


def on_device(seq_in, pair_in, w_row, w_col, w_value, conv_first, conv_second, w_out):
    rows, features = seq_in.shape
    channels = w_row.shape[1]
    half = channels // 2
    cols = pair_in.shape[2] // 2
    stride = cols + 2 * HALO
    tall = rows + 2 * HALO
    row_size, col_size = lax.axis_size("row"), lax.axis_size("col")
    chunks = 2 * col_size
    length = rows * row_size
    windows = cols // rows
    root = np.float32(np.sqrt(np.float32(length)))
    every = ("row", "col", "rep")
    weights = (w_row.T, w_col.T, w_value.T)
    swap = [(0, 1), (1, 0)]

    def pairs(begin, size):
        moves = []
        for i in range(begin, size - 1, 2):
            moves += [(i, i + 1), (i + 1, i)]
        return moves

    across = pairs(1, chunks)
    if chunks == 4:
        across += [(0, 3), (3, 0)]

    def to_columns(value):
        results = []
        for t in range(windows):
            moves = []
            for r in range(row_size):
                for q in range(chunks):
                    source = windows * q + (t + 1 - r) % windows
                    replica = (r // windows) ^ ((chunks // 2 + (t + 1) % 2) % chunks)
                    moves.append((source * chunks + replica, r * chunks + q))
            results.append(lax.ppermute(value, every, moves))
        return results

    def all_parts(value):
        if chunks & (chunks - 1):
            partners = [[(i, (i + b) % chunks) for i in range(chunks)] for b in range(1, chunks)]
        else:
            partners = [[(i, i ^ b) for i in range(chunks)] for b in range(1, chunks)]
        return [value] + [lax.ppermute(value, ("col", "rep"), moves) for moves in partners]

    far_pair = lax.ppermute(pair_in, "rep", swap)
    width = pair_in.shape[2]
    message = ((-(-GROUP * (half + features // width) // 16) * 16, width), BF16)
    first_out, second_out = call(
        strips_kernel, [message, message],
        [
            pltpu.VMEM((2, half, 2 * GROUP, width), BF16),
            pltpu.VMEM((2, 2 * GROUP, features), BF16),
            pltpu.SemaphoreType.DMA((4,)),
        ],
        pair_in, seq_in, space=pl.ANY, limit=56,
    )
    first = lax.ppermute(first_out, "row", pairs(0, row_size))
    second = lax.ppermute(second_out, "row", pairs(1, row_size))
    wide = [((tall, features), BF16), ((channels, tall), BF16), ((2 * channels, tall), BF16)]
    feats, row_proj, colval = call(
        functools.partial(project_kernel, half), wide, [],
        seq_in, first, second, *weights
    )
    col_windows = to_columns(colval)
    first_far = lax.ppermute(first, "rep", swap)
    second_far = lax.ppermute(second, "rep", swap)
    pieces = (pair_in, first, second, far_pair, first_far, second_far)
    (edge,) = call(edges_kernel, [((channels * GROUP, LANES), BF16)], [], *pieces)
    pieces += (lax.ppermute(edge, ("col", "rep"), across),)
    (pair,) = call(
        functools.partial(assemble_kernel, cols), [((channels, tall * stride), BF16)],
        [pltpu.VMEM((cols // LANES + 1, channels, tall, LANES), F32)],
        *pieces, limit=24, flops=1 << 30,
    )

    sums, pair = run_cycle(
        pair, row_proj, col_windows, conv_first, conv_second, rows, cols, length, False
    )
    parts = all_parts(sums)
    feats, row_proj, colval = call(
        functools.partial(middle_kernel, root, chunks), wide, [],
        *parts, feats, w_out, *weights,
    )
    col_windows = to_columns(colval)
    sums, own, send = run_cycle(
        pair, row_proj, col_windows, conv_first, conv_second, rows, cols, length, True
    )
    parts = all_parts(sums)
    far_half = lax.ppermute(send, "rep", swap)
    return call(
        functools.partial(finish_kernel, root, chunks),
        [(seq_in.shape, BF16), (pair_in.shape, BF16)], [],
        *parts, feats, w_out, own, far_half,
    )


def solution(mesh):
    in_specs = (
        P(("grp", "row"), None),
        P(("grp", "rep"), "row", "col"),
        P(),
        P(),
        P(),
        P(),
        P(),
        P(),
    )
    out_specs = (P(("grp", "row"), None), P(("grp", "rep"), "row", "col"))
    return jax.shard_map(
        on_device, mesh=mesh, in_specs=in_specs, out_specs=out_specs, check_vma=False
    )
```
